256 devices in a mesh: blk: 64 (over x, y_lo, z), dim: 4 (over y_hi, core).
Axes of the slice: x: 4, y: 4 (y_hi: 2, y_lo: 2; y = y_hi * 2 + y_lo), z: 8, core: 2. Of those that a mesh axis runs over, the one named last changes fastest.
Arguments:
- question_matrix: float32 [8192, 768], P('blk', 'dim'), may hold values from -20 to 20, as said below
- document_matrix: float32 [8192, 768], P('blk', 'dim'), may hold values from -0.5 to 0.5
- pool: float32 [768, 131072], P('dim', 'blk'), may hold values from -1.4 to 1.4
- hard_owner: int32 [8192, 8], P('blk'), may hold values from 0 to 63, all different within a row; in each aligned block of 128 rows (0 to 127, 128 to 255, ...) at most 32 rows name the same one
- hard_local: int32 [8192, 8], P('blk'), may hold values from 0 to 2047
Outputs:
- loss: float32 [8192], P('blk')
- question_derivative: float32 [8192, 768], P('blk', 'dim')
- document_derivative: float32 [8192, 768], P('blk', 'dim')
- grad_pool: float32 [768, 131072], P('dim', 'blk')
The draws below stay inside these ranges and needn't reach their ends.
Inputs may be any that keep to these rules, and one draw needn't show every extreme that they name: `question_matrix`: query embeddings; some rows may be much larger than the rest. `hard_owner`: the 8 owners named in one row are different. Among the rows of one index of blk, no owner is named more than 32 times, a bound that some block reaches.
All inputs are finite; a program needn't handle non-finite values.
Results may differ from the reference program's by a relative error of at most 0.0003.
Values sent between devices are 32-bit elements; how exact they have to be, the bound alone decides.
A program may use at most 64 MiB of HBM per device.

```python
import math
import jax
import jax.numpy as jnp
import numpy as np
from jax import lax

VECTOR_LENGTH = 768
H = 8
Q_DEV = 128
POOL_DEV = 2048
NQ = 8192
POOL = 131072
MOST = 32
N_BLK = 64


def draw_question_matrix(key, part):
    values = jax.random.normal(key, (NQ, VECTOR_LENGTH), jnp.float32) * 0.074
    values = jnp.clip(values, -0.5, 0.5)
    return values


def set_ends(values, rng, low, top_value):
    longest = values.shape.index(max(values.shape))
    spots = []
    for shift in (0, 1):
        where = [jax.random.randint(jax.random.fold_in(rng, axis), (), 0, length) for axis, length in enumerate(values.shape)]
        where[longest] = (where[longest] + shift) % values.shape[longest]
        spots.append(tuple(where))
    return values.at[spots[0]].set(low).at[spots[1]].set(top_value)


def steps_of(stream_key, shape, cuts, least, largest):
    level = 1.0
    for dim, parts in cuts:
        steps = jax.random.uniform(jax.random.fold_in(jax.random.fold_in(stream_key, 6), dim), (parts,), jnp.float32, least / len(cuts), largest / len(cuts))
        level = level * jnp.repeat(jnp.exp(steps), shape[dim] // parts).reshape((-1,) + (1,) * (len(shape) - 1 - dim))
    return level


def deal_out(key, own, number, rows, count, top, limit, skew):
    order = jax.random.permutation(key, count)
    packed, ordinary = portions_of(count, rows * top, limit, skew, True), portions_of(count, rows * top, limit, skew, False)
    places = jnp.arange(count)

    def named(lengths, offset_by):
        used = int((lengths > 0).sum())
        fixed = max(1, used // 4)
        shifted = fixed + (places - fixed + offset_by * (used - fixed)) % max(1, count - fixed)
        return jnp.zeros((count,), jnp.int32).at[order[jnp.where(places < fixed, places, shifted)]].set(jnp.asarray(lengths, jnp.int32))

    lengths = jnp.where(number % 4 == 0, named(packed, number // 4), named(ordinary, number - number // 4 - 1))
    mixed = jax.random.permutation(jax.random.fold_in(own, 3), count)
    source_of, taker = mixed[0:count // 2 * 2:2], mixed[1:count // 2 * 2:2]
    room = jnp.minimum(lengths[source_of] - 1, limit - lengths[taker]) // 2
    room = jnp.where((source_of == order[0]) | (taker == order[0]) | (lengths[taker] == 0), 0, jnp.maximum(room, 0))
    shifted = jax.random.randint(jax.random.fold_in(own, 4), (count // 2,), 0, 1 << 20) % (room + 1)
    lengths = lengths.at[source_of].add(-shifted).at[taker].add(shifted)
    members = jnp.searchsorted(jnp.cumsum(lengths), jnp.arange(rows * top), side="right").astype(jnp.int32)
    table = members.reshape(top, rows).T
    table = table[jax.random.permutation(jax.random.fold_in(own, 1), rows)]
    offset_by = jax.random.randint(jax.random.fold_in(own, 2), (rows, 1), 0, top)
    return jnp.take_along_axis(table, (jnp.arange(top)[None, :] + offset_by) % top, axis=1)


def portions_of(number_of, total, reach, lean, full):
    weights = [(1 << 20) // math.isqrt(rank ** lean) + 1 for rank in range(1, number_of + 1)]
    largest = reach if full else min(reach, max(-(-total // number_of), total * weights[0] // sum(weights)))
    least = 1 if total - largest >= number_of - 1 else 0
    holding, spare = [largest] + [least] * (number_of - 1), total - largest - least * (number_of - 1)
    while spare > 0:
        free = [i for i in range(1, number_of) if holding[i] < largest] or [i for i in range(1, number_of) if holding[i] < reach]
        mass, remaining = sum([weights[i] for i in free]), spare
        for i in free:
            addition = min(reach - holding[i], max(1, remaining * weights[i] // mass), spare)
            holding[i] = holding[i] + addition
            spare = spare - addition
    return np.array(holding)


def centred(stream_key, extent, spread, bound, split=(), dtype=jnp.bfloat16):
    drawn = jax.random.normal(stream_key, extent, jnp.float32) * spread
    if len(split) > 0:
        drawn = steps_of(stream_key, extent, split, -0.22, 0.18) * drawn
    return jnp.clip(drawn, min=-bound, max=bound).astype(dtype)


def setup_inputs(seed: int = 0) -> dict:
    key_of = jax.random.split(jax.random.key(seed), 6)
    question_matrix = draw_question_matrix(jax.random.fold_in(key_of[5], 71), 0)
    document_matrix = centred(key_of[1], (NQ, VECTOR_LENGTH), 0.074, 0.5, ((0, 64), (1, 4)), jnp.float32)
    pool = centred(key_of[2], (VECTOR_LENGTH, POOL), 0.22, 1.4, ((0, 4), (1, 64)), jnp.float32)
    hard_owner_keys = jax.random.split(jax.random.fold_in(key_of[3], 1), NQ // Q_DEV)
    hard_owner_turns = jax.random.permutation(jax.random.fold_in(key_of[3], 3), NQ // Q_DEV)
    hard_owner = jax.vmap(lambda own, number: deal_out(jax.random.fold_in(key_of[3], 2), own, number, Q_DEV, N_BLK, H, MOST, 2))(hard_owner_keys, hard_owner_turns).reshape((NQ, H))
    hard_local = set_ends(jax.random.randint(key_of[4], (NQ, H), 0, POOL_DEV), jax.random.fold_in(key_of[4], 1), 0, POOL_DEV - 1).astype(jnp.int32)
    return {"question_matrix": question_matrix, "document_matrix": document_matrix, "pool": pool, "hard_owner": hard_owner, "hard_local": hard_local}


logit_divisor = 0.05


def reference(question_matrix, document_matrix, pool, hard_owner, hard_local):
    highest_accuracy = lax.Precision.HIGHEST
    pool_rows = pool.T
    rows = (hard_owner * POOL_DEV + hard_local).astype(jnp.int32)
    query_blocks = question_matrix.reshape(N_BLK, Q_DEV, VECTOR_LENGTH)
    passage_blocks = document_matrix.reshape(N_BLK, Q_DEV, VECTOR_LENGTH)
    row_blocks = rows.reshape(N_BLK, Q_DEV, H)

    def advance(carry, block):
        document_derivative_round, grad_rows = carry
        question_derivative_share, document_derivative_share, named = block
        affinity_logits = jnp.dot(question_derivative_share, document_matrix.T, precision=highest_accuracy, preferred_element_type=jnp.float32) / logit_divisor
        distractor_lines = pool_rows[named]
        distractor_logits = jnp.einsum("pq,pcq->pc", question_derivative_share, distractor_lines, precision=highest_accuracy) / logit_divisor
        matching_logit = jnp.sum(question_derivative_share * document_derivative_share, axis=1) / logit_divisor
        peak = jnp.maximum(jnp.max(affinity_logits, axis=1), jnp.max(distractor_logits, axis=1))
        summed = jnp.sum(jnp.exp(affinity_logits - peak[:, None]), axis=1) + jnp.sum(jnp.exp(distractor_logits - peak[:, None]), axis=1)
        normalizer_logarithm = peak + jnp.log(summed)
        chance = jnp.exp(affinity_logits - normalizer_logarithm[:, None])
        distractor_likelihood = jnp.exp(distractor_logits - normalizer_logarithm[:, None])
        grad_query = (jnp.dot(chance, document_matrix, precision=highest_accuracy, preferred_element_type=jnp.float32)
                      + jnp.einsum("jg,jgu->ju", distractor_likelihood, distractor_lines, precision=highest_accuracy) - document_derivative_share) / logit_divisor
        document_derivative_round = document_derivative_round + jnp.dot(chance.T, question_derivative_share, precision=highest_accuracy, preferred_element_type=jnp.float32)
        dispatched_deltas = (distractor_likelihood[:, :, None] * question_derivative_share[:, None, :] / logit_divisor).reshape(-1, VECTOR_LENGTH)
        grad_rows = grad_rows.at[named.reshape(-1)].add(dispatched_deltas)
        return (document_derivative_round, grad_rows), (normalizer_logarithm - matching_logit, grad_query)

    start = (jnp.zeros((NQ, VECTOR_LENGTH), jnp.float32), jnp.zeros((POOL, VECTOR_LENGTH), jnp.float32))
    (document_derivative_round, grad_rows), (objective_entries, question_derivative) = lax.scan(advance, start, (query_blocks, passage_blocks, row_blocks))
    document_derivative = (document_derivative_round - question_matrix) / logit_divisor
    return objective_entries.reshape(NQ), question_derivative.reshape(NQ, VECTOR_LENGTH), document_derivative, grad_rows.T
```

```python
import jax
import jax.numpy as jnp
from jax import lax
from jax.experimental import pallas as pl
from jax.experimental.pallas import tpu as pltpu
from jax.sharding import PartitionSpec as P

MESH = pl.DeviceIdType.MESH
F32 = jnp.float32
BF16 = jnp.bfloat16
HIGHEST = lax.Precision.HIGHEST
SCALE = 20.0

NT = (((1,), (1,)), ((), ()))
NN = (((1,), (0,)), ((), ()))


def mm(a, b, dims, precision=None):
    return lax.dot_general(a, b, dims, precision=precision, preferred_element_type=F32)


def split3(x):
    high = x.astype(BF16)
    rest = x - high.astype(F32)
    mid = rest.astype(BF16)
    low = (rest - mid.astype(F32)).astype(BF16)
    return high, mid, low


def loop(count, body):
    def step(i, carry):
        body(i)
        return carry

    lax.fori_loop(0, count, step, 0)


REQ, DOC, ROWS, QUERY, DGRAD, PROB = range(6)
SIB_D, SIB_Q, SIB_H, SIB_G, SIB_DD, PART_Q, PART_DQ, PART_L = range(8)


def kernel(
    q_ref, d_ref, pool_ref, idx_ref,
    loss_ref, dq_ref, dd_ref, gp_ref,
    idx_all, q_all, d_mine, d_all, lr_all, sid, rq_out, rq_in, lt, pool_s,
    p_out, p_in, f_out, f_in, hs_mine, hs_sib, hq, st, ch, stat_out, stat_in,
    hc_out, hc_in, g3_out, g3_in, dd_sib, g_sib_out, g_sib_in, g_out, g_in, wcat, at_s,
    dq_out, dq_in, loss_out, loss_in, dd_out, lrow,
    plane_s, plane_r, row_s, row_r, idx_s, idx_r, qs, qr, gs, gr, one_s, one_r,
):
    blk, dim = lax.axis_index("blk"), lax.axis_index("dim")
    xy, z = blk // 8, blk % 8
    yh, c = dim // 2, dim % 2
    t = z // 2
    holder = (z % 2) == yh
    me_p = xy * 2 + yh
    me_r = z * 2 + c

    def plane_dev(p):
        return ((p // 2) * 8 + z, (p % 2) * 2 + c)

    def row_dev(r):
        return (xy * 8 + r // 2, yh * 2 + r % 2)

    def z_dev(zz):
        return (xy * 8 + zz, dim)

    sibling = (blk, yh * 2 + (1 - c))
    partner = (blk, (1 - yh) * 2 + c)

    def remote(src, dst, send, recv, device):
        return pltpu.make_async_remote_copy(
            src_ref=src, dst_ref=dst, send_sem=send, recv_sem=recv,
            device_id=device, device_id_type=MESH,
        )

    def plane(phase, src, dst_here, dst_there, p, slot):
        return remote(src, dst_there, plane_s.at[phase, p], plane_r.at[phase, slot], plane_dev(p))

    barrier = pltpu.get_barrier_semaphore()

    def greet(k):
        pl.semaphore_signal(barrier, inc=1, device_id=plane_dev((me_p + k + 1) % 16), device_id_type=MESH)
        pl.semaphore_signal(barrier, inc=1, device_id=row_dev((me_r + k + 1) % 16), device_id_type=MESH)

    loop(15, greet)
    pl.semaphore_wait(barrier, 30)

    def idx_copy(zz):
        return remote(idx_ref, idx_all.at[t], idx_s.at[zz], idx_r.at[t], z_dev(zz))

    def q_copy(part, zz):
        return remote(
            q_all.at[c, part, t], q_all.at[c, part, t], qs.at[part, zz], qr.at[part, t], z_dev(zz)
        )

    sib_d = remote(
        d_ref.at[pl.ds((1 - c) * 64, 64)], d_mine.at[c], one_s.at[SIB_D], one_r.at[SIB_D], sibling
    )
    part_q = remote(q_ref, q_all.at[c, yh, t], one_s.at[PART_Q], qr.at[yh, t], partner)
    part_q_in = remote(q_ref, q_all.at[c, 1 - yh, t], one_s.at[PART_Q], qr.at[1 - yh, t], partner)

    @pl.when(holder)
    def _():
        def send(k):
            idx_copy((z + k + 1) % 8).start()

        loop(7, send)

    sib_d.start()

    @pl.when(jnp.logical_not(holder))
    def _():
        part_q.start()

    @pl.when(holder)
    def _():
        q_all[c, yh, t] = q_ref[...]
        idx_all[t] = idx_ref[...]

        def send(k):
            q_copy(yh, (z + k + 1) % 8).start()

        loop(7, send)

    d_mine[c] = d_ref[pl.ds(pl.multiple_of(c * 64, 64), 64), :]
    d_all[yh, c, xy] = d_ref[pl.ds(pl.multiple_of(c * 64, 64), 64), :]
    sib_d.wait_recv()

    def doc_copy(p, slot):
        return remote(
            d_mine, d_all.at[slot % 2, :, slot // 2],
            plane_s.at[DOC, p], plane_r.at[DOC, slot], plane_dev(p),
        )

    loop(15, lambda k: doc_copy((me_p + k + 1) % 16, me_p).start())
    d_all[yh, 1 - c, xy] = d_mine[1 - c]

    def idx_wait(tt):
        @pl.when(2 * tt + yh != z)
        def _():
            remote(idx_ref, idx_all.at[tt], idx_s.at[0], idx_r.at[tt], partner).wait_recv()

    loop(4, idx_wait)
    sub8 = lax.broadcasted_iota(jnp.int32, (8, 128), 0)
    upper = jnp.where(
        lax.broadcasted_iota(jnp.int32, (128, 128), 0) < lax.broadcasted_iota(jnp.int32, (128, 128), 1),
        1.0, 0.0,
    ).astype(BF16)
    for tt in range(4):
        owner = idx_all[tt, 0:8]
        local = idx_all[tt, 8:16] + 1
        table = jnp.zeros((8, 128), jnp.int32)
        for a in range(8):
            row = jnp.sum(jnp.where(owner == a * 8 + z, local, 0), axis=0, keepdims=True)
            table = jnp.where(sub8 == a, row, table)
        marks = jnp.where(table > 0, 1.0, 0.0)
        rank = mm(marks.astype(BF16), upper, NN)
        lr_all[:, tt * 128 : (tt + 1) * 128] = table.astype(F32)
        sid[:, tt * 128 : (tt + 1) * 128] = jnp.where(table > 0, rank + float(tt * 32), -1.0)

    sub512 = lax.broadcasted_iota(jnp.int32, (128, 512), 0).astype(F32)
    lane128 = lax.broadcasted_iota(jnp.int32, (128, 128), 1)

    def hot(a):
        return sub512 == sid[pl.ds(a, 1), :]

    def columns(rows):
        def step(a, table):
            col = jnp.sum(jnp.where(hot(a), rows[pl.ds(a, 1), :], 0.0), axis=1, keepdims=True)
            return jnp.where(lane128 == a, col, table)

        return lax.fori_loop(0, 8, step, jnp.zeros((128, 128), F32))

    wanted = columns(lr_all).T
    for a in range(8):
        rq_out[a] = wanted[a : a + 1, :]
    rq_in[me_p] = rq_out[xy]

    def req_copy(p, slot):
        return remote(
            rq_out.at[p // 2], rq_in.at[slot], plane_s.at[REQ, p], plane_r.at[REQ, slot], plane_dev(p)
        )

    loop(15, lambda k: req_copy((me_p + k + 1) % 16, me_p).start())

    @pl.when(holder)
    def _():
        part_q_in.wait_recv()
        loop(7, lambda k: q_copy(1 - yh, (z + k + 1) % 8).start())

    for k, part in enumerate(split3(pool_ref[...])):
        pool_s[k] = part

    def req_wait(k):
        p = (me_p + k + 1) % 16
        req_copy(p, p).wait_recv()

    loop(15, req_wait)
    named = jnp.concatenate([rq_in[i] for i in range(16)] + [jnp.zeros((112, 128), F32)], axis=0)
    lt[...] = named.T
    lane2048 = lax.broadcasted_iota(jnp.int32, (128, 2048), 1).astype(F32) + 1.0

    def rows_copy(p, slot):
        return remote(
            p_out.at[p], p_in.at[slot % 2, slot // 2],
            plane_s.at[ROWS, p], plane_r.at[ROWS, slot], plane_dev(p),
        )

    def fetch(g):
        hots = []
        for i in range(4):
            col = jnp.sum(jnp.where(lane128 == g * 4 + i, lt[...], 0.0), axis=1, keepdims=True)
            hots.append(jnp.where(col == lane2048, 1.0, 0.0).astype(BF16))
        hots = jnp.concatenate(hots, axis=0)
        got = mm(hots, pool_s[0], NT) + mm(hots, pool_s[1], NT) + mm(hots, pool_s[2], NT)
        for i in range(4):
            p = g * 4 + i
            p_out[p] = got[i * 128 : (i + 1) * 128]

            @pl.when(p != me_p)
            def _():
                rows_copy(p, me_p).start()

    loop(4, fetch)
    p_in[yh, xy] = p_out[me_p]

    def q_wait(tt):
        @pl.when(2 * tt + yh != z)
        def _():
            for part in range(2):
                remote(
                    q_ref, q_all.at[c, part, tt], one_s.at[PART_Q], qr.at[part, tt], partner
                ).wait_recv()

    loop(4, q_wait)
    sib_q = remote(q_all.at[c], q_all.at[c], one_s.at[SIB_Q], one_r.at[SIB_Q], sibling)
    sib_q.start()

    def query_copy(p, slot):
        return remote(
            f_out.at[p], f_in.at[slot], plane_s.at[QUERY, p], plane_r.at[QUERY, slot], plane_dev(p)
        )

    for part in range(2):
        queries = split3(q_all[c, part].reshape(512, 192))

        def pick(g):
            hots = jnp.concatenate(
                [jnp.where(hot(g * 4 + i), 1.0, 0.0).astype(BF16) for i in range(4)], axis=0
            )
            got = mm(hots, queries[0], NN) + mm(hots, queries[1], NN) + mm(hots, queries[2], NN)
            for i in range(4):
                p = (g * 4 + i) * 2 + part
                f_out[p] = got[i * 128 : (i + 1) * 128]

                @pl.when(p != me_p)
                def _():
                    query_copy(p, me_p).start()

        loop(2, pick)
    f_in[me_p] = f_out[me_p]

    remote(q_all.at[c], q_all.at[1 - c], one_s.at[SIB_Q], one_r.at[SIB_Q], sibling).wait_recv()

    def doc_wait(k):
        p = (me_p + k + 1) % 16
        doc_copy(p, p).wait_recv()

    loop(15, doc_wait)

    def score(j):
        total = None
        for part in range(2):
            for core in range(2):
                docs = d_all[part, core, pl.ds(j * 4, 4)].reshape(256, 192)
                value = mm(docs, q_all[core, part].reshape(512, 192), NT, HIGHEST)
                total = value if total is None else total + value
        st[pl.ds(pl.multiple_of(j * 256, 256), 256), :] = total * SCALE

    loop(2, score)

    def rows_wait(k):
        p = (me_p + k + 1) % 16
        rows_copy(p, p).wait_recv()

    loop(15, rows_wait)

    def hard_part(a, table):
        col = jnp.sum(
            p_in[0, a] * f_out[a * 2] + p_in[1, a] * f_out[a * 2 + 1], axis=1, keepdims=True
        )
        return jnp.where(lane128 == a, col, table)

    hs_mine[...] = lax.fori_loop(0, 8, hard_part, jnp.zeros((128, 128), F32))
    sib_h = remote(hs_mine, hs_sib, one_s.at[SIB_H], one_r.at[SIB_H], sibling)
    sib_h.start()

    def top(j, best):
        rows = st[pl.ds(pl.multiple_of(j * 64, 64), 64), :].reshape(8, 8, 512)
        return jnp.maximum(best, jnp.max(rows, axis=0))

    best = lax.fori_loop(0, 8, top, jnp.full((8, 512), -jnp.inf, F32))
    best = jnp.max(best, axis=0, keepdims=True)
    sib_h.wait_recv()
    hard = (hs_mine[...] + hs_sib[...]) * SCALE
    for a in range(8):
        row = jnp.sum(jnp.where(hot(a), hard[:, a : a + 1], 0.0), axis=0, keepdims=True)
        hq[a : a + 1, :] = jnp.where(sid[a : a + 1, :] >= 0.0, row, -jnp.inf)
    peak = jnp.maximum(best, jnp.max(hq[...], axis=0, keepdims=True))

    def add(j, total):
        rows = jnp.exp(st[pl.ds(pl.multiple_of(j * 64, 64), 64), :] - peak)
        return total + jnp.sum(rows.reshape(8, 8, 512), axis=0)

    total = lax.fori_loop(0, 8, add, jnp.zeros((8, 512), F32))
    total = total + jnp.exp(hq[...] - peak) * jnp.where(c == 0, 1.0, 0.0)
    total = jnp.sum(total, axis=0, keepdims=True)
    square = st[pl.ds(pl.multiple_of(xy * 64, 64), 64), pl.ds(pl.multiple_of(t * 128, 128), 128)]
    on_diagonal = lax.broadcasted_iota(jnp.int32, (64, 128), 1) == (
        lax.broadcasted_iota(jnp.int32, (64, 128), 0) + c * 64
    )
    positive = jnp.sum(jnp.where(on_diagonal, square, 0.0), axis=0, keepdims=True)
    positive = positive * jnp.where(holder, 1.0, 0.0)
    positive = jnp.concatenate([positive] * 4, axis=1)
    here = lax.broadcasted_iota(jnp.int32, (1, 512), 1) // 128 == t
    positive = jnp.where(here, positive, 0.0)
    sub8w = lax.broadcasted_iota(jnp.int32, (8, 512), 0)
    stat_out[...] = jnp.where(sub8w == 0, peak, jnp.where(sub8w == 1, total, positive))
    stat_in[me_r] = stat_out[...]

    def stat_copy(r, slot):
        return remote(stat_out, stat_in.at[slot], row_s.at[r], row_r.at[slot], row_dev(r))

    loop(15, lambda k: stat_copy((me_r + k + 1) % 16, me_r).start())

    def stat_wait(k):
        r = (me_r + k + 1) % 16
        stat_copy(r, r).wait_recv()

    loop(15, stat_wait)
    peak = stat_in[0, 0:1, :]
    for r in range(1, 16):
        peak = jnp.maximum(peak, stat_in[r, 0:1, :])
    total = jnp.zeros((1, 512), F32)
    positive = jnp.zeros((1, 512), F32)
    for r in range(16):
        total = total + stat_in[r, 1:2, :] * jnp.exp(stat_in[r, 0:1, :] - peak)
        positive = positive + stat_in[r, 2:3, :]
    log_total = peak + jnp.log(total)
    lrow[...] = log_total - positive

    hcq = jnp.exp(hq[...] - log_total)
    hq[...] = hcq
    chances = columns(hq).T
    for a in range(8):
        hc_out[a] = chances[a : a + 1, :]
    hc_in[me_p] = hc_out[xy]

    def prob_copy(p, slot):
        return remote(
            hc_out.at[p // 2], hc_in.at[slot], plane_s.at[PROB, p], plane_r.at[PROB, slot], plane_dev(p)
        )

    loop(15, lambda k: prob_copy((me_p + k + 1) % 16, me_p).start())

    def chance(j):
        rows = pl.ds(pl.multiple_of(j * 64, 64), 64)
        st[rows, :] = jnp.exp(st[rows, :] - log_total)

    loop(8, chance)

    def doc_grad(k):
        part, core = k // 2, k % 2
        value = mm(st[...], q_all[core, part].reshape(512, 192), NN, HIGHEST)
        g3_out[:, part, core] = value.reshape(8, 64, 192)

    loop(4, doc_grad)

    def dgrad_copy(p, slot):
        return remote(
            g3_out.at[p // 2, p % 2], g3_in.at[slot],
            plane_s.at[DGRAD, p], plane_r.at[DGRAD, slot], plane_dev(p),
        )

    loop(15, lambda k: dgrad_copy((me_p + k + 1) % 16, me_p).start())
    g3_in[me_p] = g3_out[xy, yh]

    ch[...] = st[...].T

    def query_grad_sib(part):
        g_sib_out[part] = mm(ch[...], d_all[part, 1 - c].reshape(512, 192), NN, HIGHEST)

    loop(2, query_grad_sib)
    sib_g = remote(g_sib_out, g_sib_in, one_s.at[SIB_G], one_r.at[SIB_G], sibling)
    sib_g.start()

    filler = jnp.zeros((120, 512), F32)
    sid_t = jnp.concatenate([sid[...], filler], axis=0).T
    hc_t = jnp.concatenate([hq[...], filler], axis=0).T
    lane512 = lax.broadcasted_iota(jnp.int32, (512, 128), 1).astype(F32)
    for a in range(8):
        wcat[:, a * 128 : (a + 1) * 128] = jnp.where(
            sid_t[:, a : a + 1] == lane512, hc_t[:, a : a + 1], 0.0
        )

    def query_grad(part):
        value = mm(ch[...], d_all[part, c].reshape(512, 192), NN, HIGHEST)
        value = value + mm(wcat[...], p_in[part].reshape(1024, 192), NN, HIGHEST)
        g_out[:, part] = value.reshape(4, 128, 192)

    loop(2, query_grad)
    sib_g.wait_recv()
    for part in range(2):
        g_out[:, part] += g_sib_in[part].reshape(4, 128, 192)

    def grad_copy(tt, slot):
        return remote(g_out.at[tt], g_in.at[slot], gs.at[tt], gr.at[slot], z_dev(2 * tt + yh))

    def grad_send(tt):
        @pl.when(2 * tt + yh != z)
        def _():
            grad_copy(tt, z).start()

    loop(4, grad_send)

    @pl.when(holder)
    def _():
        g_in[z] = g_out[t]

    def query_wait(k):
        p = (me_p + k + 1) % 16
        query_copy(p, p).wait_recv()
        prob_copy(p, p).wait_recv()

    loop(15, query_wait)
    chances = jnp.concatenate([hc_in[i] for i in range(16)] + [jnp.zeros((112, 128), F32)], axis=0).T

    def turn(i):
        col = jnp.sum(jnp.where(lane128 == i, chances, 0.0), axis=1, keepdims=True)
        terms = split3((f_in[i] * (col * SCALE)).T)
        for k in range(3):
            at_s[k, :, pl.ds(pl.multiple_of(i * 128, 128), 128)] = terms[k]

    loop(16, turn)
    lane256 = lax.broadcasted_iota(jnp.int32, (128, 256), 1).astype(F32) + 1.0

    def pool_grad(n):
        base = (n * 256).astype(F32)
        hots = jnp.concatenate(
            [
                jnp.where(lt[:, i : i + 1] == lane256 + base, 1.0, 0.0).astype(BF16)
                for i in range(16)
            ],
            axis=0,
        )
        value = mm(at_s[0], hots, NN) + mm(at_s[1], hots, NN) + mm(at_s[2], hots, NN)
        gp_ref[:, pl.ds(pl.multiple_of(n * 256, 256), 256)] = value

    loop(8, pool_grad)

    def dgrad_wait(k):
        p = (me_p + k + 1) % 16
        dgrad_copy(p, p).wait_recv()

    loop(15, dgrad_wait)

    def sum_docs(core):
        value = g3_in[0, core]
        for p in range(1, 16):
            value = value + g3_in[p, core]
        return value

    dd_out[...] = sum_docs(1 - c)
    sib_dd = remote(dd_out, dd_sib, one_s.at[SIB_DD], one_r.at[SIB_DD], sibling)
    sib_dd.start()
    mine = pl.ds(pl.multiple_of(c * 64, 64), 64)
    dd_ref[mine, :] = (sum_docs(c) - q_ref[mine, :]) * SCALE

    part_dq = remote(dq_out, dq_in, one_s.at[PART_DQ], one_r.at[PART_DQ], partner)
    part_l = remote(loss_out, loss_in, one_s.at[PART_L], one_r.at[PART_L], partner)

    @pl.when(holder)
    def _():
        loss_out[...] = lrow[:, pl.ds(pl.multiple_of(t * 128, 128), 128)]
        part_l.start()

        def wait(k):
            zz = (z + k + 1) % 8
            grad_copy(t, zz).wait_recv()

        loop(7, wait)

        def sum_queries(part):
            value = g_in[0, part]
            for zz in range(1, 8):
                value = value + g_in[zz, part]
            return value

        dq_out[...] = sum_queries(1 - yh)
        part_dq.start()
        dq_ref[...] = (sum_queries(yh) - d_ref[...]) * SCALE
        loss_ref[...] = loss_out[...]

    @pl.when(jnp.logical_not(holder))
    def _():
        part_l.wait_recv()
        loss_ref[...] = loss_in[...]
        part_dq.wait_recv()
        dq_ref[...] = (dq_in[...] - d_ref[...]) * SCALE

    sib_dd.wait_recv()
    other = pl.ds(pl.multiple_of((1 - c) * 64, 64), 64)
    dd_ref[other, :] = (dd_sib[...] - q_ref[other, :]) * SCALE

    sib_d.wait_send()
    sib_q.wait_send()
    sib_h.wait_send()
    sib_g.wait_send()
    sib_dd.wait_send()

    def sent(k):
        p = (me_p + k + 1) % 16
        for copy in (doc_copy, req_copy, rows_copy, query_copy, prob_copy, dgrad_copy):
            copy(p, me_p).wait_send()
        stat_copy((me_r + k + 1) % 16, me_r).wait_send()

    loop(15, sent)

    def grad_sent(tt):
        @pl.when(2 * tt + yh != z)
        def _():
            grad_copy(tt, z).wait_send()

    loop(4, grad_sent)

    @pl.when(holder)
    def _():
        def z_sent(k):
            zz = (z + k + 1) % 8
            idx_copy(zz).wait_send()
            q_copy(yh, zz).wait_send()
            q_copy(1 - yh, zz).wait_send()

        loop(7, z_sent)
        part_l.wait_send()
        part_dq.wait_send()

    @pl.when(jnp.logical_not(holder))
    def _():
        part_q.wait_send()


def per_device(question_matrix, document_matrix, pool, hard_owner, hard_local):
    index = jnp.concatenate([hard_owner.T, hard_local.T], axis=0)
    vmem = pl.BlockSpec(memory_space=pltpu.VMEM)
    f = lambda *shape: pltpu.VMEM(shape, F32)
    scratch = [
        pltpu.VMEM((4, 16, 128), jnp.int32),
        f(2, 2, 4, 128, 192),
        f(2, 64, 192),
        f(2, 2, 8, 64, 192),
        f(8, 512),
        f(8, 512),
        f(8, 1, 128),
        f(16, 1, 128),
        f(128, 128),
        pltpu.VMEM((3, 192, 2048), BF16),
        f(16, 128, 192),
        f(2, 8, 128, 192),
        f(16, 128, 192),
        f(16, 128, 192),
        f(128, 128),
        f(128, 128),
        f(8, 512),
        f(512, 512),
        f(512, 512),
        f(8, 512),
        f(16, 8, 512),
        f(8, 1, 128),
        f(16, 1, 128),
        f(8, 2, 2, 64, 192),
        f(16, 2, 64, 192),
        f(64, 192),
        f(2, 512, 192),
        f(2, 512, 192),
        f(4, 2, 128, 192),
        f(8, 2, 128, 192),
        f(512, 1024),
        pltpu.VMEM((3, 192, 2048), BF16),
        f(128, 192),
        f(128, 192),
        f(1, 128),
        f(1, 128),
        f(64, 192),
        f(1, 512),
        pltpu.SemaphoreType.DMA((6, 16)),
        pltpu.SemaphoreType.DMA((6, 16)),
        pltpu.SemaphoreType.DMA((16,)),
        pltpu.SemaphoreType.DMA((16,)),
        pltpu.SemaphoreType.DMA((8,)),
        pltpu.SemaphoreType.DMA((4,)),
        pltpu.SemaphoreType.DMA((2, 8)),
        pltpu.SemaphoreType.DMA((2, 4)),
        pltpu.SemaphoreType.DMA((4,)),
        pltpu.SemaphoreType.DMA((8,)),
        pltpu.SemaphoreType.DMA((8,)),
        pltpu.SemaphoreType.DMA((8,)),
    ]
    loss, dq, dd, gp = pl.pallas_call(
        kernel,
        name="retriever_step",
        out_shape=(
            jax.ShapeDtypeStruct((1, 128), F32),
            jax.ShapeDtypeStruct((128, 192), F32),
            jax.ShapeDtypeStruct((128, 192), F32),
            jax.ShapeDtypeStruct((192, 2048), F32),
        ),
        in_specs=[vmem] * 4,
        out_specs=(vmem,) * 4,
        scratch_shapes=scratch,
        compiler_params=pltpu.CompilerParams(
            collective_id=0, has_side_effects=True, vmem_limit_bytes=60 * 1024 * 1024
        ),
    )(question_matrix, document_matrix, pool, index)
    return loss.reshape(128), dq, dd, gp


def solution(mesh):
    placed = (P("blk", "dim"), P("blk", "dim"), P("dim", "blk"), P("blk", None), P("blk", None))
    return jax.shard_map(
        per_device,
        mesh=mesh,
        in_specs=placed,
        out_specs=(P("blk"), P("blk", "dim"), P("blk", "dim"), P("dim", "blk")),
        check_vma=False,
    )
```

```python
import jax
import jax.numpy as jnp
from jax import lax
from jax.experimental import pallas as pl
from jax.experimental.pallas import tpu as pltpu
from jax.sharding import PartitionSpec as P

MESH = pl.DeviceIdType.MESH
F32 = jnp.float32
BF16 = jnp.bfloat16
HIGHEST = lax.Precision.HIGHEST
SCALE = 20.0

NT = (((1,), (1,)), ((), ()))
NN = (((1,), (0,)), ((), ()))


def mm(a, b, dims, precision=None):
    return lax.dot_general(a, b, dims, precision=precision, preferred_element_type=F32)


def split3(x):
    high = x.astype(BF16)
    rest = x - high.astype(F32)
    mid = rest.astype(BF16)
    low = (rest - mid.astype(F32)).astype(BF16)
    return high, mid, low


def loop(count, body):
    def step(i, carry):
        body(i)
        return carry

    lax.fori_loop(0, count, step, 0)


def halves(x):
    return x[:, :128], x[:, 128:256], x[:, 256:384]


def low(rows):
    return lax.broadcasted_iota(jnp.int32, (rows, 128), 1) < 64


def turned(x):
    return pltpu.roll(x, 64, 1)


def fold(a, b):
    keep = low(a.shape[0])
    b0, b1 = turned(b[:, :128]), turned(b[:, 128:256])
    return jnp.concatenate(
        [a[:, :128], jnp.where(keep, a[:, 128:256], b0), jnp.where(keep, b0, b1)], axis=1
    )


def unfold(x):
    x0, x1, x2 = halves(x)
    x1t, x2t = turned(x1), turned(x2)
    return (
        jnp.concatenate([x0, x1], axis=1),
        jnp.concatenate([jnp.where(low(x.shape[0]), x1t, x2t), x2t], axis=1),
    )


def regroup(x, y):
    x0, x1, x2 = halves(x)
    y0, y1, y2 = halves(y)
    keep = low(x.shape[0])
    x1t, x2t, y0t, y1t = turned(x1), turned(x2), turned(y0), turned(y1)
    first = jnp.concatenate([x0, jnp.where(keep, x1, y0t), jnp.where(keep, y0t, y1t)], axis=1)
    last = jnp.concatenate([jnp.where(keep, x1t, x2t), jnp.where(keep, x2t, y1), y2], axis=1)
    return first, last


def upright(x):
    return jnp.concatenate([x, jnp.zeros((64, 128), F32)], axis=0).T


REQ, DOC, ROWS, QUERY, DGRAD, PROB = range(6)
SIB_D, SIB_Q, SIB_H, SIB_G, SIB_DD, PART_Q, PART_DQ, PART_L = range(8)


def kernel(
    q_ref, d_ref, pool_ref, owner_ref, local_ref,
    loss_ref, dq_ref, dd_ref, gp_ref,
    idx_mine, idx_all, q_part, q_all, q_re, d_nat, d_sib, d_mine, d_raw, d_all, lr_all, sid,
    rq_out, rq_in, lt, pool_s,
    p_out, p_in, p_all, f_out, f_in, hs_mine, hs_sib, hq, st, ch, stat_out, stat_in,
    hc_out, hc_in, g3_out, g3_in, dd_out, dd_sib, dd_nat, g_sib_out, g_sib_in, g_out, g_in, wcat, at_s,
    dq_out, dq_in, loss_out, loss_in, lrow,
    plane_s, plane_r, row_s, row_r, idx_s, idx_r, qs, qr, gs, gr, one_s, one_r,
):
    blk, dim = lax.axis_index("blk"), lax.axis_index("dim")
    xy, z = blk // 8, blk % 8
    yh, c = dim // 2, dim % 2
    t = z // 2
    holder = (z % 2) == yh
    me_p = xy * 2 + yh
    me_r = z * 2 + c

    def plane_dev(p):
        return ((p // 2) * 8 + z, (p % 2) * 2 + c)

    def row_dev(r):
        return (xy * 8 + r // 2, yh * 2 + r % 2)

    def z_dev(zz):
        return (xy * 8 + zz, dim)

    sibling = (blk, yh * 2 + (1 - c))
    partner = (blk, (1 - yh) * 2 + c)

    def remote(src, dst, send, recv, device):
        return pltpu.make_async_remote_copy(
            src_ref=src, dst_ref=dst, send_sem=send, recv_sem=recv,
            device_id=device, device_id_type=MESH,
        )

    barrier = pltpu.get_barrier_semaphore()

    def greet(k):
        pl.semaphore_signal(barrier, inc=1, device_id=plane_dev((me_p + k + 1) % 16), device_id_type=MESH)
        pl.semaphore_signal(barrier, inc=1, device_id=row_dev((me_r + k + 1) % 16), device_id_type=MESH)

    loop(15, greet)
    idx_mine[0:8] = owner_ref[...]
    idx_mine[8:16] = local_ref[...]
    d_nat[...] = upright(d_ref[...])
    pl.semaphore_wait(barrier, 30)

    def idx_copy(zz):
        return remote(idx_mine, idx_all.at[t], idx_s.at[zz], idx_r.at[t], z_dev(zz))

    def q_copy(zz):
        return remote(q_all.at[c, t], q_all.at[c, t], qs.at[zz], qr.at[t], z_dev(zz))

    sib_d = remote(
        d_nat.at[pl.ds((1 - c) * 64, 64)], d_sib, one_s.at[SIB_D], one_r.at[SIB_D], sibling
    )
    part_q = remote(q_ref, q_part, one_s.at[PART_Q], one_r.at[PART_Q], partner)

    @pl.when(holder)
    def _():
        loop(7, lambda k: idx_copy((z + k + 1) % 8).start())
        idx_all[t] = idx_mine[...]

    sib_d.start()

    @pl.when(jnp.logical_not(holder))
    def _():
        part_q.start()

    for k, part in enumerate(split3(pool_ref[...])):
        pool_s[k, 0:192] = part
        pool_s[k, 192:256] = jnp.zeros((64, 2048), BF16)

    def idx_wait(tt):
        @pl.when(2 * tt + yh != z)
        def _():
            remote(idx_mine, idx_all.at[tt], idx_s.at[0], idx_r.at[tt], partner).wait_recv()

    loop(4, idx_wait)
    sub8 = lax.broadcasted_iota(jnp.int32, (8, 128), 0)
    upper = jnp.where(
        lax.broadcasted_iota(jnp.int32, (128, 128), 0) < lax.broadcasted_iota(jnp.int32, (128, 128), 1),
        1.0, 0.0,
    ).astype(BF16)
    for tt in range(4):
        owner = idx_all[tt, 0:8]
        local = idx_all[tt, 8:16] + 1
        table = jnp.zeros((8, 128), jnp.int32)
        for a in range(8):
            row = jnp.sum(jnp.where(owner == a * 8 + z, local, 0), axis=0, keepdims=True)
            table = jnp.where(sub8 == a, row, table)
        marks = jnp.where(table > 0, 1.0, 0.0)
        rank = mm(marks.astype(BF16), upper, NN)
        lr_all[:, tt * 128 : (tt + 1) * 128] = table.astype(F32)
        sid[:, tt * 128 : (tt + 1) * 128] = jnp.where(table > 0, rank + float(tt * 32), -1.0)

    sub512 = lax.broadcasted_iota(jnp.int32, (128, 512), 0).astype(F32)
    lane128 = lax.broadcasted_iota(jnp.int32, (128, 128), 1)

    def hot(a):
        return sub512 == sid[pl.ds(a, 1), :]

    def columns(rows):
        def step(a, table):
            col = jnp.sum(jnp.where(hot(a), rows[pl.ds(a, 1), :], 0.0), axis=1, keepdims=True)
            return jnp.where(lane128 == a, col, table)

        return lax.fori_loop(0, 8, step, jnp.zeros((128, 128), F32))

    wanted = columns(lr_all).T
    for a in range(8):
        rq_out[a] = wanted[a : a + 1, :]
    rq_in[me_p] = rq_out[xy]

    def req_copy(p, slot):
        return remote(
            rq_out.at[p // 2], rq_in.at[slot], plane_s.at[REQ, p], plane_r.at[REQ, slot], plane_dev(p)
        )

    loop(15, lambda k: req_copy((me_p + k + 1) % 16, me_p).start())

    @pl.when(holder)
    def _():
        remote(q_ref, q_part, one_s.at[PART_Q], one_r.at[PART_Q], partner).wait_recv()
        own, other = upright(q_ref[...]), upright(q_part[...])
        q_all[c, t] = fold(jnp.where(yh == 0, own, other), jnp.where(yh == 0, other, own))
        loop(7, lambda k: q_copy((z + k + 1) % 8).start())

    sib_d.wait_recv()
    own_d = d_nat[pl.ds(pl.multiple_of(c * 64, 64), 64), :]
    d_mine[...] = fold(jnp.where(c == 0, own_d, d_sib[...]), jnp.where(c == 0, d_sib[...], own_d))

    def doc_copy(p, slot):
        return remote(
            d_mine, d_raw.at[slot % 2, slot // 2],
            plane_s.at[DOC, p], plane_r.at[DOC, slot], plane_dev(p),
        )

    loop(15, lambda k: doc_copy((me_p + k + 1) % 16, me_p).start())
    d_raw[yh, xy] = d_mine[...]

    def req_wait(k):
        p = (me_p + k + 1) % 16
        req_copy(p, p).wait_recv()

    loop(15, req_wait)
    named = jnp.concatenate([rq_in[i] for i in range(16)] + [jnp.zeros((112, 128), F32)], axis=0)
    lt[...] = named.T
    lane2048 = lax.broadcasted_iota(jnp.int32, (128, 2048), 1).astype(F32) + 1.0

    def rows_copy(p, slot):
        return remote(
            p_out.at[p], p_in.at[slot % 2, slot // 2],
            plane_s.at[ROWS, p], plane_r.at[ROWS, slot], plane_dev(p),
        )

    def fetch(g):
        hots = []
        for i in range(4):
            col = jnp.sum(jnp.where(lane128 == g * 4 + i, lt[...], 0.0), axis=1, keepdims=True)
            hots.append(jnp.where(col == lane2048, 1.0, 0.0).astype(BF16))
        hots = jnp.concatenate(hots, axis=0)
        got = mm(hots, pool_s[0], NT) + mm(hots, pool_s[1], NT) + mm(hots, pool_s[2], NT)
        for i in range(4):
            p = g * 4 + i
            p_out[p] = fold(got[i * 128 : i * 128 + 64], got[i * 128 + 64 : i * 128 + 128])

            @pl.when(p != me_p)
            def _():
                rows_copy(p, me_p).start()

    loop(4, fetch)
    p_in[yh, xy] = p_out[me_p]

    def q_wait(tt):
        @pl.when(2 * tt + yh != z)
        def _():
            remote(q_all.at[c, tt], q_all.at[c, tt], qs.at[0], qr.at[tt], partner).wait_recv()

    loop(4, q_wait)
    sib_q = remote(q_all.at[c], q_all.at[c], one_s.at[SIB_Q], one_r.at[SIB_Q], sibling)
    sib_q.start()

    queries = split3(q_all[c].reshape(512, 384))

    def pick(g):
        hots = jnp.concatenate(
            [jnp.where(hot(g * 4 + i), 1.0, 0.0).astype(BF16) for i in range(4)], axis=0
        )
        got = mm(hots, queries[0], NN) + mm(hots, queries[1], NN) + mm(hots, queries[2], NN)
        for i in range(4):
            first, last = regroup(got[i * 128 : i * 128 + 64], got[i * 128 + 64 : i * 128 + 128])
            f_out[(g * 4 + i) * 2] = first
            f_out[(g * 4 + i) * 2 + 1] = last

    loop(2, pick)
    f_in[me_p] = f_out[me_p]

    remote(q_all.at[c], q_all.at[1 - c], one_s.at[SIB_Q], one_r.at[SIB_Q], sibling).wait_recv()

    def rearrange_q(tt):
        first, last = regroup(q_all[0, tt], q_all[1, tt])
        q_re[0, tt] = first
        q_re[1, tt] = last

    loop(4, rearrange_q)

    def doc_wait(k):
        p = (me_p + k + 1) % 16
        doc_copy(p, p).wait_recv()

    loop(15, doc_wait)

    def score(j):
        total = None
        for part in range(2):
            docs = d_raw[part, pl.ds(j * 4, 4)].reshape(256, 384)
            value = mm(docs, q_re[part].reshape(512, 384), NT, HIGHEST)
            total = value if total is None else total + value
        st[pl.ds(pl.multiple_of(j * 256, 256), 256), :] = total * SCALE

    loop(2, score)

    def top(j, best):
        rows = st[pl.ds(pl.multiple_of(j * 64, 64), 64), :].reshape(8, 8, 512)
        return jnp.maximum(best, jnp.max(rows, axis=0))

    best = lax.fori_loop(0, 8, top, jnp.full((8, 512), -jnp.inf, F32))
    best = jnp.max(best, axis=0, keepdims=True)

    def rows_wait(k):
        p = (me_p + k + 1) % 16
        rows_copy(p, p).wait_recv()

    loop(15, rows_wait)
    low64 = low(64)

    def hard_part(a, table):
        terms = p_in[0, a] * f_out[a * 2] + p_in[1, a] * f_out[a * 2 + 1]
        t0, t1, t2 = halves(terms)
        first = jnp.sum(t0 + jnp.where(low64, t1, 0.0), axis=1, keepdims=True)
        last = jnp.sum(t2 + jnp.where(low64, 0.0, t1), axis=1, keepdims=True)
        return jnp.where(lane128 == a, jnp.concatenate([first, last], axis=0), table)

    hs_mine[...] = lax.fori_loop(0, 8, hard_part, jnp.zeros((128, 128), F32))
    sib_h = remote(hs_mine, hs_sib, one_s.at[SIB_H], one_r.at[SIB_H], sibling)
    sib_h.start()

    def query_copy(p, slot):
        return remote(
            f_out.at[p], f_in.at[slot], plane_s.at[QUERY, p], plane_r.at[QUERY, slot], plane_dev(p)
        )

    loop(15, lambda k: query_copy((me_p + k + 1) % 16, me_p).start())

    sib_h.wait_recv()
    hard = (hs_mine[...] + hs_sib[...]) * SCALE
    for a in range(8):
        row = jnp.sum(jnp.where(hot(a), hard[:, a : a + 1], 0.0), axis=0, keepdims=True)
        hq[a : a + 1, :] = jnp.where(sid[a : a + 1, :] >= 0.0, row, -jnp.inf)
    peak = jnp.maximum(best, jnp.max(hq[...], axis=0, keepdims=True))

    def add(j, total):
        rows = jnp.exp(st[pl.ds(pl.multiple_of(j * 64, 64), 64), :] - peak)
        return total + jnp.sum(rows.reshape(8, 8, 512), axis=0)

    total = lax.fori_loop(0, 8, add, jnp.zeros((8, 512), F32))
    total = total + jnp.exp(hq[...] - peak) * jnp.where(c == 0, 1.0, 0.0)
    total = jnp.sum(total, axis=0, keepdims=True)
    square = st[pl.ds(pl.multiple_of(xy * 64, 64), 64), pl.ds(pl.multiple_of(t * 128, 128), 128)]
    on_diagonal = lax.broadcasted_iota(jnp.int32, (64, 128), 1) == (
        lax.broadcasted_iota(jnp.int32, (64, 128), 0) + c * 64
    )
    positive = jnp.sum(jnp.where(on_diagonal, square, 0.0), axis=0, keepdims=True)
    positive = positive * jnp.where(holder, 1.0, 0.0)
    positive = jnp.concatenate([positive] * 4, axis=1)
    here = lax.broadcasted_iota(jnp.int32, (1, 512), 1) // 128 == t
    positive = jnp.where(here, positive, 0.0)
    sub8w = lax.broadcasted_iota(jnp.int32, (8, 512), 0)
    stat_out[...] = jnp.where(sub8w == 0, peak, jnp.where(sub8w == 1, total, positive))
    stat_in[me_r] = stat_out[...]

    def stat_copy(r, slot):
        return remote(stat_out, stat_in.at[slot], row_s.at[r], row_r.at[slot], row_dev(r))

    loop(15, lambda k: stat_copy((me_r + k + 1) % 16, me_r).start())

    def rearrange_d(k):
        first, last = regroup(d_raw[0, k], d_raw[1, k])
        d_all[0, k] = first
        d_all[1, k] = last
        first, last = regroup(p_in[0, k], p_in[1, k])
        p_all[k, 0:64] = first
        p_all[k, 64:128] = last

    loop(8, rearrange_d)
    filler = jnp.zeros((120, 512), F32)
    sid_t = jnp.concatenate([sid[...], filler], axis=0).T

    def stat_wait(k):
        r = (me_r + k + 1) % 16
        stat_copy(r, r).wait_recv()

    loop(15, stat_wait)
    peak = stat_in[0, 0:1, :]
    for r in range(1, 16):
        peak = jnp.maximum(peak, stat_in[r, 0:1, :])
    total = jnp.zeros((1, 512), F32)
    positive = jnp.zeros((1, 512), F32)
    for r in range(16):
        total = total + stat_in[r, 1:2, :] * jnp.exp(stat_in[r, 0:1, :] - peak)
        positive = positive + stat_in[r, 2:3, :]
    log_total = peak + jnp.log(total)
    lrow[...] = log_total - positive

    hq[...] = jnp.exp(hq[...] - log_total)

    def chance(j):
        rows = pl.ds(pl.multiple_of(j * 128, 128), 128)
        value = jnp.exp(st[rows, :] - log_total)
        st[rows, :] = value
        ch[:, rows] = value.T

    loop(4, chance)

    g_sib_out[...] = mm(ch[...], d_all[1 - c].reshape(512, 384), NN, HIGHEST)
    sib_g = remote(g_sib_out, g_sib_in, one_s.at[SIB_G], one_r.at[SIB_G], sibling)
    sib_g.start()
    hc_t = jnp.concatenate([hq[...], filler], axis=0).T
    lane512 = lax.broadcasted_iota(jnp.int32, (512, 128), 1).astype(F32)
    for a in range(8):
        wcat[:, a * 128 : (a + 1) * 128] = jnp.where(
            sid_t[:, a : a + 1] == lane512, hc_t[:, a : a + 1], 0.0
        )
    g_own = mm(ch[...], d_all[c].reshape(512, 384), NN, HIGHEST)
    g_own = g_own + mm(wcat[...], p_all[...].reshape(1024, 384), NN, HIGHEST)
    sib_g.wait_recv()
    g_out[...] = (g_own + g_sib_in[...]).reshape(4, 128, 384)

    def grad_copy(tt, slot):
        return remote(g_out.at[tt], g_in.at[slot], gs.at[tt], gr.at[slot], z_dev(2 * tt + yh))

    def grad_send(tt):
        @pl.when(2 * tt + yh != z)
        def _():
            grad_copy(tt, z).start()

    loop(4, grad_send)

    @pl.when(holder)
    def _():
        g_in[z] = g_out[t]

    def doc_grad(part):
        value = mm(st[...], q_re[part].reshape(512, 384), NN, HIGHEST)
        g3_out[:, part] = value.reshape(8, 64, 384)

    loop(2, doc_grad)

    def dgrad_copy(p, slot):
        return remote(
            g3_out.at[p // 2, p % 2], g3_in.at[slot],
            plane_s.at[DGRAD, p], plane_r.at[DGRAD, slot], plane_dev(p),
        )

    chances = columns(hq).T
    for a in range(8):
        hc_out[a] = chances[a : a + 1, :]
    hc_in[me_p] = hc_out[xy]

    def prob_copy(p, slot):
        return remote(
            hc_out.at[p // 2], hc_in.at[slot], plane_s.at[PROB, p], plane_r.at[PROB, slot], plane_dev(p)
        )

    loop(15, lambda k: prob_copy((me_p + k + 1) % 16, me_p).start())
    loop(15, lambda k: dgrad_copy((me_p + k + 1) % 16, me_p).start())
    g3_in[me_p] = g3_out[xy, yh]

    def query_wait(k):
        p = (me_p + k + 1) % 16
        query_copy(p, p).wait_recv()
        prob_copy(p, p).wait_recv()

    loop(15, query_wait)
    chances = jnp.concatenate([hc_in[i] for i in range(16)] + [jnp.zeros((112, 128), F32)], axis=0).T

    def turn(i):
        col = jnp.sum(jnp.where(lane128 == i, chances, 0.0), axis=1, keepdims=True)
        rows = jnp.concatenate(unfold(f_in[i]), axis=0) * (col * SCALE)
        terms = split3(rows.T[0:192])
        for k in range(3):
            at_s[k, :, pl.ds(pl.multiple_of(i * 128, 128), 128)] = terms[k]

    loop(16, turn)
    lane256 = lax.broadcasted_iota(jnp.int32, (128, 256), 1).astype(F32) + 1.0

    def pool_grad(n):
        base = (n * 256).astype(F32)
        hots = jnp.concatenate(
            [
                jnp.where(lt[:, i : i + 1] == lane256 + base, 1.0, 0.0).astype(BF16)
                for i in range(16)
            ],
            axis=0,
        )
        value = mm(at_s[0], hots, NN) + mm(at_s[1], hots, NN) + mm(at_s[2], hots, NN)
        gp_ref[:, pl.ds(pl.multiple_of(n * 256, 256), 256)] = value

    loop(8, pool_grad)

    part_dq = remote(dq_out, dq_in, one_s.at[PART_DQ], one_r.at[PART_DQ], partner)
    part_l = remote(loss_out, loss_in, one_s.at[PART_L], one_r.at[PART_L], partner)

    @pl.when(holder)
    def _():
        loss_out[...] = lrow[:, pl.ds(pl.multiple_of(t * 128, 128), 128)]
        part_l.start()

        def wait(k):
            zz = (z + k + 1) % 8
            grad_copy(t, zz).wait_recv()

        loop(7, wait)
        value = g_in[0]
        for zz in range(1, 8):
            value = value + g_in[zz]
        first, last = unfold(value)
        dq_out[...] = jnp.where(yh == 0, last, first).T[0:192]
        part_dq.start()
        dq_ref[...] = (jnp.where(yh == 0, first, last).T[0:192] - d_ref[...]) * SCALE
        loss_ref[...] = loss_out[...]

    def dgrad_wait(k):
        p = (me_p + k + 1) % 16
        dgrad_copy(p, p).wait_recv()

    loop(15, dgrad_wait)
    value = g3_in[0]
    for p in range(1, 16):
        value = value + g3_in[p]
    first, last = unfold(value)
    dd_out[...] = jnp.where(c == 0, last, first)
    sib_dd = remote(dd_out, dd_sib, one_s.at[SIB_DD], one_r.at[SIB_DD], sibling)
    sib_dd.start()
    dd_nat[pl.ds(pl.multiple_of(c * 64, 64), 64), :] = jnp.where(c == 0, first, last)

    @pl.when(jnp.logical_not(holder))
    def _():
        part_l.wait_recv()
        loss_ref[...] = loss_in[...]
        part_dq.wait_recv()
        dq_ref[...] = (dq_in[...] - d_ref[...]) * SCALE

    sib_dd.wait_recv()
    dd_nat[pl.ds(pl.multiple_of((1 - c) * 64, 64), 64), :] = dd_sib[...]
    dd_ref[...] = (dd_nat[...].T[0:192] - q_ref[...]) * SCALE

    sib_d.wait_send()
    sib_q.wait_send()
    sib_h.wait_send()
    sib_g.wait_send()
    sib_dd.wait_send()

    def sent(k):
        p = (me_p + k + 1) % 16
        for copy in (doc_copy, req_copy, rows_copy, query_copy, prob_copy, dgrad_copy):
            copy(p, me_p).wait_send()
        stat_copy((me_r + k + 1) % 16, me_r).wait_send()

    loop(15, sent)

    def grad_sent(tt):
        @pl.when(2 * tt + yh != z)
        def _():
            grad_copy(tt, z).wait_send()

    loop(4, grad_sent)

    @pl.when(holder)
    def _():
        def z_sent(k):
            zz = (z + k + 1) % 8
            idx_copy(zz).wait_send()
            q_copy(zz).wait_send()

        loop(7, z_sent)
        part_l.wait_send()
        part_dq.wait_send()

    @pl.when(jnp.logical_not(holder))
    def _():
        part_q.wait_send()


def per_device(question_matrix, document_matrix, pool, hard_owner, hard_local):
    vmem = pl.BlockSpec(memory_space=pltpu.VMEM)
    f = lambda *shape: pltpu.VMEM(shape, F32)
    scratch = [
        pltpu.VMEM((16, 128), jnp.int32),
        pltpu.VMEM((4, 16, 128), jnp.int32),
        f(192, 128),
        f(2, 4, 128, 384),
        f(2, 4, 128, 384),
        f(128, 256),
        f(64, 256),
        f(64, 384),
        f(2, 8, 64, 384),
        f(2, 8, 64, 384),
        f(8, 512),
        f(8, 512),
        f(8, 1, 128),
        f(16, 1, 128),
        f(128, 128),
        pltpu.VMEM((3, 256, 2048), BF16),
        f(16, 64, 384),
        f(2, 8, 64, 384),
        f(8, 128, 384),
        f(16, 64, 384),
        f(16, 64, 384),
        f(128, 128),
        f(128, 128),
        f(8, 512),
        f(512, 512),
        f(512, 512),
        f(8, 512),
        f(16, 8, 512),
        f(8, 1, 128),
        f(16, 1, 128),
        f(8, 2, 64, 384),
        f(16, 64, 384),
        f(64, 256),
        f(64, 256),
        f(128, 256),
        f(512, 384),
        f(512, 384),
        f(4, 128, 384),
        f(8, 128, 384),
        f(512, 1024),
        pltpu.VMEM((3, 192, 2048), BF16),
        f(192, 128),
        f(192, 128),
        f(1, 128),
        f(1, 128),
        f(1, 512),
        pltpu.SemaphoreType.DMA((6, 16)),
        pltpu.SemaphoreType.DMA((6, 16)),
        pltpu.SemaphoreType.DMA((16,)),
        pltpu.SemaphoreType.DMA((16,)),
        pltpu.SemaphoreType.DMA((8,)),
        pltpu.SemaphoreType.DMA((4,)),
        pltpu.SemaphoreType.DMA((8,)),
        pltpu.SemaphoreType.DMA((4,)),
        pltpu.SemaphoreType.DMA((4,)),
        pltpu.SemaphoreType.DMA((8,)),
        pltpu.SemaphoreType.DMA((8,)),
        pltpu.SemaphoreType.DMA((8,)),
    ]
    loss, dq, dd, gp = pl.pallas_call(
        kernel,
        name="retriever_step",
        out_shape=(
            jax.ShapeDtypeStruct((1, 128), F32),
            jax.ShapeDtypeStruct((192, 128), F32),
            jax.ShapeDtypeStruct((192, 128), F32),
            jax.ShapeDtypeStruct((192, 2048), F32),
        ),
        in_specs=[vmem] * 5,
        out_specs=(vmem,) * 4,
        scratch_shapes=scratch,
        compiler_params=pltpu.CompilerParams(
            collective_id=0, has_side_effects=True, vmem_limit_bytes=60 * 1024 * 1024
        ),
    )(question_matrix.T, document_matrix.T, pool, hard_owner.T, hard_local.T)
    return loss.reshape(128), dq.T, dd.T, gp


def solution(mesh):
    placed = (P("blk", "dim"), P("blk", "dim"), P("dim", "blk"), P("blk", None), P("blk", None))
    return jax.shard_map(
        per_device,
        mesh=mesh,
        in_specs=placed,
        out_specs=(P("blk"), P("blk", "dim"), P("blk", "dim"), P("dim", "blk")),
        check_vma=False,
    )
```

```python
import jax
import jax.numpy as jnp
from jax import lax
from jax.experimental import pallas as pl
from jax.experimental.pallas import tpu as pltpu
from jax.sharding import PartitionSpec as P

MESH = pl.DeviceIdType.MESH
F32 = jnp.float32
BF16 = jnp.bfloat16
HIGHEST = lax.Precision.HIGHEST
SCALE = 20.0

NT = (((1,), (1,)), ((), ()))
NN = (((1,), (0,)), ((), ()))


def mm(a, b, dims, precision=None):
    return lax.dot_general(a, b, dims, precision=precision, preferred_element_type=F32)


def split3(x):
    high = x.astype(BF16)
    rest = x - high.astype(F32)
    mid = rest.astype(BF16)
    low = (rest - mid.astype(F32)).astype(BF16)
    return high, mid, low


def loop(count, body):
    def step(i, carry):
        body(i)
        return carry

    lax.fori_loop(0, count, step, 0)


def halves(x):
    return x[:, :128], x[:, 128:256], x[:, 256:384]


def low(rows):
    return lax.broadcasted_iota(jnp.int32, (rows, 128), 1) < 64


def turned(x):
    return pltpu.roll(x, 64, 1)


def fold(a, b):
    keep = low(a.shape[0])
    b0, b1 = turned(b[:, :128]), turned(b[:, 128:256])
    return jnp.concatenate(
        [a[:, :128], jnp.where(keep, a[:, 128:256], b0), jnp.where(keep, b0, b1)], axis=1
    )


def unfold(x):
    x0, x1, x2 = halves(x)
    x1t, x2t = turned(x1), turned(x2)
    return (
        jnp.concatenate([x0, x1], axis=1),
        jnp.concatenate([jnp.where(low(x.shape[0]), x1t, x2t), x2t], axis=1),
    )


def regroup(x, y):
    x0, x1, x2 = halves(x)
    y0, y1, y2 = halves(y)
    keep = low(x.shape[0])
    x1t, x2t, y0t, y1t = turned(x1), turned(x2), turned(y0), turned(y1)
    first = jnp.concatenate([x0, jnp.where(keep, x1, y0t), jnp.where(keep, y0t, y1t)], axis=1)
    last = jnp.concatenate([jnp.where(keep, x1t, x2t), jnp.where(keep, x2t, y1), y2], axis=1)
    return first, last


def upright(x):
    return jnp.concatenate([x, jnp.zeros((64, 128), F32)], axis=0).T


REQ, ROWS, QUERY, PROB = range(4)
SIB_D, SIB_Q, SIB_H, SIB_G, SIB_DD, SIB_P, PART_Q, PART_DQ, PART_L = range(9)
DOC_1, DOC_2, GRAD_1, GRAD_2 = range(4)


def kernel(
    q_ref, d_ref, pool_ref, owner_ref, local_ref,
    loss_ref, dq_ref, dd_ref, gp_ref,
    idx_mine, idx_all, q_part, q_all, q_re, d_nat, d_sib, d_raw, d_all, lr_all, sid,
    rq_out, rq_in, lt, pool_s,
    p_out, p_in, p_all, f_out, f_in, hs_mine, hs_sib, hq, st, ch, stat_out, stat_in,
    hc_out, hc_in, g3_out, c1x, c1y, cx, cy, c2x, c2y, dd_out, dd_sib, dd_nat, g_sib_out, g_sib_in, g_out, g_in, wcat, at_s,
    dq_out, dq_in, loss_out, loss_in, pos_out, pos_in, lrow,
    plane_s, plane_r, x_s, x_r, y_s, y_r, row_s, row_r, idx_s, idx_r, qs, qr, gs, gr, one_s, one_r,
):
    blk, dim = lax.axis_index("blk"), lax.axis_index("dim")
    xy, z = blk // 8, blk % 8
    yh, c = dim // 2, dim % 2
    t = z // 2
    holder = (z % 2) == yh
    me_p = xy * 2 + yh
    me_r = z * 2 + c
    x, yl = xy // 2, xy % 2
    y = yh * 2 + yl

    def plane_dev(p):
        return ((p // 2) * 8 + z, (p % 2) * 2 + c)

    def row_dev(r):
        return (xy * 8 + r // 2, yh * 2 + r % 2)

    def x_dev(xx):
        return ((xx * 2 + yl) * 8 + z, dim)

    def y_dev(yy):
        return ((x * 2 + yy % 2) * 8 + z, (yy // 2) * 2 + c)

    def z_dev(zz):
        return (xy * 8 + zz, dim)

    sibling = (blk, yh * 2 + (1 - c))
    partner = (blk, (1 - yh) * 2 + c)

    def remote(src, dst, send, recv, device):
        return pltpu.make_async_remote_copy(
            src_ref=src, dst_ref=dst, send_sem=send, recv_sem=recv,
            device_id=device, device_id_type=MESH,
        )

    barrier = pltpu.get_barrier_semaphore()

    def greet(k):
        pl.semaphore_signal(barrier, inc=1, device_id=plane_dev((me_p + k + 1) % 16), device_id_type=MESH)
        pl.semaphore_signal(barrier, inc=1, device_id=row_dev((me_r + k + 1) % 16), device_id_type=MESH)

    loop(15, greet)
    idx_mine[0:8] = owner_ref[...]
    idx_mine[8:16] = local_ref[...]
    d_nat[...] = upright(d_ref[...])
    for k, part in enumerate(split3(pool_ref[...])):
        pool_s[k, 0:192] = part
        pool_s[k, 192:256] = jnp.zeros((64, 2048), BF16)
    pl.semaphore_wait(barrier, 30)

    def idx_copy(zz):
        return remote(idx_mine, idx_all.at[t], idx_s.at[zz], idx_r.at[t], z_dev(zz))

    def q_copy(zz):
        return remote(q_all.at[c, t], q_all.at[c, t], qs.at[zz], qr.at[t], z_dev(zz))

    sib_d = remote(
        d_nat.at[pl.ds((1 - c) * 64, 64)], d_sib, one_s.at[SIB_D], one_r.at[SIB_D], sibling
    )
    part_q = remote(q_ref, q_part, one_s.at[PART_Q], one_r.at[PART_Q], partner)

    @pl.when(holder)
    def _():
        loop(7, lambda k: idx_copy((z + k + 1) % 8).start())
        idx_all[t] = idx_mine[...]

    sib_d.start()

    @pl.when(jnp.logical_not(holder))
    def _():
        part_q.start()

    sib_d.wait_recv()
    own_d = d_nat[pl.ds(pl.multiple_of(c * 64, 64), 64), :]
    d_raw[yh, x, yl] = fold(
        jnp.where(c == 0, own_d, d_sib[...]), jnp.where(c == 0, d_sib[...], own_d)
    )

    def doc_x1(xx, slot):
        piece = d_raw.at[yh, slot, yl, pl.ds(0, 32)]
        return remote(piece, piece, x_s.at[DOC_1, xx], x_r.at[DOC_1, slot], x_dev(xx))

    def doc_y1(yy, slot):
        piece = d_raw.at[slot // 2, x, slot % 2, pl.ds(32, 32)]
        return remote(piece, piece, y_s.at[DOC_1, yy], y_r.at[DOC_1, slot], y_dev(yy))

    def doc_y2(yy, slot):
        piece = d_raw.at[slot // 2, :, slot % 2, pl.ds(0, 32)]
        return remote(piece, piece, y_s.at[DOC_2, yy], y_r.at[DOC_2, slot], y_dev(yy))

    def doc_x2(xx, slot):
        piece = d_raw.at[:, slot, :, pl.ds(32, 32)]
        return remote(piece, piece, x_s.at[DOC_2, xx], x_r.at[DOC_2, slot], x_dev(xx))

    def doc_first(k):
        doc_x1((x + k + 1) % 4, x).start()
        doc_y1((y + k + 1) % 4, y).start()

    loop(3, doc_first)

    @pl.when(holder)
    def _():
        remote(q_ref, q_part, one_s.at[PART_Q], one_r.at[PART_Q], partner).wait_recv()
        own, other = upright(q_ref[...]), upright(q_part[...])
        q_all[c, t] = fold(jnp.where(yh == 0, own, other), jnp.where(yh == 0, other, own))
        loop(7, lambda k: q_copy((z + k + 1) % 8).start())

    def idx_wait(tt):
        @pl.when(2 * tt + yh != z)
        def _():
            remote(idx_mine, idx_all.at[tt], idx_s.at[0], idx_r.at[tt], partner).wait_recv()

    loop(4, idx_wait)
    sub8 = lax.broadcasted_iota(jnp.int32, (8, 128), 0)
    upper = jnp.where(
        lax.broadcasted_iota(jnp.int32, (128, 128), 0) < lax.broadcasted_iota(jnp.int32, (128, 128), 1),
        1.0, 0.0,
    ).astype(BF16)
    for tt in range(4):
        owner = idx_all[tt, 0:8]
        local = idx_all[tt, 8:16] + 1
        table = jnp.zeros((8, 128), jnp.int32)
        for a in range(8):
            row = jnp.sum(jnp.where(owner == a * 8 + z, local, 0), axis=0, keepdims=True)
            table = jnp.where(sub8 == a, row, table)
        marks = jnp.where(table > 0, 1.0, 0.0)
        rank = mm(marks.astype(BF16), upper, NN)
        lr_all[:, tt * 128 : (tt + 1) * 128] = table.astype(F32)
        sid[:, tt * 128 : (tt + 1) * 128] = jnp.where(table > 0, rank + float(tt * 32), -1.0)

    sub512 = lax.broadcasted_iota(jnp.int32, (128, 512), 0).astype(F32)
    lane128 = lax.broadcasted_iota(jnp.int32, (128, 128), 1)

    def hot(a):
        return sub512 == sid[pl.ds(a, 1), :]

    def columns(rows):
        def step(a, table):
            col = jnp.sum(jnp.where(hot(a), rows[pl.ds(a, 1), :], 0.0), axis=1, keepdims=True)
            return jnp.where(lane128 == a, col, table)

        return lax.fori_loop(0, 8, step, jnp.zeros((128, 128), F32))

    wanted = columns(lr_all).T
    for a in range(8):
        rq_out[a] = wanted[a : a + 1, :]
    rq_in[me_p] = rq_out[xy]

    def req_copy(p, slot):
        return remote(
            rq_out.at[p // 2], rq_in.at[slot], plane_s.at[REQ, p], plane_r.at[REQ, slot], plane_dev(p)
        )

    loop(15, lambda k: req_copy((me_p + k + 1) % 16, me_p).start())

    def doc_second(k):
        xx, yy = (x + k + 1) % 4, (y + k + 1) % 4
        doc_x1(xx, xx).wait_recv()
        doc_y1(yy, yy).wait_recv()

    loop(3, doc_second)

    def doc_on(k):
        doc_y2((y + k + 1) % 4, y).start()
        doc_x2((x + k + 1) % 4, x).start()

    loop(3, doc_on)

    def req_wait(k):
        p = (me_p + k + 1) % 16
        req_copy(p, p).wait_recv()

    loop(15, req_wait)
    named = jnp.concatenate([rq_in[i] for i in range(16)] + [jnp.zeros((112, 128), F32)], axis=0)
    lt[...] = named.T
    lane2048 = lax.broadcasted_iota(jnp.int32, (128, 2048), 1).astype(F32) + 1.0

    def rows_copy(p, slot):
        return remote(
            p_out.at[p], p_in.at[slot % 2, slot // 2],
            plane_s.at[ROWS, p], plane_r.at[ROWS, slot], plane_dev(p),
        )

    def fetch(g):
        hots = []
        for i in range(4):
            col = jnp.sum(jnp.where(lane128 == g * 4 + i, lt[...], 0.0), axis=1, keepdims=True)
            hots.append(jnp.where(col == lane2048, 1.0, 0.0).astype(BF16))
        hots = jnp.concatenate(hots, axis=0)
        got = mm(hots, pool_s[0], NT) + mm(hots, pool_s[1], NT) + mm(hots, pool_s[2], NT)
        for i in range(4):
            p = g * 4 + i
            p_out[p] = fold(got[i * 128 : i * 128 + 64], got[i * 128 + 64 : i * 128 + 128])

            @pl.when(p != me_p)
            def _():
                rows_copy(p, me_p).start()

    loop(4, fetch)
    p_in[yh, xy] = p_out[me_p]

    def q_wait(tt):
        @pl.when(2 * tt + yh != z)
        def _():
            remote(q_all.at[c, tt], q_all.at[c, tt], qs.at[0], qr.at[tt], partner).wait_recv()

    loop(4, q_wait)
    sib_q = remote(q_all.at[c], q_all.at[c], one_s.at[SIB_Q], one_r.at[SIB_Q], sibling)
    sib_q.start()

    queries = split3(q_all[c].reshape(512, 384))

    def pick(g):
        hots = jnp.concatenate(
            [jnp.where(hot(g * 4 + i), 1.0, 0.0).astype(BF16) for i in range(4)], axis=0
        )
        got = mm(hots, queries[0], NN) + mm(hots, queries[1], NN) + mm(hots, queries[2], NN)
        for i in range(4):
            first, last = regroup(got[i * 128 : i * 128 + 64], got[i * 128 + 64 : i * 128 + 128])
            f_out[(g * 4 + i) * 2] = first
            f_out[(g * 4 + i) * 2 + 1] = last

    loop(2, pick)
    f_in[me_p] = f_out[me_p]

    remote(q_all.at[c], q_all.at[1 - c], one_s.at[SIB_Q], one_r.at[SIB_Q], sibling).wait_recv()

    def rearrange_q(tt):
        first, last = regroup(q_all[0, tt], q_all[1, tt])
        q_re[0, tt] = first
        q_re[1, tt] = last

    loop(4, rearrange_q)

    def doc_wait(k):
        xx, yy = (x + k + 1) % 4, (y + k + 1) % 4
        doc_y2(yy, yy).wait_recv()
        doc_x2(xx, xx).wait_recv()

    loop(3, doc_wait)

    def score(j):
        total = None
        for part in range(2):
            docs = d_raw[part, pl.ds(j * 2, 2)].reshape(256, 384)
            value = mm(docs, q_re[part].reshape(512, 384), NT, HIGHEST)
            total = value if total is None else total + value
        st[pl.ds(pl.multiple_of(j * 256, 256), 256), :] = total * SCALE

    loop(2, score)

    def top(j, best):
        rows = st[pl.ds(pl.multiple_of(j * 64, 64), 64), :].reshape(8, 8, 512)
        return jnp.maximum(best, jnp.max(rows, axis=0))

    best = lax.fori_loop(0, 8, top, jnp.full((8, 512), -jnp.inf, F32))
    best = jnp.max(best, axis=0, keepdims=True)

    def rows_wait(k):
        p = (me_p + k + 1) % 16
        rows_copy(p, p).wait_recv()

    loop(15, rows_wait)
    low64 = low(64)

    def hard_part(a, table):
        terms = p_in[0, a] * f_out[a * 2] + p_in[1, a] * f_out[a * 2 + 1]
        t0, t1, t2 = halves(terms)
        first = jnp.sum(t0 + jnp.where(low64, t1, 0.0), axis=1, keepdims=True)
        last = jnp.sum(t2 + jnp.where(low64, 0.0, t1), axis=1, keepdims=True)
        return jnp.where(lane128 == a, jnp.concatenate([first, last], axis=0), table)

    hs_mine[...] = lax.fori_loop(0, 8, hard_part, jnp.zeros((128, 128), F32))
    sib_h = remote(hs_mine, hs_sib, one_s.at[SIB_H], one_r.at[SIB_H], sibling)
    sib_h.start()

    def query_copy(p, slot):
        return remote(
            f_out.at[p], f_in.at[slot], plane_s.at[QUERY, p], plane_r.at[QUERY, slot], plane_dev(p)
        )

    loop(15, lambda k: query_copy((me_p + k + 1) % 16, me_p).start())

    sib_h.wait_recv()
    hard = (hs_mine[...] + hs_sib[...]) * SCALE
    for a in range(8):
        row = jnp.sum(jnp.where(hot(a), hard[:, a : a + 1], 0.0), axis=0, keepdims=True)
        hq[a : a + 1, :] = jnp.where(sid[a : a + 1, :] >= 0.0, row, -jnp.inf)
    peak = jnp.maximum(best, jnp.max(hq[...], axis=0, keepdims=True))

    def add(j, total):
        rows = jnp.exp(st[pl.ds(pl.multiple_of(j * 64, 64), 64), :] - peak)
        return total + jnp.sum(rows.reshape(8, 8, 512), axis=0)

    total = lax.fori_loop(0, 8, add, jnp.zeros((8, 512), F32))
    total = total + jnp.exp(hq[...] - peak) * jnp.where(c == 0, 1.0, 0.0)
    total = jnp.sum(total, axis=0, keepdims=True)
    square = st[pl.ds(pl.multiple_of(xy * 64, 64), 64), pl.ds(pl.multiple_of(t * 128, 128), 128)]
    on_diagonal = lax.broadcasted_iota(jnp.int32, (64, 128), 1) == (
        lax.broadcasted_iota(jnp.int32, (64, 128), 0) + c * 64
    )
    positive = jnp.sum(jnp.where(on_diagonal, square, 0.0), axis=0, keepdims=True)
    pos_out[...] = positive
    sib_p = remote(pos_out, pos_in, one_s.at[SIB_P], one_r.at[SIB_P], sibling)
    stat_out[:, 0:512] = peak
    stat_out[:, 512:1024] = total
    stat_in[me_r] = stat_out[...]

    def stat_copy(r, slot):
        return remote(stat_out, stat_in.at[slot], row_s.at[r], row_r.at[slot], row_dev(r))

    loop(15, lambda k: stat_copy((me_r + k + 1) % 16, me_r).start())
    sib_p.start()

    def rearrange_d(k):
        first, last = regroup(d_raw[0, k // 2, k % 2], d_raw[1, k // 2, k % 2])
        d_all[0, k] = first
        d_all[1, k] = last
        first, last = regroup(p_in[0, k], p_in[1, k])
        p_all[k, 0:64] = first
        p_all[k, 64:128] = last

    loop(8, rearrange_d)
    filler = jnp.zeros((120, 512), F32)
    sid_t = jnp.concatenate([sid[...], filler], axis=0).T

    def stat_wait(k):
        r = (me_r + k + 1) % 16
        stat_copy(r, r).wait_recv()

    loop(15, stat_wait)
    peaks = jnp.concatenate([stat_in[r, :, 0:512] for r in range(16)], axis=0)
    totals = jnp.concatenate([stat_in[r, :, 512:1024] for r in range(16)], axis=0)
    peak = jnp.max(peaks, axis=0, keepdims=True)
    total = jnp.sum(totals * jnp.exp(peaks - peak), axis=0, keepdims=True)
    log_total = peak + jnp.log(total)
    lrow[...] = log_total

    hq[...] = jnp.exp(hq[...] - log_total)

    def chance(j):
        rows = pl.ds(pl.multiple_of(j * 128, 128), 128)
        value = jnp.exp(st[rows, :] - log_total)
        st[rows, :] = value
        ch[:, rows] = value.T

    loop(4, chance)

    g_sib_out[...] = mm(ch[...], d_all[1 - c].reshape(512, 384), NN, HIGHEST)
    sib_g = remote(g_sib_out, g_sib_in, one_s.at[SIB_G], one_r.at[SIB_G], sibling)
    sib_g.start()
    hc_t = jnp.concatenate([hq[...], filler], axis=0).T
    lane512 = lax.broadcasted_iota(jnp.int32, (512, 128), 1).astype(F32)
    for a in range(8):
        wcat[:, a * 128 : (a + 1) * 128] = jnp.where(
            sid_t[:, a : a + 1] == lane512, hc_t[:, a : a + 1], 0.0
        )
    g_own = mm(ch[...], d_all[c].reshape(512, 384), NN, HIGHEST)
    g_own = g_own + mm(wcat[...], p_all[...].reshape(1024, 384), NN, HIGHEST)
    sib_g.wait_recv()
    g_out[...] = (g_own + g_sib_in[...]).reshape(4, 128, 384)

    def grad_copy(tt, slot):
        return remote(g_out.at[tt], g_in.at[slot], gs.at[tt], gr.at[slot], z_dev(2 * tt + yh))

    def grad_send(tt):
        @pl.when(2 * tt + yh != z)
        def _():
            grad_copy(tt, z).start()

    loop(4, grad_send)

    @pl.when(holder)
    def _():
        g_in[z] = g_out[t]

    def doc_grad(part):
        value = mm(st[...], q_re[part].reshape(512, 384), NN, HIGHEST)
        g3_out[part] = value.reshape(4, 2, 64, 384)

    loop(2, doc_grad)

    def grad_y1(yy, slot):
        return remote(
            g3_out.at[yy // 2, :, yy % 2, pl.ds(0, 32)], c1y.at[slot],
            y_s.at[GRAD_1, yy], y_r.at[GRAD_1, slot], y_dev(yy),
        )

    def grad_x1(xx, slot):
        return remote(
            g3_out.at[:, xx, :, pl.ds(32, 32)], c1x.at[slot],
            x_s.at[GRAD_1, xx], x_r.at[GRAD_1, slot], x_dev(xx),
        )

    def grad_x2(xx, slot):
        return remote(cy.at[xx], c2x.at[slot], x_s.at[GRAD_2, xx], x_r.at[GRAD_2, slot], x_dev(xx))

    def grad_y2(yy, slot):
        return remote(
            cx.at[yy // 2, yy % 2], c2y.at[slot], y_s.at[GRAD_2, yy], y_r.at[GRAD_2, slot], y_dev(yy)
        )

    def grad_first(k):
        grad_y1((y + k + 1) % 4, y).start()
        grad_x1((x + k + 1) % 4, x).start()

    loop(3, grad_first)
    chances = columns(hq).T
    for a in range(8):
        hc_out[a] = chances[a : a + 1, :]
    hc_in[me_p] = hc_out[xy]

    def prob_copy(p, slot):
        return remote(
            hc_out.at[p // 2], hc_in.at[slot], plane_s.at[PROB, p], plane_r.at[PROB, slot], plane_dev(p)
        )

    loop(15, lambda k: prob_copy((me_p + k + 1) % 16, me_p).start())

    def query_wait(k):
        p = (me_p + k + 1) % 16
        query_copy(p, p).wait_recv()
        prob_copy(p, p).wait_recv()

    loop(15, query_wait)
    chances = jnp.concatenate([hc_in[i] for i in range(16)] + [jnp.zeros((112, 128), F32)], axis=0).T

    def turn(i):
        col = jnp.sum(jnp.where(lane128 == i, chances, 0.0), axis=1, keepdims=True)
        rows = jnp.concatenate(unfold(f_in[i]), axis=0) * (col * SCALE)
        terms = split3(rows.T[0:192])
        for k in range(2):
            at_s[k, :, pl.ds(pl.multiple_of(i * 128, 128), 128)] = terms[k]

    loop(16, turn)
    lane256 = lax.broadcasted_iota(jnp.int32, (128, 256), 1).astype(F32) + 1.0

    def pool_grad(n):
        base = (n * 256).astype(F32)
        hots = jnp.concatenate(
            [
                jnp.where(lt[:, i : i + 1] == lane256 + base, 1.0, 0.0).astype(BF16)
                for i in range(16)
            ],
            axis=0,
        )
        value = mm(at_s[0], hots, NN) + mm(at_s[1], hots, NN)
        gp_ref[:, pl.ds(pl.multiple_of(n * 256, 256), 256)] = value

    loop(4, pool_grad)

    def grad_second(k):
        xx, yy = (x + k + 1) % 4, (y + k + 1) % 4
        grad_y1(yy, yy).wait_recv()
        grad_x1(xx, xx).wait_recv()

    loop(3, grad_second)

    def sum_y(xx):
        cy[xx] = (g3_out[yh, xx, yl, 0:32] + c1y[(y + 1) % 4, xx]) + (
            c1y[(y + 2) % 4, xx] + c1y[(y + 3) % 4, xx]
        )

    loop(4, sum_y)

    def sum_x(k):
        a, b = k // 2, k % 2
        cx[a, b] = (g3_out[a, x, b, 32:64] + c1x[(x + 1) % 4, a, b]) + (
            c1x[(x + 2) % 4, a, b] + c1x[(x + 3) % 4, a, b]
        )

    loop(4, sum_x)

    def grad_on(k):
        grad_x2((x + k + 1) % 4, x).start()
        grad_y2((y + k + 1) % 4, y).start()

    loop(3, grad_on)
    loop(4, lambda n: pool_grad(n + 4))

    part_dq = remote(dq_out, dq_in, one_s.at[PART_DQ], one_r.at[PART_DQ], partner)
    part_l = remote(loss_out, loss_in, one_s.at[PART_L], one_r.at[PART_L], partner)
    sib_p.wait_recv()

    @pl.when(holder)
    def _():
        loss_out[...] = lrow[:, pl.ds(pl.multiple_of(t * 128, 128), 128)] - (pos_out[...] + pos_in[...])
        part_l.start()

        def wait(k):
            zz = (z + k + 1) % 8
            grad_copy(t, zz).wait_recv()

        loop(7, wait)
        value = g_in[0]
        for zz in range(1, 8):
            value = value + g_in[zz]
        first, last = unfold(value)
        dq_out[...] = jnp.where(yh == 0, last, first).T[0:192]
        part_dq.start()
        dq_ref[...] = (jnp.where(yh == 0, first, last).T[0:192] - d_ref[...]) * SCALE
        loss_ref[...] = loss_out[...]

    def grad_wait(k):
        xx, yy = (x + k + 1) % 4, (y + k + 1) % 4
        grad_x2(xx, xx).wait_recv()
        grad_y2(yy, yy).wait_recv()

    loop(3, grad_wait)
    upper_rows = (cy[x] + c2x[(x + 1) % 4]) + (c2x[(x + 2) % 4] + c2x[(x + 3) % 4])
    lower_rows = (cx[yh, yl] + c2y[(y + 1) % 4]) + (c2y[(y + 2) % 4] + c2y[(y + 3) % 4])
    value = jnp.concatenate([upper_rows, lower_rows], axis=0)
    first, last = unfold(value)
    dd_out[...] = jnp.where(c == 0, last, first)
    sib_dd = remote(dd_out, dd_sib, one_s.at[SIB_DD], one_r.at[SIB_DD], sibling)
    sib_dd.start()
    dd_nat[pl.ds(pl.multiple_of(c * 64, 64), 64), :] = jnp.where(c == 0, first, last)

    @pl.when(jnp.logical_not(holder))
    def _():
        part_l.wait_recv()
        loss_ref[...] = loss_in[...]
        part_dq.wait_recv()
        dq_ref[...] = (dq_in[...] - d_ref[...]) * SCALE

    sib_dd.wait_recv()
    dd_nat[pl.ds(pl.multiple_of((1 - c) * 64, 64), 64), :] = dd_sib[...]
    dd_ref[...] = (dd_nat[...].T[0:192] - q_ref[...]) * SCALE

    sib_d.wait_send()
    sib_q.wait_send()
    sib_h.wait_send()
    sib_g.wait_send()
    sib_dd.wait_send()

    def sent(k):
        p = (me_p + k + 1) % 16
        for copy in (req_copy, rows_copy, query_copy, prob_copy):
            copy(p, me_p).wait_send()
        stat_copy((me_r + k + 1) % 16, me_r).wait_send()

    loop(15, sent)

    def sent4(k):
        for copy in (doc_x1, doc_x2, grad_x1, grad_x2):
            copy((x + k + 1) % 4, x).wait_send()
        for copy in (doc_y1, doc_y2, grad_y1, grad_y2):
            copy((y + k + 1) % 4, y).wait_send()

    loop(3, sent4)
    sib_p.wait_send()

    def grad_sent(tt):
        @pl.when(2 * tt + yh != z)
        def _():
            grad_copy(tt, z).wait_send()

    loop(4, grad_sent)

    @pl.when(holder)
    def _():
        def z_sent(k):
            zz = (z + k + 1) % 8
            idx_copy(zz).wait_send()
            q_copy(zz).wait_send()

        loop(7, z_sent)
        part_l.wait_send()
        part_dq.wait_send()

    @pl.when(jnp.logical_not(holder))
    def _():
        part_q.wait_send()


def hand_on(*refs):
    for source, target in zip(refs[:4], refs[4:]):
        target[...] = source[...]


def per_device(question_matrix, document_matrix, pool, hard_owner, hard_local):
    vmem = pl.BlockSpec(memory_space=pltpu.VMEM)
    f = lambda *shape: pltpu.VMEM(shape, F32)
    scratch = [
        pltpu.VMEM((16, 128), jnp.int32),
        pltpu.VMEM((4, 16, 128), jnp.int32),
        f(192, 128),
        f(2, 4, 128, 384),
        f(2, 4, 128, 384),
        f(128, 256),
        f(64, 256),
        f(2, 4, 2, 64, 384),
        f(2, 8, 64, 384),
        f(8, 512),
        f(8, 512),
        f(8, 1, 128),
        f(16, 1, 128),
        f(128, 128),
        pltpu.VMEM((3, 256, 2048), BF16),
        f(16, 64, 384),
        f(2, 8, 64, 384),
        f(8, 128, 384),
        f(16, 64, 384),
        f(16, 64, 384),
        f(128, 128),
        f(128, 128),
        f(8, 512),
        f(512, 512),
        f(512, 512),
        f(1, 1024),
        f(16, 1, 1024),
        f(8, 1, 128),
        f(16, 1, 128),
        f(2, 4, 2, 64, 384),
        f(4, 2, 2, 32, 384),
        f(4, 4, 32, 384),
        f(2, 2, 32, 384),
        f(4, 32, 384),
        f(4, 32, 384),
        f(4, 32, 384),
        f(64, 256),
        f(64, 256),
        f(128, 256),
        f(512, 384),
        f(512, 384),
        f(4, 128, 384),
        f(8, 128, 384),
        f(512, 1024),
        pltpu.VMEM((2, 192, 2048), BF16),
        f(192, 128),
        f(192, 128),
        f(1, 128),
        f(1, 128),
        f(1, 128),
        f(1, 128),
        f(1, 512),
        pltpu.SemaphoreType.DMA((4, 16)),
        pltpu.SemaphoreType.DMA((4, 16)),
        pltpu.SemaphoreType.DMA((4, 4)),
        pltpu.SemaphoreType.DMA((4, 4)),
        pltpu.SemaphoreType.DMA((4, 4)),
        pltpu.SemaphoreType.DMA((4, 4)),
        pltpu.SemaphoreType.DMA((16,)),
        pltpu.SemaphoreType.DMA((16,)),
        pltpu.SemaphoreType.DMA((8,)),
        pltpu.SemaphoreType.DMA((4,)),
        pltpu.SemaphoreType.DMA((8,)),
        pltpu.SemaphoreType.DMA((4,)),
        pltpu.SemaphoreType.DMA((4,)),
        pltpu.SemaphoreType.DMA((8,)),
        pltpu.SemaphoreType.DMA((9,)),
        pltpu.SemaphoreType.DMA((9,)),
    ]
    results = pl.pallas_call(
        kernel,
        name="retriever_step",
        out_shape=(
            jax.ShapeDtypeStruct((1, 128), F32),
            jax.ShapeDtypeStruct((192, 128), F32),
            jax.ShapeDtypeStruct((192, 128), F32),
            jax.ShapeDtypeStruct((192, 2048), F32),
        ),
        in_specs=[vmem] * 5,
        out_specs=(vmem,) * 4,
        scratch_shapes=scratch,
        compiler_params=pltpu.CompilerParams(
            collective_id=0, has_side_effects=True, vmem_limit_bytes=60 * 1024 * 1024
        ),
    )(question_matrix.T, document_matrix.T, pool, hard_owner.T, hard_local.T)
    loss, dq, dd, gp = pl.pallas_call(
        hand_on,
        name="results",
        out_shape=tuple(jax.ShapeDtypeStruct(r.shape, r.dtype) for r in results),
        in_specs=[vmem] * 4,
        out_specs=(vmem,) * 4,
    )(*results)
    return loss.reshape(128), dq.T, dd.T, gp


def solution(mesh):
    placed = (P("blk", "dim"), P("blk", "dim"), P("dim", "blk"), P("blk", None), P("blk", None))
    return jax.shard_map(
        per_device,
        mesh=mesh,
        in_specs=placed,
        out_specs=(P("blk"), P("blk", "dim"), P("blk", "dim"), P("dim", "blk")),
        check_vma=False,
    )
```

```python
import jax
import jax.numpy as jnp
from jax import lax
from jax.experimental import pallas as pl
from jax.experimental.pallas import tpu as pltpu
from jax.sharding import PartitionSpec as P

MESH = pl.DeviceIdType.MESH
F32 = jnp.float32
BF16 = jnp.bfloat16
HIGHEST = lax.Precision.HIGHEST
SCALE = 20.0

NT = (((1,), (1,)), ((), ()))
NN = (((1,), (0,)), ((), ()))


def mm(a, b, dims, precision=None):
    return lax.dot_general(a, b, dims, precision=precision, preferred_element_type=F32)


def split3(x):
    high = x.astype(BF16)
    rest = x - high.astype(F32)
    mid = rest.astype(BF16)
    low = (rest - mid.astype(F32)).astype(BF16)
    return high, mid, low


def loop(count, body):
    def step(i, carry):
        body(i)
        return carry

    lax.fori_loop(0, count, step, 0)


def halves(x):
    return x[:, :128], x[:, 128:256], x[:, 256:384]


def low(rows):
    return lax.broadcasted_iota(jnp.int32, (rows, 128), 1) < 64


def turned(x):
    return pltpu.roll(x, 64, 1)


def fold(a, b):
    keep = low(a.shape[0])
    b0, b1 = turned(b[:, :128]), turned(b[:, 128:256])
    return jnp.concatenate(
        [a[:, :128], jnp.where(keep, a[:, 128:256], b0), jnp.where(keep, b0, b1)], axis=1
    )


def unfold(x):
    x0, x1, x2 = halves(x)
    x1t, x2t = turned(x1), turned(x2)
    return (
        jnp.concatenate([x0, x1], axis=1),
        jnp.concatenate([jnp.where(low(x.shape[0]), x1t, x2t), x2t], axis=1),
    )


def regroup(x, y):
    x0, x1, x2 = halves(x)
    y0, y1, y2 = halves(y)
    keep = low(x.shape[0])
    x1t, x2t, y0t, y1t = turned(x1), turned(x2), turned(y0), turned(y1)
    first = jnp.concatenate([x0, jnp.where(keep, x1, y0t), jnp.where(keep, y0t, y1t)], axis=1)
    last = jnp.concatenate([jnp.where(keep, x1t, x2t), jnp.where(keep, x2t, y1), y2], axis=1)
    return first, last


def upright(x):
    return jnp.concatenate([x, jnp.zeros((64, 128), F32)], axis=0).T


REQ, ROWS, QUERY, PROB = range(4)
SIB_D, SIB_Q, SIB_H, _, SIB_DD, SIB_P, PART_Q, PART_DQ, PART_L = range(9)
DOC_1, DOC_2, GRAD_1, GRAD_2 = range(4)


def kernel(
    q_ref, d_ref, pool_ref, owner_ref, local_ref,
    loss_ref, dq_ref, dd_ref, gp_ref,
    idx_mine, idx_all, q_part, q_all, q_re, d_nat, d_sib, d_raw, d_all, lr_all, sid,
    rq_out, rq_in, lt, pool_s,
    p_out, p_in, p_all, f_out, f_in, hs_mine, hs_sib, hq, st, ch, stat_out, stat_in,
    hc_out, hc_in, g3_out, c1x, c1y, cx, cy, c2x, c2y, dd_out, dd_sib, dd_nat, g_sib_out, g_sib_in, g_out, g_in, hots_t, hp, at_s,
    dq_out, dq_in, loss_out, loss_in, pos_out, pos_in, lrow,
    plane_s, plane_r, x_s, x_r, y_s, y_r, row_s, row_r, idx_s, idx_r, qs, qr, gs, gr, sg_s, sg_r, one_s, one_r,
):
    blk, dim = lax.axis_index("blk"), lax.axis_index("dim")
    xy, z = blk // 8, blk % 8
    yh, c = dim // 2, dim % 2
    t = z // 2
    holder = (z % 2) == yh
    me_p = xy * 2 + yh
    me_r = z * 2 + c
    x, yl = xy // 2, xy % 2
    y = yh * 2 + yl

    def plane_dev(p):
        return ((p // 2) * 8 + z, (p % 2) * 2 + c)

    def row_dev(r):
        return (xy * 8 + r // 2, yh * 2 + r % 2)

    def x_dev(xx):
        return ((xx * 2 + yl) * 8 + z, dim)

    def y_dev(yy):
        return ((x * 2 + yy % 2) * 8 + z, (yy // 2) * 2 + c)

    def z_dev(zz):
        return (xy * 8 + zz, dim)

    sibling = (blk, yh * 2 + (1 - c))
    partner = (blk, (1 - yh) * 2 + c)

    def remote(src, dst, send, recv, device):
        return pltpu.make_async_remote_copy(
            src_ref=src, dst_ref=dst, send_sem=send, recv_sem=recv,
            device_id=device, device_id_type=MESH,
        )

    barrier = pltpu.get_barrier_semaphore()

    def greet(k):
        pl.semaphore_signal(barrier, inc=1, device_id=plane_dev((me_p + k + 1) % 16), device_id_type=MESH)
        pl.semaphore_signal(barrier, inc=1, device_id=row_dev((me_r + k + 1) % 16), device_id_type=MESH)

    loop(15, greet)
    idx_mine[0:8] = owner_ref[...]
    idx_mine[8:16] = local_ref[...]
    d_nat[...] = upright(d_ref[...])
    for k, part in enumerate(split3(pool_ref[...])):
        pool_s[k, 0:192] = part
        pool_s[k, 192:256] = jnp.zeros((64, 2048), BF16)
    pl.semaphore_wait(barrier, 30)

    def idx_copy(zz):
        return remote(idx_mine, idx_all.at[t], idx_s.at[zz], idx_r.at[t], z_dev(zz))

    def q_copy(zz):
        return remote(q_all.at[c, t], q_all.at[c, t], qs.at[zz], qr.at[t], z_dev(zz))

    sib_d = remote(
        d_nat.at[pl.ds((1 - c) * 64, 64)], d_sib, one_s.at[SIB_D], one_r.at[SIB_D], sibling
    )
    part_q = remote(q_ref, q_part, one_s.at[PART_Q], one_r.at[PART_Q], partner)

    @pl.when(holder)
    def _():
        loop(7, lambda k: idx_copy((z + k + 1) % 8).start())
        idx_all[t] = idx_mine[...]

    sib_d.start()

    @pl.when(jnp.logical_not(holder))
    def _():
        part_q.start()

    sib_d.wait_recv()
    own_d = d_nat[pl.ds(pl.multiple_of(c * 64, 64), 64), :]
    d_raw[yh, x, yl] = fold(
        jnp.where(c == 0, own_d, d_sib[...]), jnp.where(c == 0, d_sib[...], own_d)
    )

    def doc_x1(xx, slot):
        piece = d_raw.at[yh, slot, yl, pl.ds(0, 32)]
        return remote(piece, piece, x_s.at[DOC_1, xx], x_r.at[DOC_1, slot], x_dev(xx))

    def doc_y1(yy, slot):
        piece = d_raw.at[slot // 2, x, slot % 2, pl.ds(32, 32)]
        return remote(piece, piece, y_s.at[DOC_1, yy], y_r.at[DOC_1, slot], y_dev(yy))

    def doc_y2(yy, slot):
        piece = d_raw.at[slot // 2, :, slot % 2, pl.ds(0, 32)]
        return remote(piece, piece, y_s.at[DOC_2, yy], y_r.at[DOC_2, slot], y_dev(yy))

    def doc_x2(xx, slot):
        piece = d_raw.at[:, slot, :, pl.ds(32, 32)]
        return remote(piece, piece, x_s.at[DOC_2, xx], x_r.at[DOC_2, slot], x_dev(xx))

    def doc_first(k):
        doc_x1((x + k + 1) % 4, x).start()
        doc_y1((y + k + 1) % 4, y).start()

    loop(3, doc_first)

    def idx_wait(tt):
        @pl.when(2 * tt + yh != z)
        def _():
            remote(idx_mine, idx_all.at[tt], idx_s.at[0], idx_r.at[tt], partner).wait_recv()

    loop(4, idx_wait)
    sub8 = lax.broadcasted_iota(jnp.int32, (8, 128), 0)
    upper = jnp.where(
        lax.broadcasted_iota(jnp.int32, (128, 128), 0) < lax.broadcasted_iota(jnp.int32, (128, 128), 1),
        1.0, 0.0,
    ).astype(BF16)
    for tt in range(4):
        owner = idx_all[tt, 0:8]
        local = idx_all[tt, 8:16] + 1
        table = jnp.zeros((8, 128), jnp.int32)
        for a in range(8):
            row = jnp.sum(jnp.where(owner == a * 8 + z, local, 0), axis=0, keepdims=True)
            table = jnp.where(sub8 == a, row, table)
        marks = jnp.where(table > 0, 1.0, 0.0)
        rank = mm(marks.astype(BF16), upper, NN)
        lr_all[:, tt * 128 : (tt + 1) * 128] = table.astype(F32)
        sid[:, tt * 128 : (tt + 1) * 128] = jnp.where(table > 0, rank + float(tt * 32), -1.0)

    sub512 = lax.broadcasted_iota(jnp.int32, (128, 512), 0).astype(F32)
    lane128 = lax.broadcasted_iota(jnp.int32, (128, 128), 1)

    def hot(a):
        return sub512 == sid[pl.ds(a, 1), :]

    def columns(rows):
        def step(a, table):
            col = jnp.sum(jnp.where(hot(a), rows[pl.ds(a, 1), :], 0.0), axis=1, keepdims=True)
            return jnp.where(lane128 == a, col, table)

        return lax.fori_loop(0, 8, step, jnp.zeros((128, 128), F32))

    wanted = columns(lr_all).T
    for a in range(8):
        rq_out[a] = wanted[a : a + 1, :]
    rq_in[me_p] = rq_out[xy]

    def req_copy(p, slot):
        return remote(
            rq_out.at[p // 2], rq_in.at[slot], plane_s.at[REQ, p], plane_r.at[REQ, slot], plane_dev(p)
        )

    loop(15, lambda k: req_copy((me_p + k + 1) % 16, me_p).start())

    @pl.when(holder)
    def _():
        remote(q_ref, q_part, one_s.at[PART_Q], one_r.at[PART_Q], partner).wait_recv()
        own, other = upright(q_ref[...]), upright(q_part[...])
        q_all[c, t] = fold(jnp.where(yh == 0, own, other), jnp.where(yh == 0, other, own))
        loop(7, lambda k: q_copy((z + k + 1) % 8).start())

    def doc_second(k):
        xx, yy = (x + k + 1) % 4, (y + k + 1) % 4
        doc_x1(xx, xx).wait_recv()
        doc_y1(yy, yy).wait_recv()

    loop(3, doc_second)

    def doc_on(k):
        doc_y2((y + k + 1) % 4, y).start()
        doc_x2((x + k + 1) % 4, x).start()

    loop(3, doc_on)

    def req_wait(k):
        p = (me_p + k + 1) % 16
        req_copy(p, p).wait_recv()

    loop(15, req_wait)
    named = jnp.concatenate([rq_in[i] for i in range(16)] + [jnp.zeros((112, 128), F32)], axis=0)
    lt[...] = named.T
    lane2048 = lax.broadcasted_iota(jnp.int32, (128, 2048), 1).astype(F32) + 1.0

    def rows_copy(p, slot):
        return remote(
            p_out.at[p], p_in.at[slot % 2, slot // 2],
            plane_s.at[ROWS, p], plane_r.at[ROWS, slot], plane_dev(p),
        )

    def fetch(g):
        hots = []
        for i in range(4):
            col = jnp.sum(jnp.where(lane128 == g * 4 + i, lt[...], 0.0), axis=1, keepdims=True)
            hots.append(jnp.where(col == lane2048, 1.0, 0.0).astype(BF16))
        hots = jnp.concatenate(hots, axis=0)
        got = mm(hots, pool_s[0], NT) + mm(hots, pool_s[1], NT) + mm(hots, pool_s[2], NT)
        for i in range(4):
            p = g * 4 + i
            p_out[p] = fold(got[i * 128 : i * 128 + 64], got[i * 128 + 64 : i * 128 + 128])

            @pl.when(p != me_p)
            def _():
                rows_copy(p, me_p).start()

    loop(4, fetch)
    p_in[yh, xy] = p_out[me_p]

    def q_wait(tt):
        @pl.when(2 * tt + yh != z)
        def _():
            remote(q_all.at[c, tt], q_all.at[c, tt], qs.at[0], qr.at[tt], partner).wait_recv()

    loop(4, q_wait)
    sib_q = remote(q_all.at[c], q_all.at[c], one_s.at[SIB_Q], one_r.at[SIB_Q], sibling)
    sib_q.start()

    queries = split3(q_all[c].reshape(512, 384))

    def pick(g):
        hots = jnp.concatenate(
            [jnp.where(hot(g * 4 + i), 1.0, 0.0).astype(BF16) for i in range(4)], axis=0
        )
        got = mm(hots, queries[0], NN) + mm(hots, queries[1], NN) + mm(hots, queries[2], NN)
        for i in range(4):
            first, last = regroup(got[i * 128 : i * 128 + 64], got[i * 128 + 64 : i * 128 + 128])
            f_out[(g * 4 + i) * 2] = first
            f_out[(g * 4 + i) * 2 + 1] = last

    loop(2, pick)
    f_in[me_p] = f_out[me_p]

    remote(q_all.at[c], q_all.at[1 - c], one_s.at[SIB_Q], one_r.at[SIB_Q], sibling).wait_recv()

    def rearrange_q(tt):
        first, last = regroup(q_all[0, tt], q_all[1, tt])
        q_re[0, tt] = first
        q_re[1, tt] = last

    loop(4, rearrange_q)

    def doc_wait(k):
        xx, yy = (x + k + 1) % 4, (y + k + 1) % 4
        doc_y2(yy, yy).wait_recv()
        doc_x2(xx, xx).wait_recv()

    loop(3, doc_wait)

    def score(j):
        total = None
        for part in range(2):
            docs = d_raw[part, pl.ds(j * 2, 2)].reshape(256, 384)
            value = mm(docs, q_re[part].reshape(512, 384), NT, HIGHEST)
            total = value if total is None else total + value
        st[pl.ds(pl.multiple_of(j * 256, 256), 256), :] = total * SCALE

    loop(2, score)

    def top(j, best):
        rows = st[pl.ds(pl.multiple_of(j * 64, 64), 64), :].reshape(8, 8, 512)
        return jnp.maximum(best, jnp.max(rows, axis=0))

    best = lax.fori_loop(0, 8, top, jnp.full((8, 512), -jnp.inf, F32))
    best = jnp.max(best, axis=0, keepdims=True)

    def rows_wait(k):
        p = (me_p + k + 1) % 16
        rows_copy(p, p).wait_recv()

    loop(15, rows_wait)
    low64 = low(64)

    def hard_part(a, table):
        terms = p_in[0, a] * f_out[a * 2] + p_in[1, a] * f_out[a * 2 + 1]
        t0, t1, t2 = halves(terms)
        first = jnp.sum(t0 + jnp.where(low64, t1, 0.0), axis=1, keepdims=True)
        last = jnp.sum(t2 + jnp.where(low64, 0.0, t1), axis=1, keepdims=True)
        return jnp.where(lane128 == a, jnp.concatenate([first, last], axis=0), table)

    hs_mine[...] = lax.fori_loop(0, 8, hard_part, jnp.zeros((128, 128), F32))
    sib_h = remote(hs_mine, hs_sib, one_s.at[SIB_H], one_r.at[SIB_H], sibling)
    sib_h.start()

    def query_copy(p, slot):
        return remote(
            f_out.at[p], f_in.at[slot], plane_s.at[QUERY, p], plane_r.at[QUERY, slot], plane_dev(p)
        )

    loop(15, lambda k: query_copy((me_p + k + 1) % 16, me_p).start())

    sib_h.wait_recv()
    hard = (hs_mine[...] + hs_sib[...]) * SCALE
    for a in range(8):
        row = jnp.sum(jnp.where(hot(a), hard[:, a : a + 1], 0.0), axis=0, keepdims=True)
        hq[a : a + 1, :] = jnp.where(sid[a : a + 1, :] >= 0.0, row, -jnp.inf)
    peak = jnp.maximum(best, jnp.max(hq[...], axis=0, keepdims=True))

    def add(j, total):
        rows = jnp.exp(st[pl.ds(pl.multiple_of(j * 64, 64), 64), :] - peak)
        return total + jnp.sum(rows.reshape(8, 8, 512), axis=0)

    total = lax.fori_loop(0, 8, add, jnp.zeros((8, 512), F32))
    total = total + jnp.exp(hq[...] - peak) * jnp.where(c == 0, 1.0, 0.0)
    total = jnp.sum(total, axis=0, keepdims=True)
    square = st[pl.ds(pl.multiple_of(xy * 64, 64), 64), pl.ds(pl.multiple_of(t * 128, 128), 128)]
    on_diagonal = lax.broadcasted_iota(jnp.int32, (64, 128), 1) == (
        lax.broadcasted_iota(jnp.int32, (64, 128), 0) + c * 64
    )
    positive = jnp.sum(jnp.where(on_diagonal, square, 0.0), axis=0, keepdims=True)
    pos_out[...] = positive
    sib_p = remote(pos_out, pos_in, one_s.at[SIB_P], one_r.at[SIB_P], sibling)
    stat_out[:, 0:512] = peak
    stat_out[:, 512:1024] = total
    stat_in[me_r] = stat_out[...]

    def stat_copy(r, slot):
        return remote(stat_out, stat_in.at[slot], row_s.at[r], row_r.at[slot], row_dev(r))

    loop(15, lambda k: stat_copy((me_r + k + 1) % 16, me_r).start())
    sib_p.start()

    def rearrange_d(k):
        first, last = regroup(d_raw[0, k // 2, k % 2], d_raw[1, k // 2, k % 2])
        d_all[0, k] = first
        d_all[1, k] = last
        first, last = regroup(p_in[0, k], p_in[1, k])
        p_all[k, 0:64] = first
        p_all[k, 64:128] = last

    loop(8, rearrange_d)
    sid_t = jnp.concatenate([sid[...], jnp.zeros((120, 512), F32)], axis=0).T
    lane512 = lax.broadcasted_iota(jnp.int32, (512, 128), 1).astype(F32)
    for a in range(8):
        hots_t[:, a * 128 : (a + 1) * 128] = jnp.where(
            sid_t[:, a : a + 1] == lane512, 1.0, 0.0
        ).astype(BF16)

    def stat_wait(k):
        r = (me_r + k + 1) % 16
        stat_copy(r, r).wait_recv()

    loop(15, stat_wait)
    peaks = jnp.concatenate([stat_in[r, :, 0:512] for r in range(16)], axis=0)
    totals = jnp.concatenate([stat_in[r, :, 512:1024] for r in range(16)], axis=0)
    peak = jnp.max(peaks, axis=0, keepdims=True)
    total = jnp.sum(totals * jnp.exp(peaks - peak), axis=0, keepdims=True)
    log_total = peak + jnp.log(total)
    lrow[...] = log_total

    hq[...] = jnp.exp(hq[...] - log_total)

    shares = columns(hq)
    chances = shares.T
    for a in range(8):
        hc_out[a] = chances[a : a + 1, :]
    hc_in[me_p] = hc_out[xy]

    def prob_copy(p, slot):
        return remote(
            hc_out.at[p // 2], hc_in.at[slot], plane_s.at[PROB, p], plane_r.at[PROB, slot], plane_dev(p)
        )

    loop(15, lambda k: prob_copy((me_p + k + 1) % 16, me_p).start())

    for a in range(8):
        for k, part in enumerate(split3(p_all[a] * shares[:, a : a + 1])):
            hp[k, a] = part

    def chance(j):
        rows = pl.ds(pl.multiple_of(j * 128, 128), 128)
        value = jnp.exp(st[rows, :] - log_total)
        st[rows, :] = value
        ch[:, rows] = value.T

    loop(4, chance)

    def sib_g(h):
        return remote(g_sib_out.at[h], g_sib_in.at[h], sg_s.at[h], sg_r.at[h], sibling)

    def grad_copy(tt, slot):
        return remote(g_out.at[tt], g_in.at[slot], gs.at[tt], gr.at[slot], z_dev(2 * tt + yh))

    def grad_half(h):
        rows = pl.ds(pl.multiple_of(h * 256, 256), 256)
        g_sib_out[h] = mm(ch[rows, :], d_all[1 - c].reshape(512, 384), NN, HIGHEST)
        sib_g(h).start()
        g_own = mm(ch[rows, :], d_all[c].reshape(512, 384), NN, HIGHEST)
        for k in range(3):
            g_own = g_own + mm(hots_t[rows, :], hp[k].reshape(1024, 384), NN)
        sib_g(h).wait_recv()
        g_out[pl.ds(h * 2, 2)] = (g_own + g_sib_in[h]).reshape(2, 128, 384)
        for i in range(2):
            tt = h * 2 + i

            @pl.when(2 * tt + yh != z)
            def _():
                grad_copy(tt, z).start()

    loop(2, grad_half)

    @pl.when(holder)
    def _():
        g_in[z] = g_out[t]

    def doc_grad(part):
        value = mm(st[...], q_re[part].reshape(512, 384), NN, HIGHEST)
        g3_out[part] = value.reshape(4, 2, 64, 384)

    loop(2, doc_grad)

    def grad_y1(yy, slot):
        return remote(
            g3_out.at[yy // 2, :, yy % 2, pl.ds(0, 32)], c1y.at[slot],
            y_s.at[GRAD_1, yy], y_r.at[GRAD_1, slot], y_dev(yy),
        )

    def grad_x1(xx, slot):
        return remote(
            g3_out.at[:, xx, :, pl.ds(32, 32)], c1x.at[slot],
            x_s.at[GRAD_1, xx], x_r.at[GRAD_1, slot], x_dev(xx),
        )

    def grad_x2(xx, slot):
        return remote(cy.at[xx], c2x.at[slot], x_s.at[GRAD_2, xx], x_r.at[GRAD_2, slot], x_dev(xx))

    def grad_y2(yy, slot):
        return remote(
            cx.at[yy // 2, yy % 2], c2y.at[slot], y_s.at[GRAD_2, yy], y_r.at[GRAD_2, slot], y_dev(yy)
        )

    def grad_first(k):
        grad_y1((y + k + 1) % 4, y).start()
        grad_x1((x + k + 1) % 4, x).start()

    loop(3, grad_first)
    def query_wait(k):
        p = (me_p + k + 1) % 16
        query_copy(p, p).wait_recv()
        prob_copy(p, p).wait_recv()

    loop(15, query_wait)
    chances = jnp.concatenate([hc_in[i] for i in range(16)] + [jnp.zeros((112, 128), F32)], axis=0).T

    def turn(i):
        col = jnp.sum(jnp.where(lane128 == i, chances, 0.0), axis=1, keepdims=True)
        rows = jnp.concatenate(unfold(f_in[i]), axis=0) * (col * SCALE)
        terms = split3(rows.T[0:192])
        for k in range(2):
            at_s[k, :, pl.ds(pl.multiple_of(i * 128, 128), 128)] = terms[k]

    loop(16, turn)
    lane256 = lax.broadcasted_iota(jnp.int32, (128, 256), 1).astype(F32) + 1.0

    def pool_grad(n):
        base = (n * 256).astype(F32)
        hots = jnp.concatenate(
            [
                jnp.where(lt[:, i : i + 1] == lane256 + base, 1.0, 0.0).astype(BF16)
                for i in range(16)
            ],
            axis=0,
        )
        value = mm(at_s[0], hots, NN) + mm(at_s[1], hots, NN)
        gp_ref[:, pl.ds(pl.multiple_of(n * 256, 256), 256)] = value

    loop(4, pool_grad)

    def grad_second(k):
        xx, yy = (x + k + 1) % 4, (y + k + 1) % 4
        grad_y1(yy, yy).wait_recv()
        grad_x1(xx, xx).wait_recv()

    loop(3, grad_second)

    def sum_y(xx):
        cy[xx] = (g3_out[yh, xx, yl, 0:32] + c1y[(y + 1) % 4, xx]) + (
            c1y[(y + 2) % 4, xx] + c1y[(y + 3) % 4, xx]
        )

    loop(4, sum_y)

    def sum_x(k):
        a, b = k // 2, k % 2
        cx[a, b] = (g3_out[a, x, b, 32:64] + c1x[(x + 1) % 4, a, b]) + (
            c1x[(x + 2) % 4, a, b] + c1x[(x + 3) % 4, a, b]
        )

    loop(4, sum_x)

    def grad_on(k):
        grad_x2((x + k + 1) % 4, x).start()
        grad_y2((y + k + 1) % 4, y).start()

    loop(3, grad_on)
    loop(4, lambda n: pool_grad(n + 4))

    def grad_wait(k):
        xx, yy = (x + k + 1) % 4, (y + k + 1) % 4
        grad_x2(xx, xx).wait_recv()
        grad_y2(yy, yy).wait_recv()

    loop(3, grad_wait)
    upper_rows = (cy[x] + c2x[(x + 1) % 4]) + (c2x[(x + 2) % 4] + c2x[(x + 3) % 4])
    lower_rows = (cx[yh, yl] + c2y[(y + 1) % 4]) + (c2y[(y + 2) % 4] + c2y[(y + 3) % 4])
    value = jnp.concatenate([upper_rows, lower_rows], axis=0)
    first, last = unfold(value)
    dd_out[...] = jnp.where(c == 0, last, first)
    sib_dd = remote(dd_out, dd_sib, one_s.at[SIB_DD], one_r.at[SIB_DD], sibling)
    sib_dd.start()
    dd_nat[pl.ds(pl.multiple_of(c * 64, 64), 64), :] = jnp.where(c == 0, first, last)

    sib_d.wait_send()
    sib_q.wait_send()
    sib_h.wait_send()
    loop(2, lambda h: sib_g(h).wait_send())

    def sent(k):
        p = (me_p + k + 1) % 16
        for copy in (req_copy, rows_copy, query_copy, prob_copy):
            copy(p, me_p).wait_send()
        stat_copy((me_r + k + 1) % 16, me_r).wait_send()

    loop(15, sent)

    def sent4(k):
        for copy in (doc_x1, doc_x2, grad_x1, grad_x2):
            copy((x + k + 1) % 4, x).wait_send()
        for copy in (doc_y1, doc_y2, grad_y1, grad_y2):
            copy((y + k + 1) % 4, y).wait_send()

    loop(3, sent4)
    sib_p.wait_send()

    def grad_sent(tt):
        @pl.when(2 * tt + yh != z)
        def _():
            grad_copy(tt, z).wait_send()

    loop(4, grad_sent)

    @pl.when(holder)
    def _():
        def z_sent(k):
            zz = (z + k + 1) % 8
            idx_copy(zz).wait_send()
            q_copy(zz).wait_send()

        loop(7, z_sent)

    @pl.when(jnp.logical_not(holder))
    def _():
        part_q.wait_send()

    part_dq = remote(dq_out, dq_in, one_s.at[PART_DQ], one_r.at[PART_DQ], partner)
    part_l = remote(loss_out, loss_in, one_s.at[PART_L], one_r.at[PART_L], partner)
    sib_p.wait_recv()

    @pl.when(holder)
    def _():
        loss_out[...] = lrow[:, pl.ds(pl.multiple_of(t * 128, 128), 128)] - (pos_out[...] + pos_in[...])
        part_l.start()

        def wait(k):
            zz = (z + k + 1) % 8
            grad_copy(t, zz).wait_recv()

        loop(7, wait)
        value = g_in[0]
        for zz in range(1, 8):
            value = value + g_in[zz]
        first, last = unfold(value)
        dq_out[...] = jnp.where(yh == 0, last, first).T[0:192]
        part_dq.start()
        dq_ref[...] = (jnp.where(yh == 0, first, last).T[0:192] - d_ref[...]) * SCALE
        loss_ref[...] = loss_out[...]

    sib_dd.wait_recv()
    dd_nat[pl.ds(pl.multiple_of((1 - c) * 64, 64), 64), :] = dd_sib[...]
    dd_ref[...] = (dd_nat[...].T[0:192] - q_ref[...]) * SCALE

    @pl.when(jnp.logical_not(holder))
    def _():
        part_l.wait_recv()
        loss_ref[...] = loss_in[...]
        part_dq.wait_recv()
        dq_ref[...] = (dq_in[...] - d_ref[...]) * SCALE

    sib_dd.wait_send()

    @pl.when(holder)
    def _():
        part_l.wait_send()
        part_dq.wait_send()


def hand_on(*refs):
    for source, target in zip(refs[:4], refs[4:]):
        target[...] = source[...]


def per_device(question_matrix, document_matrix, pool, hard_owner, hard_local):
    vmem = pl.BlockSpec(memory_space=pltpu.VMEM)
    f = lambda *shape: pltpu.VMEM(shape, F32)
    scratch = [
        pltpu.VMEM((16, 128), jnp.int32),
        pltpu.VMEM((4, 16, 128), jnp.int32),
        f(192, 128),
        f(2, 4, 128, 384),
        f(2, 4, 128, 384),
        f(128, 256),
        f(64, 256),
        f(2, 4, 2, 64, 384),
        f(2, 8, 64, 384),
        f(8, 512),
        f(8, 512),
        f(8, 1, 128),
        f(16, 1, 128),
        f(128, 128),
        pltpu.VMEM((3, 256, 2048), BF16),
        f(16, 64, 384),
        f(2, 8, 64, 384),
        f(8, 128, 384),
        f(16, 64, 384),
        f(16, 64, 384),
        f(128, 128),
        f(128, 128),
        f(8, 512),
        f(512, 512),
        f(512, 512),
        f(1, 1024),
        f(16, 1, 1024),
        f(8, 1, 128),
        f(16, 1, 128),
        f(2, 4, 2, 64, 384),
        f(4, 2, 2, 32, 384),
        f(4, 4, 32, 384),
        f(2, 2, 32, 384),
        f(4, 32, 384),
        f(4, 32, 384),
        f(4, 32, 384),
        f(64, 256),
        f(64, 256),
        f(128, 256),
        f(2, 256, 384),
        f(2, 256, 384),
        f(4, 128, 384),
        f(8, 128, 384),
        pltpu.VMEM((512, 1024), BF16),
        pltpu.VMEM((3, 8, 128, 384), BF16),
        pltpu.VMEM((2, 192, 2048), BF16),
        f(192, 128),
        f(192, 128),
        f(1, 128),
        f(1, 128),
        f(1, 128),
        f(1, 128),
        f(1, 512),
        pltpu.SemaphoreType.DMA((4, 16)),
        pltpu.SemaphoreType.DMA((4, 16)),
        pltpu.SemaphoreType.DMA((4, 4)),
        pltpu.SemaphoreType.DMA((4, 4)),
        pltpu.SemaphoreType.DMA((4, 4)),
        pltpu.SemaphoreType.DMA((4, 4)),
        pltpu.SemaphoreType.DMA((16,)),
        pltpu.SemaphoreType.DMA((16,)),
        pltpu.SemaphoreType.DMA((8,)),
        pltpu.SemaphoreType.DMA((4,)),
        pltpu.SemaphoreType.DMA((8,)),
        pltpu.SemaphoreType.DMA((4,)),
        pltpu.SemaphoreType.DMA((4,)),
        pltpu.SemaphoreType.DMA((8,)),
        pltpu.SemaphoreType.DMA((2,)),
        pltpu.SemaphoreType.DMA((2,)),
        pltpu.SemaphoreType.DMA((9,)),
        pltpu.SemaphoreType.DMA((9,)),
    ]
    results = pl.pallas_call(
        kernel,
        name="retriever_step",
        out_shape=(
            jax.ShapeDtypeStruct((1, 128), F32),
            jax.ShapeDtypeStruct((192, 128), F32),
            jax.ShapeDtypeStruct((192, 128), F32),
            jax.ShapeDtypeStruct((192, 2048), F32),
        ),
        in_specs=[vmem] * 5,
        out_specs=(vmem,) * 4,
        scratch_shapes=scratch,
        compiler_params=pltpu.CompilerParams(
            collective_id=0, has_side_effects=True, vmem_limit_bytes=60 * 1024 * 1024
        ),
    )(question_matrix.T, document_matrix.T, pool, hard_owner.T, hard_local.T)
    loss, dq, dd, gp = pl.pallas_call(
        hand_on,
        name="results",
        out_shape=tuple(jax.ShapeDtypeStruct(r.shape, r.dtype) for r in results),
        in_specs=[vmem] * 4,
        out_specs=(vmem,) * 4,
    )(*results)
    return loss.reshape(128), dq.T, dd.T, gp


def solution(mesh):
    placed = (P("blk", "dim"), P("blk", "dim"), P("dim", "blk"), P("blk", None), P("blk", None))
    return jax.shard_map(
        per_device,
        mesh=mesh,
        in_specs=placed,
        out_specs=(P("blk"), P("blk", "dim"), P("blk", "dim"), P("dim", "blk")),
        check_vma=False,
    )
```

```python
import jax
import jax.numpy as jnp
from jax import lax
from jax.experimental import pallas as pl
from jax.experimental.pallas import tpu as pltpu
from jax.sharding import PartitionSpec as P

MESH = pl.DeviceIdType.MESH
F32 = jnp.float32
BF16 = jnp.bfloat16
HIGHEST = lax.Precision.HIGHEST
SCALE = 20.0

NT = (((1,), (1,)), ((), ()))
NN = (((1,), (0,)), ((), ()))


def mm(a, b, dims, precision=None):
    return lax.dot_general(a, b, dims, precision=precision, preferred_element_type=F32)


def split3(x):
    high = x.astype(BF16)
    rest = x - high.astype(F32)
    mid = rest.astype(BF16)
    low = (rest - mid.astype(F32)).astype(BF16)
    return high, mid, low


def loop(count, body):
    def step(i, carry):
        body(i)
        return carry

    lax.fori_loop(0, count, step, 0)


def halves(x):
    return x[:, :128], x[:, 128:256], x[:, 256:384]


def low(rows):
    return lax.broadcasted_iota(jnp.int32, (rows, 128), 1) < 64


def turned(x):
    return pltpu.roll(x, 64, 1)


def fold(a, b):
    keep = low(a.shape[0])
    b0, b1 = turned(b[:, :128]), turned(b[:, 128:256])
    return jnp.concatenate(
        [a[:, :128], jnp.where(keep, a[:, 128:256], b0), jnp.where(keep, b0, b1)], axis=1
    )


def unfold(x):
    x0, x1, x2 = halves(x)
    x1t, x2t = turned(x1), turned(x2)
    return (
        jnp.concatenate([x0, x1], axis=1),
        jnp.concatenate([jnp.where(low(x.shape[0]), x1t, x2t), x2t], axis=1),
    )


def regroup(x, y):
    x0, x1, x2 = halves(x)
    y0, y1, y2 = halves(y)
    keep = low(x.shape[0])
    x1t, x2t, y0t, y1t = turned(x1), turned(x2), turned(y0), turned(y1)
    first = jnp.concatenate([x0, jnp.where(keep, x1, y0t), jnp.where(keep, y0t, y1t)], axis=1)
    last = jnp.concatenate([jnp.where(keep, x1t, x2t), jnp.where(keep, x2t, y1), y2], axis=1)
    return first, last


def upright(x):
    return jnp.concatenate([x, jnp.zeros((64, 128), F32)], axis=0).T


REQ, ROWS, QUERY, PROB = range(4)
SIB_D, SIB_Q, SIB_H, SIB_G, SIB_DD, SIB_P, PART_Q, PART_DQ, PART_L = range(9)
DOC_1, DOC_2, GRAD_1, GRAD_2 = range(4)


def kernel(
    q_ref, d_ref, pool_ref, owner_ref, local_ref,
    loss_ref, dq_ref, dd_ref, gp_ref,
    idx_mine, idx_all, q_part, q_all, q_re, d_nat, d_sib, d_raw, d_all, lr_all, sid,
    rq_out, rq_in, lt, pool_s,
    p_out, p_in, p_all, f_out, f_in, hs_mine, hs_sib, hq, st, ch, stat_out, stat_in,
    hc_out, hc_in, g3_out, c1x, c1y, cx, cy, c2x, c2y, dd_out, dd_sib, dd_nat, g_sib_out, g_sib_in, g_own, g_hard, scales, g_out, g_in, hots_t, hp, at_s,
    dq_out, dq_in, loss_out, loss_in, pos_out, pos_in, lrow,
    plane_s, plane_r, x_s, x_r, y_s, y_r, row_s, row_r, idx_s, idx_r, qs, qr, gs, gr, one_s, one_r,
):
    blk, dim = lax.axis_index("blk"), lax.axis_index("dim")
    xy, z = blk // 8, blk % 8
    yh, c = dim // 2, dim % 2
    t = z // 2
    holder = (z % 2) == yh
    me_p = xy * 2 + yh
    me_r = z * 2 + c
    x, yl = xy // 2, xy % 2
    y = yh * 2 + yl

    def plane_dev(p):
        return ((p // 2) * 8 + z, (p % 2) * 2 + c)

    def row_dev(r):
        return (xy * 8 + r // 2, yh * 2 + r % 2)

    def x_dev(xx):
        return ((xx * 2 + yl) * 8 + z, dim)

    def y_dev(yy):
        return ((x * 2 + yy % 2) * 8 + z, (yy // 2) * 2 + c)

    def z_dev(zz):
        return (xy * 8 + zz, dim)

    sibling = (blk, yh * 2 + (1 - c))
    partner = (blk, (1 - yh) * 2 + c)

    def remote(src, dst, send, recv, device):
        return pltpu.make_async_remote_copy(
            src_ref=src, dst_ref=dst, send_sem=send, recv_sem=recv,
            device_id=device, device_id_type=MESH,
        )

    barrier = pltpu.get_barrier_semaphore()

    def greet(k):
        pl.semaphore_signal(barrier, inc=1, device_id=plane_dev((me_p + k + 1) % 16), device_id_type=MESH)
        pl.semaphore_signal(barrier, inc=1, device_id=row_dev((me_r + k + 1) % 16), device_id_type=MESH)

    loop(15, greet)
    idx_mine[0:8] = owner_ref[...]
    idx_mine[8:16] = local_ref[...]
    d_nat[...] = upright(d_ref[...])
    for k, part in enumerate(split3(pool_ref[...])):
        pool_s[k, 0:192] = part
        pool_s[k, 192:256] = jnp.zeros((64, 2048), BF16)
    pl.semaphore_wait(barrier, 30)

    def idx_copy(zz):
        return remote(idx_mine, idx_all.at[t], idx_s.at[zz], idx_r.at[t], z_dev(zz))

    def q_copy(zz):
        return remote(q_all.at[c, t], q_all.at[c, t], qs.at[zz], qr.at[t], z_dev(zz))

    sib_d = remote(
        d_nat.at[pl.ds((1 - c) * 64, 64)], d_sib, one_s.at[SIB_D], one_r.at[SIB_D], sibling
    )
    part_q = remote(q_ref, q_part, one_s.at[PART_Q], one_r.at[PART_Q], partner)

    @pl.when(holder)
    def _():
        loop(7, lambda k: idx_copy((z + k + 1) % 8).start())
        idx_all[t] = idx_mine[...]

    sib_d.start()

    @pl.when(jnp.logical_not(holder))
    def _():
        part_q.start()

    sib_d.wait_recv()
    own_d = d_nat[pl.ds(pl.multiple_of(c * 64, 64), 64), :]
    d_raw[yh, x, yl] = fold(
        jnp.where(c == 0, own_d, d_sib[...]), jnp.where(c == 0, d_sib[...], own_d)
    )

    def doc_x1(xx, slot):
        piece = d_raw.at[yh, slot, yl, pl.ds(0, 32)]
        return remote(piece, piece, x_s.at[DOC_1, xx], x_r.at[DOC_1, slot], x_dev(xx))

    def doc_y1(yy, slot):
        piece = d_raw.at[slot // 2, x, slot % 2, pl.ds(32, 32)]
        return remote(piece, piece, y_s.at[DOC_1, yy], y_r.at[DOC_1, slot], y_dev(yy))

    def doc_y2(yy, slot):
        piece = d_raw.at[slot // 2, :, slot % 2, pl.ds(0, 32)]
        return remote(piece, piece, y_s.at[DOC_2, yy], y_r.at[DOC_2, slot], y_dev(yy))

    def doc_x2(xx, slot):
        piece = d_raw.at[:, slot, :, pl.ds(32, 32)]
        return remote(piece, piece, x_s.at[DOC_2, xx], x_r.at[DOC_2, slot], x_dev(xx))

    def doc_first(k):
        doc_x1((x + k + 1) % 4, x).start()
        doc_y1((y + k + 1) % 4, y).start()

    loop(3, doc_first)

    def idx_wait(tt):
        @pl.when(2 * tt + yh != z)
        def _():
            remote(idx_mine, idx_all.at[tt], idx_s.at[0], idx_r.at[tt], partner).wait_recv()

    loop(4, idx_wait)
    sub8 = lax.broadcasted_iota(jnp.int32, (8, 128), 0)
    upper = jnp.where(
        lax.broadcasted_iota(jnp.int32, (128, 128), 0) < lax.broadcasted_iota(jnp.int32, (128, 128), 1),
        1.0, 0.0,
    ).astype(BF16)
    for tt in range(4):
        owner = idx_all[tt, 0:8]
        local = idx_all[tt, 8:16] + 1
        table = jnp.zeros((8, 128), jnp.int32)
        for a in range(8):
            row = jnp.sum(jnp.where(owner == a * 8 + z, local, 0), axis=0, keepdims=True)
            table = jnp.where(sub8 == a, row, table)
        marks = jnp.where(table > 0, 1.0, 0.0)
        rank = mm(marks.astype(BF16), upper, NN)
        lr_all[:, tt * 128 : (tt + 1) * 128] = table.astype(F32)
        sid[:, tt * 128 : (tt + 1) * 128] = jnp.where(table > 0, rank + float(tt * 32), -1.0)

    sub512 = lax.broadcasted_iota(jnp.int32, (128, 512), 0).astype(F32)
    lane128 = lax.broadcasted_iota(jnp.int32, (128, 128), 1)

    def hot(a):
        return sub512 == sid[pl.ds(a, 1), :]

    def columns(rows):
        def step(a, table):
            col = jnp.sum(jnp.where(hot(a), rows[pl.ds(a, 1), :], 0.0), axis=1, keepdims=True)
            return jnp.where(lane128 == a, col, table)

        return lax.fori_loop(0, 8, step, jnp.zeros((128, 128), F32))

    wanted = columns(lr_all).T
    for a in range(8):
        rq_out[a] = wanted[a : a + 1, :]
    rq_in[me_p] = rq_out[xy]

    def req_copy(p, slot):
        return remote(
            rq_out.at[p // 2], rq_in.at[slot], plane_s.at[REQ, p], plane_r.at[REQ, slot], plane_dev(p)
        )

    loop(15, lambda k: req_copy((me_p + k + 1) % 16, me_p).start())

    def doc_second(k):
        xx, yy = (x + k + 1) % 4, (y + k + 1) % 4
        doc_x1(xx, xx).wait_recv()
        doc_y1(yy, yy).wait_recv()

    loop(3, doc_second)

    def doc_on(k):
        doc_y2((y + k + 1) % 4, y).start()
        doc_x2((x + k + 1) % 4, x).start()

    loop(3, doc_on)

    @pl.when(holder)
    def _():
        remote(q_ref, q_part, one_s.at[PART_Q], one_r.at[PART_Q], partner).wait_recv()
        own, other = upright(q_ref[...]), upright(q_part[...])
        q_all[c, t] = fold(jnp.where(yh == 0, own, other), jnp.where(yh == 0, other, own))
        loop(7, lambda k: q_copy((z + k + 1) % 8).start())

    def req_wait(k):
        p = (me_p + k + 1) % 16
        req_copy(p, p).wait_recv()

    loop(15, req_wait)
    named = jnp.concatenate([rq_in[i] for i in range(16)] + [jnp.zeros((112, 128), F32)], axis=0)
    lt[...] = named.T
    lane2048 = lax.broadcasted_iota(jnp.int32, (128, 2048), 1).astype(F32) + 1.0

    def rows_copy(p, slot):
        return remote(
            p_out.at[p], p_in.at[slot % 2, slot // 2],
            plane_s.at[ROWS, p], plane_r.at[ROWS, slot], plane_dev(p),
        )

    def fetch(g):
        hots = []
        for i in range(4):
            col = jnp.sum(jnp.where(lane128 == g * 4 + i, lt[...], 0.0), axis=1, keepdims=True)
            hots.append(jnp.where(col == lane2048, 1.0, 0.0).astype(BF16))
        hots = jnp.concatenate(hots, axis=0)
        got = mm(hots, pool_s[0], NT) + mm(hots, pool_s[1], NT) + mm(hots, pool_s[2], NT)
        for i in range(4):
            p = g * 4 + i
            p_out[p] = fold(got[i * 128 : i * 128 + 64], got[i * 128 + 64 : i * 128 + 128])

            @pl.when(p != me_p)
            def _():
                rows_copy(p, me_p).start()

    loop(4, fetch)
    p_in[yh, xy] = p_out[me_p]

    def q_wait(tt):
        @pl.when(2 * tt + yh != z)
        def _():
            remote(q_all.at[c, tt], q_all.at[c, tt], qs.at[0], qr.at[tt], partner).wait_recv()

    loop(4, q_wait)
    sib_q = remote(q_all.at[c], q_all.at[c], one_s.at[SIB_Q], one_r.at[SIB_Q], sibling)
    sib_q.start()

    queries = split3(q_all[c].reshape(512, 384))

    def pick(g):
        hots = jnp.concatenate(
            [jnp.where(hot(g * 4 + i), 1.0, 0.0).astype(BF16) for i in range(4)], axis=0
        )
        got = mm(hots, queries[0], NN) + mm(hots, queries[1], NN) + mm(hots, queries[2], NN)
        for i in range(4):
            first, last = regroup(got[i * 128 : i * 128 + 64], got[i * 128 + 64 : i * 128 + 128])
            f_out[(g * 4 + i) * 2] = first
            f_out[(g * 4 + i) * 2 + 1] = last

    loop(2, pick)
    f_in[me_p] = f_out[me_p]

    remote(q_all.at[c], q_all.at[1 - c], one_s.at[SIB_Q], one_r.at[SIB_Q], sibling).wait_recv()

    def rearrange_q(tt):
        first, last = regroup(q_all[0, tt], q_all[1, tt])
        q_re[0, tt] = first
        q_re[1, tt] = last

    loop(4, rearrange_q)

    def doc_wait(k):
        xx, yy = (x + k + 1) % 4, (y + k + 1) % 4
        doc_y2(yy, yy).wait_recv()
        doc_x2(xx, xx).wait_recv()

    loop(3, doc_wait)

    def score(j):
        total = None
        for part in range(2):
            docs = d_raw[part, pl.ds(j * 2, 2)].reshape(256, 384)
            value = mm(docs, q_re[part].reshape(512, 384), NT, HIGHEST)
            total = value if total is None else total + value
        st[pl.ds(pl.multiple_of(j * 256, 256), 256), :] = total * SCALE

    loop(2, score)

    def top(j, best):
        rows = st[pl.ds(pl.multiple_of(j * 64, 64), 64), :].reshape(8, 8, 512)
        return jnp.maximum(best, jnp.max(rows, axis=0))

    best = lax.fori_loop(0, 8, top, jnp.full((8, 512), -jnp.inf, F32))
    best = jnp.max(best, axis=0, keepdims=True)

    square = st[pl.ds(pl.multiple_of(xy * 64, 64), 64), pl.ds(pl.multiple_of(t * 128, 128), 128)]
    on_diagonal = lax.broadcasted_iota(jnp.int32, (64, 128), 1) == (
        lax.broadcasted_iota(jnp.int32, (64, 128), 0) + c * 64
    )
    positive = jnp.sum(jnp.where(on_diagonal, square, 0.0), axis=0, keepdims=True)
    pos_out[:, 0:128] = positive
    pos_out[:, 128:640] = best
    sib_p = remote(pos_out, pos_in, one_s.at[SIB_P], one_r.at[SIB_P], sibling)

    def weigh(j, total):
        rows = pl.ds(pl.multiple_of(j * 128, 128), 128)
        value = jnp.exp(st[rows, :] - best)
        st[rows, :] = value
        ch[:, rows] = value.T
        return total + jnp.sum(value.reshape(16, 8, 512), axis=0)

    weight = lax.fori_loop(0, 4, weigh, jnp.zeros((8, 512), F32))
    weight = jnp.sum(weight, axis=0, keepdims=True)

    def rearrange_d(k):
        first, last = regroup(d_raw[0, k // 2, k % 2], d_raw[1, k // 2, k % 2])
        d_all[0, k] = first
        d_all[1, k] = last

    loop(8, rearrange_d)
    sib_p.start()

    def rows_wait(k):
        p = (me_p + k + 1) % 16
        rows_copy(p, p).wait_recv()

    loop(15, rows_wait)
    low64 = low(64)

    def hard_part(a, table):
        terms = p_in[0, a] * f_out[a * 2] + p_in[1, a] * f_out[a * 2 + 1]
        t0, t1, t2 = halves(terms)
        first = jnp.sum(t0 + jnp.where(low64, t1, 0.0), axis=1, keepdims=True)
        last = jnp.sum(t2 + jnp.where(low64, 0.0, t1), axis=1, keepdims=True)
        return jnp.where(lane128 == a, jnp.concatenate([first, last], axis=0), table)

    hs_mine[...] = lax.fori_loop(0, 8, hard_part, jnp.zeros((128, 128), F32))
    sib_h = remote(hs_mine, hs_sib, one_s.at[SIB_H], one_r.at[SIB_H], sibling)
    sib_h.start()

    def query_copy(p, slot):
        return remote(
            f_out.at[p], f_in.at[slot], plane_s.at[QUERY, p], plane_r.at[QUERY, slot], plane_dev(p)
        )

    loop(15, lambda k: query_copy((me_p + k + 1) % 16, me_p).start())

    g_sib_out[...] = mm(ch[...], d_all[1 - c].reshape(512, 384), NN, HIGHEST)
    sib_g = remote(g_sib_out, g_sib_in, one_s.at[SIB_G], one_r.at[SIB_G], sibling)
    sib_g.start()

    sib_h.wait_recv()
    hard = (hs_mine[...] + hs_sib[...]) * SCALE
    for a in range(8):
        row = jnp.sum(jnp.where(hot(a), hard[:, a : a + 1], 0.0), axis=0, keepdims=True)
        hq[a : a + 1, :] = jnp.where(sid[a : a + 1, :] >= 0.0, row, -jnp.inf)
    peak = jnp.maximum(best, jnp.max(hq[...], axis=0, keepdims=True))
    hq[...] = jnp.exp(hq[...] - peak)
    total = jnp.sum(hq[...], axis=0, keepdims=True) * jnp.where(c == 0, 1.0, 0.0)
    total = total + weight * jnp.exp(best - peak)

    stat_out[:, 0:512] = peak
    stat_out[:, 512:1024] = total
    stat_in[me_r] = stat_out[...]

    def stat_copy(r, slot):
        return remote(stat_out, stat_in.at[slot], row_s.at[r], row_r.at[slot], row_dev(r))

    loop(15, lambda k: stat_copy((me_r + k + 1) % 16, me_r).start())

    def rearrange_p(k):
        first, last = regroup(p_in[0, k], p_in[1, k])
        p_all[k, 0:64] = first
        p_all[k, 64:128] = last

    loop(8, rearrange_p)
    sid_t = jnp.concatenate([sid[...], jnp.zeros((120, 512), F32)], axis=0).T
    lane512 = lax.broadcasted_iota(jnp.int32, (512, 128), 1).astype(F32)
    for a in range(8):
        hots_t[:, a * 128 : (a + 1) * 128] = jnp.where(
            sid_t[:, a : a + 1] == lane512, 1.0, 0.0
        ).astype(BF16)

    shares = columns(hq)
    for a in range(8):
        for k, part in enumerate(split3(p_all[a] * shares[:, a : a + 1])):
            hp[k, a] = part
    g_hard[...] = (
        mm(hots_t[...], hp[0].reshape(1024, 384), NN)
        + mm(hots_t[...], hp[1].reshape(1024, 384), NN)
        + mm(hots_t[...], hp[2].reshape(1024, 384), NN)
    )
    g_own[...] = mm(ch[...], d_all[c].reshape(512, 384), NN, HIGHEST)

    def stat_wait(k):
        r = (me_r + k + 1) % 16
        stat_copy(r, r).wait_recv()

    loop(15, stat_wait)
    peaks = jnp.concatenate([stat_in[r, :, 0:512] for r in range(16)], axis=0)
    totals = jnp.concatenate([stat_in[r, :, 512:1024] for r in range(16)], axis=0)
    most = jnp.max(peaks, axis=0, keepdims=True)
    total = jnp.sum(totals * jnp.exp(peaks - most), axis=0, keepdims=True)
    log_total = most + jnp.log(total)
    lrow[...] = log_total

    sib_p.wait_recv()
    to_own = jnp.exp(best - log_total)
    to_hard = jnp.exp(peak - log_total)
    to_sib = jnp.exp(pos_in[:, 128:640] - log_total)
    scales[...] = jnp.concatenate([to_own, to_hard, to_sib, jnp.zeros((125, 512), F32)], axis=0).T
    sib_g.wait_recv()

    def grad_copy(tt, slot):
        return remote(g_out.at[tt], g_in.at[slot], gs.at[tt], gr.at[slot], z_dev(2 * tt + yh))

    def grad_send(tt):
        rows = pl.ds(pl.multiple_of(tt * 128, 128), 128)
        by = scales[rows, :]
        g_out[tt] = (
            g_own[rows, :] * by[:, 0:1] + g_sib_in[rows, :] * by[:, 2:3]
        ) + g_hard[rows, :] * by[:, 1:2]

        @pl.when(2 * tt + yh != z)
        def _():
            grad_copy(tt, z).start()

    loop(4, grad_send)

    @pl.when(holder)
    def _():
        g_in[z] = g_out[t]

    hq[...] = hq[...] * to_hard
    chances = columns(hq).T
    for a in range(8):
        hc_out[a] = chances[a : a + 1, :]
    hc_in[me_p] = hc_out[xy]

    def prob_copy(p, slot):
        return remote(
            hc_out.at[p // 2], hc_in.at[slot], plane_s.at[PROB, p], plane_r.at[PROB, slot], plane_dev(p)
        )

    loop(15, lambda k: prob_copy((me_p + k + 1) % 16, me_p).start())

    def chance(j):
        rows = pl.ds(pl.multiple_of(j * 128, 128), 128)
        st[rows, :] = st[rows, :] * to_own

    loop(4, chance)

    def doc_grad(part):
        value = mm(st[...], q_re[part].reshape(512, 384), NN, HIGHEST)
        g3_out[part] = value.reshape(4, 2, 64, 384)

    loop(2, doc_grad)

    def grad_y1(yy, slot):
        return remote(
            g3_out.at[yy // 2, :, yy % 2, pl.ds(0, 32)], c1y.at[slot],
            y_s.at[GRAD_1, yy], y_r.at[GRAD_1, slot], y_dev(yy),
        )

    def grad_x1(xx, slot):
        return remote(
            g3_out.at[:, xx, :, pl.ds(32, 32)], c1x.at[slot],
            x_s.at[GRAD_1, xx], x_r.at[GRAD_1, slot], x_dev(xx),
        )

    def grad_x2(xx, slot):
        return remote(cy.at[xx], c2x.at[slot], x_s.at[GRAD_2, xx], x_r.at[GRAD_2, slot], x_dev(xx))

    def grad_y2(yy, slot):
        return remote(
            cx.at[yy // 2, yy % 2], c2y.at[slot], y_s.at[GRAD_2, yy], y_r.at[GRAD_2, slot], y_dev(yy)
        )

    def grad_first(k):
        grad_y1((y + k + 1) % 4, y).start()
        grad_x1((x + k + 1) % 4, x).start()

    loop(3, grad_first)

    def query_wait(k):
        p = (me_p + k + 1) % 16
        query_copy(p, p).wait_recv()
        prob_copy(p, p).wait_recv()

    loop(15, query_wait)
    chances = jnp.concatenate([hc_in[i] for i in range(16)] + [jnp.zeros((112, 128), F32)], axis=0).T

    def turn(i):
        col = jnp.sum(jnp.where(lane128 == i, chances, 0.0), axis=1, keepdims=True)
        rows = jnp.concatenate(unfold(f_in[i]), axis=0) * (col * SCALE)
        terms = split3(rows.T[0:192])
        for k in range(2):
            at_s[k, :, pl.ds(pl.multiple_of(i * 128, 128), 128)] = terms[k]

    loop(16, turn)
    lane256 = lax.broadcasted_iota(jnp.int32, (128, 256), 1).astype(F32) + 1.0

    def pool_grad(n):
        base = (n * 256).astype(F32)
        hots = jnp.concatenate(
            [
                jnp.where(lt[:, i : i + 1] == lane256 + base, 1.0, 0.0).astype(BF16)
                for i in range(16)
            ],
            axis=0,
        )
        value = mm(at_s[0], hots, NN) + mm(at_s[1], hots, NN)
        gp_ref[:, pl.ds(pl.multiple_of(n * 256, 256), 256)] = value

    loop(4, pool_grad)

    def grad_second(k):
        xx, yy = (x + k + 1) % 4, (y + k + 1) % 4
        grad_y1(yy, yy).wait_recv()
        grad_x1(xx, xx).wait_recv()

    loop(3, grad_second)

    def sum_y(xx):
        cy[xx] = (g3_out[yh, xx, yl, 0:32] + c1y[(y + 1) % 4, xx]) + (
            c1y[(y + 2) % 4, xx] + c1y[(y + 3) % 4, xx]
        )

    loop(4, sum_y)

    def sum_x(k):
        a, b = k // 2, k % 2
        cx[a, b] = (g3_out[a, x, b, 32:64] + c1x[(x + 1) % 4, a, b]) + (
            c1x[(x + 2) % 4, a, b] + c1x[(x + 3) % 4, a, b]
        )

    loop(4, sum_x)

    def grad_on(k):
        grad_x2((x + k + 1) % 4, x).start()
        grad_y2((y + k + 1) % 4, y).start()

    loop(3, grad_on)
    loop(4, lambda n: pool_grad(n + 4))

    def grad_wait(k):
        xx, yy = (x + k + 1) % 4, (y + k + 1) % 4
        grad_x2(xx, xx).wait_recv()
        grad_y2(yy, yy).wait_recv()

    loop(3, grad_wait)
    upper_rows = (cy[x] + c2x[(x + 1) % 4]) + (c2x[(x + 2) % 4] + c2x[(x + 3) % 4])
    lower_rows = (cx[yh, yl] + c2y[(y + 1) % 4]) + (c2y[(y + 2) % 4] + c2y[(y + 3) % 4])
    value = jnp.concatenate([upper_rows, lower_rows], axis=0)
    first, last = unfold(value)
    dd_out[...] = jnp.where(c == 0, last, first)
    sib_dd = remote(dd_out, dd_sib, one_s.at[SIB_DD], one_r.at[SIB_DD], sibling)
    sib_dd.start()
    dd_nat[pl.ds(pl.multiple_of(c * 64, 64), 64), :] = jnp.where(c == 0, first, last)

    sib_d.wait_send()
    sib_q.wait_send()
    sib_h.wait_send()
    sib_g.wait_send()

    def sent(k):
        p = (me_p + k + 1) % 16
        for copy in (req_copy, rows_copy, query_copy, prob_copy):
            copy(p, me_p).wait_send()
        stat_copy((me_r + k + 1) % 16, me_r).wait_send()

    loop(15, sent)

    def sent4(k):
        for copy in (doc_x1, doc_x2, grad_x1, grad_x2):
            copy((x + k + 1) % 4, x).wait_send()
        for copy in (doc_y1, doc_y2, grad_y1, grad_y2):
            copy((y + k + 1) % 4, y).wait_send()

    loop(3, sent4)
    sib_p.wait_send()

    def grad_sent(tt):
        @pl.when(2 * tt + yh != z)
        def _():
            grad_copy(tt, z).wait_send()

    loop(4, grad_sent)

    @pl.when(holder)
    def _():
        def z_sent(k):
            zz = (z + k + 1) % 8
            idx_copy(zz).wait_send()
            q_copy(zz).wait_send()

        loop(7, z_sent)

    @pl.when(jnp.logical_not(holder))
    def _():
        part_q.wait_send()

    part_dq = remote(dq_out, dq_in, one_s.at[PART_DQ], one_r.at[PART_DQ], partner)
    part_l = remote(loss_out, loss_in, one_s.at[PART_L], one_r.at[PART_L], partner)

    @pl.when(holder)
    def _():
        loss_out[...] = lrow[:, pl.ds(pl.multiple_of(t * 128, 128), 128)] - (
            pos_out[:, 0:128] + pos_in[:, 0:128]
        )
        part_l.start()

        def wait(k):
            zz = (z + k + 1) % 8
            grad_copy(t, zz).wait_recv()

        loop(7, wait)
        value = g_in[0]
        for zz in range(1, 8):
            value = value + g_in[zz]
        first, last = unfold(value)
        dq_out[...] = jnp.where(yh == 0, last, first).T[0:192]
        part_dq.start()
        dq_ref[...] = (jnp.where(yh == 0, first, last).T[0:192] - d_ref[...]) * SCALE
        loss_ref[...] = loss_out[...]

    sib_dd.wait_recv()
    dd_nat[pl.ds(pl.multiple_of((1 - c) * 64, 64), 64), :] = dd_sib[...]
    dd_ref[...] = (dd_nat[...].T[0:192] - q_ref[...]) * SCALE

    @pl.when(jnp.logical_not(holder))
    def _():
        part_l.wait_recv()
        loss_ref[...] = loss_in[...]
        part_dq.wait_recv()
        dq_ref[...] = (dq_in[...] - d_ref[...]) * SCALE

    sib_dd.wait_send()

    @pl.when(holder)
    def _():
        part_l.wait_send()
        part_dq.wait_send()


def hand_on(*refs):
    for source, target in zip(refs[:4], refs[4:]):
        target[...] = source[...]


def per_device(question_matrix, document_matrix, pool, hard_owner, hard_local):
    vmem = pl.BlockSpec(memory_space=pltpu.VMEM)
    f = lambda *shape: pltpu.VMEM(shape, F32)
    scratch = [
        pltpu.VMEM((16, 128), jnp.int32),
        pltpu.VMEM((4, 16, 128), jnp.int32),
        f(192, 128),
        f(2, 4, 128, 384),
        f(2, 4, 128, 384),
        f(128, 256),
        f(64, 256),
        f(2, 4, 2, 64, 384),
        f(2, 8, 64, 384),
        f(8, 512),
        f(8, 512),
        f(8, 1, 128),
        f(16, 1, 128),
        f(128, 128),
        pltpu.VMEM((3, 256, 2048), BF16),
        f(16, 64, 384),
        f(2, 8, 64, 384),
        f(8, 128, 384),
        f(16, 64, 384),
        f(16, 64, 384),
        f(128, 128),
        f(128, 128),
        f(8, 512),
        f(512, 512),
        f(512, 512),
        f(1, 1024),
        f(16, 1, 1024),
        f(8, 1, 128),
        f(16, 1, 128),
        f(2, 4, 2, 64, 384),
        f(4, 2, 2, 32, 384),
        f(4, 4, 32, 384),
        f(2, 2, 32, 384),
        f(4, 32, 384),
        f(4, 32, 384),
        f(4, 32, 384),
        f(64, 256),
        f(64, 256),
        f(128, 256),
        f(512, 384),
        f(512, 384),
        f(512, 384),
        f(512, 384),
        f(512, 128),
        f(4, 128, 384),
        f(8, 128, 384),
        pltpu.VMEM((512, 1024), BF16),
        pltpu.VMEM((3, 8, 128, 384), BF16),
        pltpu.VMEM((2, 192, 2048), BF16),
        f(192, 128),
        f(192, 128),
        f(1, 128),
        f(1, 128),
        f(1, 640),
        f(1, 640),
        f(1, 512),
        pltpu.SemaphoreType.DMA((4, 16)),
        pltpu.SemaphoreType.DMA((4, 16)),
        pltpu.SemaphoreType.DMA((4, 4)),
        pltpu.SemaphoreType.DMA((4, 4)),
        pltpu.SemaphoreType.DMA((4, 4)),
        pltpu.SemaphoreType.DMA((4, 4)),
        pltpu.SemaphoreType.DMA((16,)),
        pltpu.SemaphoreType.DMA((16,)),
        pltpu.SemaphoreType.DMA((8,)),
        pltpu.SemaphoreType.DMA((4,)),
        pltpu.SemaphoreType.DMA((8,)),
        pltpu.SemaphoreType.DMA((4,)),
        pltpu.SemaphoreType.DMA((4,)),
        pltpu.SemaphoreType.DMA((8,)),
        pltpu.SemaphoreType.DMA((9,)),
        pltpu.SemaphoreType.DMA((9,)),
    ]
    results = pl.pallas_call(
        kernel,
        name="retriever_step",
        out_shape=(
            jax.ShapeDtypeStruct((1, 128), F32),
            jax.ShapeDtypeStruct((192, 128), F32),
            jax.ShapeDtypeStruct((192, 128), F32),
            jax.ShapeDtypeStruct((192, 2048), F32),
        ),
        in_specs=[vmem] * 5,
        out_specs=(vmem,) * 4,
        scratch_shapes=scratch,
        compiler_params=pltpu.CompilerParams(
            collective_id=0, has_side_effects=True, vmem_limit_bytes=60 * 1024 * 1024
        ),
    )(question_matrix.T, document_matrix.T, pool, hard_owner.T, hard_local.T)
    loss, dq, dd, gp = pl.pallas_call(
        hand_on,
        name="results",
        out_shape=tuple(jax.ShapeDtypeStruct(r.shape, r.dtype) for r in results),
        in_specs=[vmem] * 4,
        out_specs=(vmem,) * 4,
    )(*results)
    return loss.reshape(128), dq.T, dd.T, gp


def solution(mesh):
    placed = (P("blk", "dim"), P("blk", "dim"), P("dim", "blk"), P("blk", None), P("blk", None))
    return jax.shard_map(
        per_device,
        mesh=mesh,
        in_specs=placed,
        out_specs=(P("blk"), P("blk", "dim"), P("blk", "dim"), P("dim", "blk")),
        check_vma=False,
    )
```

```python
import jax
import jax.numpy as jnp
from jax import lax
from jax.experimental import pallas as pl
from jax.experimental.pallas import tpu as pltpu
from jax.sharding import PartitionSpec as P

MESH = pl.DeviceIdType.MESH
F32 = jnp.float32
BF16 = jnp.bfloat16
HIGHEST = lax.Precision.HIGHEST
SCALE = 20.0

NT = (((1,), (1,)), ((), ()))
NN = (((1,), (0,)), ((), ()))


def mm(a, b, dims, precision=None):
    return lax.dot_general(a, b, dims, precision=precision, preferred_element_type=F32)


def split3(x):
    high = x.astype(BF16)
    rest = x - high.astype(F32)
    mid = rest.astype(BF16)
    low = (rest - mid.astype(F32)).astype(BF16)
    return high, mid, low


def loop(count, body):
    def step(i, carry):
        body(i)
        return carry

    lax.fori_loop(0, count, step, 0)


def halves(x):
    return x[:, :128], x[:, 128:256], x[:, 256:384]


def low(rows):
    return lax.broadcasted_iota(jnp.int32, (rows, 128), 1) < 64


def turned(x):
    return pltpu.roll(x, 64, 1)


def fold(a, b):
    keep = low(a.shape[0])
    b0, b1 = turned(b[:, :128]), turned(b[:, 128:256])
    return jnp.concatenate(
        [a[:, :128], jnp.where(keep, a[:, 128:256], b0), jnp.where(keep, b0, b1)], axis=1
    )


def unfold(x):
    x0, x1, x2 = halves(x)
    x1t, x2t = turned(x1), turned(x2)
    return (
        jnp.concatenate([x0, x1], axis=1),
        jnp.concatenate([jnp.where(low(x.shape[0]), x1t, x2t), x2t], axis=1),
    )


def regroup(x, y):
    x0, x1, x2 = halves(x)
    y0, y1, y2 = halves(y)
    keep = low(x.shape[0])
    x1t, x2t, y0t, y1t = turned(x1), turned(x2), turned(y0), turned(y1)
    first = jnp.concatenate([x0, jnp.where(keep, x1, y0t), jnp.where(keep, y0t, y1t)], axis=1)
    last = jnp.concatenate([jnp.where(keep, x1t, x2t), jnp.where(keep, x2t, y1), y2], axis=1)
    return first, last


def upright(x):
    return jnp.concatenate([x, jnp.zeros((64, 128), F32)], axis=0).T


REQ, ROWS, QUERY, PROB = range(4)
SIB_D, SIB_Q, SIB_H, _, SIB_DD, SIB_P, PART_Q, PART_DQ, PART_L = range(9)
DOC_1, DOC_2, GRAD_1, GRAD_2 = range(4)


def kernel(
    q_ref, d_ref, pool_ref, owner_ref, local_ref,
    loss_ref, dq_ref, dd_ref, gp_ref,
    idx_mine, idx_all, q_part, q_all, q_re, d_nat, d_sib, d_raw, d_all, lr_all, sid,
    rq_out, rq_in, lt, pool_s,
    p_out, p_in, p_all, f_out, f_in, hs_mine, hs_sib, hq, st, ch, stat_out, stat_in,
    hc_out, hc_in, g3_out, c1x, c1y, cx, cy, c2x, c2y, dd_out, dd_sib, dd_nat, g_sib_out, g_sib_in, g_out, g_in, hots_t, hp, at_s, hots_r,
    dq_out, dq_in, loss_out, loss_in, pos_out, pos_in, lrow,
    plane_s, plane_r, x_s, x_r, y_s, y_r, row_s, row_r, idx_s, idx_r, qs, qr, gs, gr, sg_s, sg_r, one_s, one_r,
):
    blk, dim = lax.axis_index("blk"), lax.axis_index("dim")
    xy, z = blk // 8, blk % 8
    yh, c = dim // 2, dim % 2
    t = z // 2
    holder = (z % 2) == yh
    me_p = xy * 2 + yh
    me_r = z * 2 + c
    x, yl = xy // 2, xy % 2
    y = yh * 2 + yl

    def plane_dev(p):
        return ((p // 2) * 8 + z, (p % 2) * 2 + c)

    def row_dev(r):
        return (xy * 8 + r // 2, yh * 2 + r % 2)

    def x_dev(xx):
        return ((xx * 2 + yl) * 8 + z, dim)

    def y_dev(yy):
        return ((x * 2 + yy % 2) * 8 + z, (yy // 2) * 2 + c)

    def z_dev(zz):
        return (xy * 8 + zz, dim)

    sibling = (blk, yh * 2 + (1 - c))
    partner = (blk, (1 - yh) * 2 + c)

    def remote(src, dst, send, recv, device):
        return pltpu.make_async_remote_copy(
            src_ref=src, dst_ref=dst, send_sem=send, recv_sem=recv,
            device_id=device, device_id_type=MESH,
        )

    barrier = pltpu.get_barrier_semaphore()

    def greet(k):
        pl.semaphore_signal(barrier, inc=1, device_id=plane_dev((me_p + k + 1) % 16), device_id_type=MESH)
        pl.semaphore_signal(barrier, inc=1, device_id=row_dev((me_r + k + 1) % 16), device_id_type=MESH)

    loop(15, greet)
    idx_mine[0:8] = owner_ref[...]
    idx_mine[8:16] = local_ref[...]
    d_nat[...] = upright(d_ref[...])
    for k, part in enumerate(split3(pool_ref[...])):
        pool_s[k, 0:192] = part
        pool_s[k, 192:256] = jnp.zeros((64, 2048), BF16)
    pl.semaphore_wait(barrier, 30)

    def idx_copy(zz):
        return remote(idx_mine, idx_all.at[t], idx_s.at[zz], idx_r.at[t], z_dev(zz))

    def q_copy(zz):
        return remote(q_all.at[c, t], q_all.at[c, t], qs.at[zz], qr.at[t], z_dev(zz))

    sib_d = remote(
        d_nat.at[pl.ds((1 - c) * 64, 64)], d_sib, one_s.at[SIB_D], one_r.at[SIB_D], sibling
    )
    part_q = remote(q_ref, q_part, one_s.at[PART_Q], one_r.at[PART_Q], partner)

    @pl.when(holder)
    def _():
        loop(7, lambda k: idx_copy((z + k + 1) % 8).start())
        idx_all[t] = idx_mine[...]

    sib_d.start()

    @pl.when(jnp.logical_not(holder))
    def _():
        part_q.start()

    sib_d.wait_recv()
    own_d = d_nat[pl.ds(pl.multiple_of(c * 64, 64), 64), :]
    d_raw[yh, x, yl] = fold(
        jnp.where(c == 0, own_d, d_sib[...]), jnp.where(c == 0, d_sib[...], own_d)
    )

    def doc_x1(xx, slot):
        piece = d_raw.at[yh, slot, yl, pl.ds(0, 32)]
        return remote(piece, piece, x_s.at[DOC_1, xx], x_r.at[DOC_1, slot], x_dev(xx))

    def doc_y1(yy, slot):
        piece = d_raw.at[slot // 2, x, slot % 2, pl.ds(32, 32)]
        return remote(piece, piece, y_s.at[DOC_1, yy], y_r.at[DOC_1, slot], y_dev(yy))

    def doc_y2(yy, slot):
        piece = d_raw.at[slot // 2, :, slot % 2, pl.ds(0, 32)]
        return remote(piece, piece, y_s.at[DOC_2, yy], y_r.at[DOC_2, slot], y_dev(yy))

    def doc_x2(xx, slot):
        piece = d_raw.at[:, slot, :, pl.ds(32, 32)]
        return remote(piece, piece, x_s.at[DOC_2, xx], x_r.at[DOC_2, slot], x_dev(xx))

    def doc_first(k):
        doc_x1((x + k + 1) % 4, x).start()
        doc_y1((y + k + 1) % 4, y).start()

    loop(3, doc_first)

    def idx_wait(tt):
        @pl.when(2 * tt + yh != z)
        def _():
            remote(idx_mine, idx_all.at[tt], idx_s.at[0], idx_r.at[tt], partner).wait_recv()

    loop(4, idx_wait)
    sub8 = lax.broadcasted_iota(jnp.int32, (8, 128), 0)
    upper = jnp.where(
        lax.broadcasted_iota(jnp.int32, (128, 128), 0) < lax.broadcasted_iota(jnp.int32, (128, 128), 1),
        1.0, 0.0,
    ).astype(BF16)
    for tt in range(4):
        owner = idx_all[tt, 0:8]
        local = idx_all[tt, 8:16] + 1
        table = jnp.zeros((8, 128), jnp.int32)
        for a in range(8):
            row = jnp.sum(jnp.where(owner == a * 8 + z, local, 0), axis=0, keepdims=True)
            table = jnp.where(sub8 == a, row, table)
        marks = jnp.where(table > 0, 1.0, 0.0)
        rank = mm(marks.astype(BF16), upper, NN)
        lr_all[:, tt * 128 : (tt + 1) * 128] = table.astype(F32)
        sid[:, tt * 128 : (tt + 1) * 128] = jnp.where(table > 0, rank + float(tt * 32), -1.0)

    sub512 = lax.broadcasted_iota(jnp.int32, (128, 512), 0).astype(F32)
    lane128 = lax.broadcasted_iota(jnp.int32, (128, 128), 1)

    def hot(a):
        return sub512 == sid[pl.ds(a, 1), :]

    def columns(rows):
        def step(a, table):
            col = jnp.sum(jnp.where(hot(a), rows[pl.ds(a, 1), :], 0.0), axis=1, keepdims=True)
            return jnp.where(lane128 == a, col, table)

        return lax.fori_loop(0, 8, step, jnp.zeros((128, 128), F32))

    wanted = columns(lr_all).T
    for a in range(8):
        rq_out[a] = wanted[a : a + 1, :]
    rq_in[me_p] = rq_out[xy]

    def req_copy(p, slot):
        return remote(
            rq_out.at[p // 2], rq_in.at[slot], plane_s.at[REQ, p], plane_r.at[REQ, slot], plane_dev(p)
        )

    loop(15, lambda k: req_copy((me_p + k + 1) % 16, me_p).start())

    @pl.when(holder)
    def _():
        remote(q_ref, q_part, one_s.at[PART_Q], one_r.at[PART_Q], partner).wait_recv()
        own, other = upright(q_ref[...]), upright(q_part[...])
        q_all[c, t] = fold(jnp.where(yh == 0, own, other), jnp.where(yh == 0, other, own))
        loop(7, lambda k: q_copy((z + k + 1) % 8).start())

    def doc_second(k):
        xx, yy = (x + k + 1) % 4, (y + k + 1) % 4
        doc_x1(xx, xx).wait_recv()
        doc_y1(yy, yy).wait_recv()

    loop(3, doc_second)

    def doc_on(k):
        doc_y2((y + k + 1) % 4, y).start()
        doc_x2((x + k + 1) % 4, x).start()

    loop(3, doc_on)

    def req_wait(k):
        p = (me_p + k + 1) % 16
        req_copy(p, p).wait_recv()

    loop(15, req_wait)
    named = jnp.concatenate([rq_in[i] for i in range(16)] + [jnp.zeros((112, 128), F32)], axis=0)
    lt[...] = named.T
    lane2048 = lax.broadcasted_iota(jnp.int32, (128, 2048), 1).astype(F32) + 1.0

    def rows_copy(p, slot):
        return remote(
            p_out.at[p], p_in.at[slot % 2, slot // 2],
            plane_s.at[ROWS, p], plane_r.at[ROWS, slot], plane_dev(p),
        )

    def fetch(g):
        hots = []
        for i in range(4):
            col = jnp.sum(jnp.where(lane128 == g * 4 + i, lt[...], 0.0), axis=1, keepdims=True)
            hots.append(jnp.where(col == lane2048, 1.0, 0.0).astype(BF16))
        hots = jnp.concatenate(hots, axis=0)
        hots_r[pl.ds(pl.multiple_of(g * 512, 512), 512), :] = hots
        got = mm(hots, pool_s[0], NT) + mm(hots, pool_s[1], NT) + mm(hots, pool_s[2], NT)
        for i in range(4):
            p = g * 4 + i
            p_out[p] = fold(got[i * 128 : i * 128 + 64], got[i * 128 + 64 : i * 128 + 128])

            @pl.when(p != me_p)
            def _():
                rows_copy(p, me_p).start()

    loop(4, fetch)
    p_in[yh, xy] = p_out[me_p]

    def q_wait(tt):
        @pl.when(2 * tt + yh != z)
        def _():
            remote(q_all.at[c, tt], q_all.at[c, tt], qs.at[0], qr.at[tt], partner).wait_recv()

    loop(4, q_wait)
    sib_q = remote(q_all.at[c], q_all.at[c], one_s.at[SIB_Q], one_r.at[SIB_Q], sibling)
    sib_q.start()

    queries = split3(q_all[c].reshape(512, 384))

    def pick(g):
        hots = jnp.concatenate(
            [jnp.where(hot(g * 4 + i), 1.0, 0.0).astype(BF16) for i in range(4)], axis=0
        )
        got = mm(hots, queries[0], NN) + mm(hots, queries[1], NN) + mm(hots, queries[2], NN)
        for i in range(4):
            first, last = regroup(got[i * 128 : i * 128 + 64], got[i * 128 + 64 : i * 128 + 128])
            f_out[(g * 4 + i) * 2] = first
            f_out[(g * 4 + i) * 2 + 1] = last

    loop(2, pick)
    f_in[me_p] = f_out[me_p]

    remote(q_all.at[c], q_all.at[1 - c], one_s.at[SIB_Q], one_r.at[SIB_Q], sibling).wait_recv()

    def rearrange_q(tt):
        first, last = regroup(q_all[0, tt], q_all[1, tt])
        q_re[0, tt] = first
        q_re[1, tt] = last

    loop(4, rearrange_q)

    def doc_wait(k):
        xx, yy = (x + k + 1) % 4, (y + k + 1) % 4
        doc_y2(yy, yy).wait_recv()
        doc_x2(xx, xx).wait_recv()

    loop(3, doc_wait)

    def score(j):
        total = None
        for part in range(2):
            docs = d_raw[part, pl.ds(j * 2, 2)].reshape(256, 384)
            value = mm(docs, q_re[part].reshape(512, 384), NT, HIGHEST)
            total = value if total is None else total + value
        st[pl.ds(pl.multiple_of(j * 256, 256), 256), :] = total * SCALE

    loop(2, score)

    def top(j, best):
        rows = st[pl.ds(pl.multiple_of(j * 64, 64), 64), :].reshape(8, 8, 512)
        return jnp.maximum(best, jnp.max(rows, axis=0))

    best = lax.fori_loop(0, 8, top, jnp.full((8, 512), -jnp.inf, F32))
    best = jnp.max(best, axis=0, keepdims=True)

    def rows_wait(k):
        p = (me_p + k + 1) % 16
        rows_copy(p, p).wait_recv()

    loop(15, rows_wait)
    low64 = low(64)

    def hard_part(a, table):
        terms = p_in[0, a] * f_out[a * 2] + p_in[1, a] * f_out[a * 2 + 1]
        t0, t1, t2 = halves(terms)
        first = jnp.sum(t0 + jnp.where(low64, t1, 0.0), axis=1, keepdims=True)
        last = jnp.sum(t2 + jnp.where(low64, 0.0, t1), axis=1, keepdims=True)
        return jnp.where(lane128 == a, jnp.concatenate([first, last], axis=0), table)

    hs_mine[...] = lax.fori_loop(0, 8, hard_part, jnp.zeros((128, 128), F32))
    sib_h = remote(hs_mine, hs_sib, one_s.at[SIB_H], one_r.at[SIB_H], sibling)
    sib_h.start()

    def query_copy(p, slot):
        return remote(
            f_out.at[p], f_in.at[slot], plane_s.at[QUERY, p], plane_r.at[QUERY, slot], plane_dev(p)
        )

    loop(15, lambda k: query_copy((me_p + k + 1) % 16, me_p).start())

    sib_h.wait_recv()
    hard = (hs_mine[...] + hs_sib[...]) * SCALE
    for a in range(8):
        row = jnp.sum(jnp.where(hot(a), hard[:, a : a + 1], 0.0), axis=0, keepdims=True)
        hq[a : a + 1, :] = jnp.where(sid[a : a + 1, :] >= 0.0, row, -jnp.inf)
    peak = jnp.maximum(best, jnp.max(hq[...], axis=0, keepdims=True))

    def add(j, total):
        rows = jnp.exp(st[pl.ds(pl.multiple_of(j * 64, 64), 64), :] - peak)
        return total + jnp.sum(rows.reshape(8, 8, 512), axis=0)

    total = lax.fori_loop(0, 8, add, jnp.zeros((8, 512), F32))
    total = total + jnp.exp(hq[...] - peak) * jnp.where(c == 0, 1.0, 0.0)
    total = jnp.sum(total, axis=0, keepdims=True)
    square = st[pl.ds(pl.multiple_of(xy * 64, 64), 64), pl.ds(pl.multiple_of(t * 128, 128), 128)]
    on_diagonal = lax.broadcasted_iota(jnp.int32, (64, 128), 1) == (
        lax.broadcasted_iota(jnp.int32, (64, 128), 0) + c * 64
    )
    positive = jnp.sum(jnp.where(on_diagonal, square, 0.0), axis=0, keepdims=True)
    pos_out[...] = positive
    sib_p = remote(pos_out, pos_in, one_s.at[SIB_P], one_r.at[SIB_P], sibling)
    stat_out[:, 0:512] = peak
    stat_out[:, 512:1024] = total
    stat_in[me_r] = stat_out[...]

    def stat_copy(r, slot):
        return remote(stat_out, stat_in.at[slot], row_s.at[r], row_r.at[slot], row_dev(r))

    loop(15, lambda k: stat_copy((me_r + k + 1) % 16, me_r).start())
    sib_p.start()

    def rearrange_d(k):
        first, last = regroup(d_raw[0, k // 2, k % 2], d_raw[1, k // 2, k % 2])
        d_all[0, k] = first
        d_all[1, k] = last
        first, last = regroup(p_in[0, k], p_in[1, k])
        p_all[k, 0:64] = first
        p_all[k, 64:128] = last

    loop(8, rearrange_d)
    sid_t = jnp.concatenate([sid[...], jnp.zeros((120, 512), F32)], axis=0).T
    lane512 = lax.broadcasted_iota(jnp.int32, (512, 128), 1).astype(F32)
    for a in range(8):
        hots_t[:, a * 128 : (a + 1) * 128] = jnp.where(
            sid_t[:, a : a + 1] == lane512, 1.0, 0.0
        ).astype(BF16)

    def stat_wait(k):
        r = (me_r + k + 1) % 16
        stat_copy(r, r).wait_recv()

    loop(15, stat_wait)
    peaks = jnp.concatenate([stat_in[r, :, 0:512] for r in range(16)], axis=0)
    totals = jnp.concatenate([stat_in[r, :, 512:1024] for r in range(16)], axis=0)
    peak = jnp.max(peaks, axis=0, keepdims=True)
    total = jnp.sum(totals * jnp.exp(peaks - peak), axis=0, keepdims=True)
    log_total = peak + jnp.log(total)
    lrow[...] = log_total

    hq[...] = jnp.exp(hq[...] - log_total)

    shares = columns(hq)
    chances = shares.T
    for a in range(8):
        hc_out[a] = chances[a : a + 1, :]
    hc_in[me_p] = hc_out[xy]

    def prob_copy(p, slot):
        return remote(
            hc_out.at[p // 2], hc_in.at[slot], plane_s.at[PROB, p], plane_r.at[PROB, slot], plane_dev(p)
        )

    loop(15, lambda k: prob_copy((me_p + k + 1) % 16, me_p).start())

    for a in range(8):
        for k, part in enumerate(split3(p_all[a] * shares[:, a : a + 1])):
            hp[k, a] = part

    def chance(j):
        rows = pl.ds(pl.multiple_of(j * 128, 128), 128)
        value = jnp.exp(st[rows, :] - log_total)
        st[rows, :] = value
        ch[:, rows] = value.T

    loop(4, chance)

    def sib_g(h):
        return remote(g_sib_out.at[h], g_sib_in.at[h], sg_s.at[h], sg_r.at[h], sibling)

    def grad_copy(tt, slot):
        return remote(g_out.at[tt], g_in.at[slot], gs.at[tt], gr.at[slot], z_dev(2 * tt + yh))

    def grad_half(h):
        rows = pl.ds(pl.multiple_of(h * 256, 256), 256)
        g_sib_out[h] = mm(ch[rows, :], d_all[1 - c].reshape(512, 384), NN, HIGHEST)
        sib_g(h).start()
        g_own = mm(ch[rows, :], d_all[c].reshape(512, 384), NN, HIGHEST)
        for k in range(3):
            g_own = g_own + mm(hots_t[rows, :], hp[k].reshape(1024, 384), NN)
        sib_g(h).wait_recv()
        g_out[pl.ds(h * 2, 2)] = (g_own + g_sib_in[h]).reshape(2, 128, 384)
        for i in range(2):
            tt = h * 2 + i

            @pl.when(2 * tt + yh != z)
            def _():
                grad_copy(tt, z).start()

    loop(2, grad_half)

    @pl.when(holder)
    def _():
        g_in[z] = g_out[t]

    def doc_grad(part):
        value = mm(st[...], q_re[part].reshape(512, 384), NN, HIGHEST)
        g3_out[part] = value.reshape(4, 2, 64, 384)

    loop(2, doc_grad)

    def grad_y1(yy, slot):
        return remote(
            g3_out.at[yy // 2, :, yy % 2, pl.ds(0, 32)], c1y.at[slot],
            y_s.at[GRAD_1, yy], y_r.at[GRAD_1, slot], y_dev(yy),
        )

    def grad_x1(xx, slot):
        return remote(
            g3_out.at[:, xx, :, pl.ds(32, 32)], c1x.at[slot],
            x_s.at[GRAD_1, xx], x_r.at[GRAD_1, slot], x_dev(xx),
        )

    def grad_x2(xx, slot):
        return remote(cy.at[xx], c2x.at[slot], x_s.at[GRAD_2, xx], x_r.at[GRAD_2, slot], x_dev(xx))

    def grad_y2(yy, slot):
        return remote(
            cx.at[yy // 2, yy % 2], c2y.at[slot], y_s.at[GRAD_2, yy], y_r.at[GRAD_2, slot], y_dev(yy)
        )

    def grad_first(k):
        grad_y1((y + k + 1) % 4, y).start()
        grad_x1((x + k + 1) % 4, x).start()

    loop(3, grad_first)
    def query_wait(k):
        p = (me_p + k + 1) % 16
        query_copy(p, p).wait_recv()
        prob_copy(p, p).wait_recv()

    loop(15, query_wait)
    chances = jnp.concatenate([hc_in[i] for i in range(16)] + [jnp.zeros((112, 128), F32)], axis=0).T

    def turn(i):
        col = jnp.sum(jnp.where(lane128 == i, chances, 0.0), axis=1, keepdims=True)
        rows = jnp.concatenate(unfold(f_in[i]), axis=0) * (col * SCALE)
        terms = split3(rows.T[0:192])
        for k in range(2):
            at_s[k * 192 : k * 192 + 192, pl.ds(pl.multiple_of(i * 128, 128), 128)] = terms[k]

    loop(16, turn)

    def pool_grad(n):
        columns_n = pl.ds(pl.multiple_of(n * 256, 256), 256)
        value = mm(at_s[...], hots_r[:, columns_n], NN)
        gp_ref[:, columns_n] = value[0:192] + value[192:384]

    loop(4, pool_grad)

    def grad_second(k):
        xx, yy = (x + k + 1) % 4, (y + k + 1) % 4
        grad_y1(yy, yy).wait_recv()
        grad_x1(xx, xx).wait_recv()

    loop(3, grad_second)

    def sum_y(xx):
        cy[xx] = (g3_out[yh, xx, yl, 0:32] + c1y[(y + 1) % 4, xx]) + (
            c1y[(y + 2) % 4, xx] + c1y[(y + 3) % 4, xx]
        )

    loop(4, sum_y)

    def sum_x(k):
        a, b = k // 2, k % 2
        cx[a, b] = (g3_out[a, x, b, 32:64] + c1x[(x + 1) % 4, a, b]) + (
            c1x[(x + 2) % 4, a, b] + c1x[(x + 3) % 4, a, b]
        )

    loop(4, sum_x)

    def grad_on(k):
        grad_x2((x + k + 1) % 4, x).start()
        grad_y2((y + k + 1) % 4, y).start()

    loop(3, grad_on)
    loop(4, lambda n: pool_grad(n + 4))

    def grad_wait(k):
        xx, yy = (x + k + 1) % 4, (y + k + 1) % 4
        grad_x2(xx, xx).wait_recv()
        grad_y2(yy, yy).wait_recv()

    loop(3, grad_wait)
    upper_rows = (cy[x] + c2x[(x + 1) % 4]) + (c2x[(x + 2) % 4] + c2x[(x + 3) % 4])
    lower_rows = (cx[yh, yl] + c2y[(y + 1) % 4]) + (c2y[(y + 2) % 4] + c2y[(y + 3) % 4])
    value = jnp.concatenate([upper_rows, lower_rows], axis=0)
    first, last = unfold(value)
    dd_out[...] = jnp.where(c == 0, last, first)
    sib_dd = remote(dd_out, dd_sib, one_s.at[SIB_DD], one_r.at[SIB_DD], sibling)
    sib_dd.start()
    dd_nat[pl.ds(pl.multiple_of(c * 64, 64), 64), :] = jnp.where(c == 0, first, last)

    sib_d.wait_send()
    sib_q.wait_send()
    sib_h.wait_send()
    loop(2, lambda h: sib_g(h).wait_send())

    def sent(k):
        p = (me_p + k + 1) % 16
        for copy in (req_copy, rows_copy, query_copy, prob_copy):
            copy(p, me_p).wait_send()
        stat_copy((me_r + k + 1) % 16, me_r).wait_send()

    loop(15, sent)

    def sent4(k):
        for copy in (doc_x1, doc_x2, grad_x1, grad_x2):
            copy((x + k + 1) % 4, x).wait_send()
        for copy in (doc_y1, doc_y2, grad_y1, grad_y2):
            copy((y + k + 1) % 4, y).wait_send()

    loop(3, sent4)
    sib_p.wait_send()

    def grad_sent(tt):
        @pl.when(2 * tt + yh != z)
        def _():
            grad_copy(tt, z).wait_send()

    loop(4, grad_sent)

    @pl.when(holder)
    def _():
        def z_sent(k):
            zz = (z + k + 1) % 8
            idx_copy(zz).wait_send()
            q_copy(zz).wait_send()

        loop(7, z_sent)

    @pl.when(jnp.logical_not(holder))
    def _():
        part_q.wait_send()

    part_dq = remote(dq_out, dq_in, one_s.at[PART_DQ], one_r.at[PART_DQ], partner)
    part_l = remote(loss_out, loss_in, one_s.at[PART_L], one_r.at[PART_L], partner)
    sib_p.wait_recv()

    @pl.when(holder)
    def _():
        loss_out[...] = lrow[:, pl.ds(pl.multiple_of(t * 128, 128), 128)] - (pos_out[...] + pos_in[...])
        part_l.start()

        def wait(k):
            zz = (z + k + 1) % 8
            grad_copy(t, zz).wait_recv()

        loop(7, wait)
        value = g_in[0]
        for zz in range(1, 8):
            value = value + g_in[zz]
        first, last = unfold(value)
        dq_out[...] = jnp.where(yh == 0, last, first).T[0:192]
        part_dq.start()
        dq_ref[...] = (jnp.where(yh == 0, first, last).T[0:192] - d_ref[...]) * SCALE
        loss_ref[...] = loss_out[...]

    sib_dd.wait_recv()
    dd_nat[pl.ds(pl.multiple_of((1 - c) * 64, 64), 64), :] = dd_sib[...]
    dd_ref[...] = (dd_nat[...].T[0:192] - q_ref[...]) * SCALE

    @pl.when(jnp.logical_not(holder))
    def _():
        part_l.wait_recv()
        loss_ref[...] = loss_in[...]
        part_dq.wait_recv()
        dq_ref[...] = (dq_in[...] - d_ref[...]) * SCALE

    sib_dd.wait_send()

    @pl.when(holder)
    def _():
        part_l.wait_send()
        part_dq.wait_send()


def hand_on(*refs):
    for source, target in zip(refs[:4], refs[4:]):
        target[...] = source[...]


def per_device(question_matrix, document_matrix, pool, hard_owner, hard_local):
    vmem = pl.BlockSpec(memory_space=pltpu.VMEM)
    f = lambda *shape: pltpu.VMEM(shape, F32)
    scratch = [
        pltpu.VMEM((16, 128), jnp.int32),
        pltpu.VMEM((4, 16, 128), jnp.int32),
        f(192, 128),
        f(2, 4, 128, 384),
        f(2, 4, 128, 384),
        f(128, 256),
        f(64, 256),
        f(2, 4, 2, 64, 384),
        f(2, 8, 64, 384),
        f(8, 512),
        f(8, 512),
        f(8, 1, 128),
        f(16, 1, 128),
        f(128, 128),
        pltpu.VMEM((3, 256, 2048), BF16),
        f(16, 64, 384),
        f(2, 8, 64, 384),
        f(8, 128, 384),
        f(16, 64, 384),
        f(16, 64, 384),
        f(128, 128),
        f(128, 128),
        f(8, 512),
        f(512, 512),
        f(512, 512),
        f(1, 1024),
        f(16, 1, 1024),
        f(8, 1, 128),
        f(16, 1, 128),
        f(2, 4, 2, 64, 384),
        f(4, 2, 2, 32, 384),
        f(4, 4, 32, 384),
        f(2, 2, 32, 384),
        f(4, 32, 384),
        f(4, 32, 384),
        f(4, 32, 384),
        f(64, 256),
        f(64, 256),
        f(128, 256),
        f(2, 256, 384),
        f(2, 256, 384),
        f(4, 128, 384),
        f(8, 128, 384),
        pltpu.VMEM((512, 1024), BF16),
        pltpu.VMEM((3, 8, 128, 384), BF16),
        pltpu.VMEM((384, 2048), BF16),
        pltpu.VMEM((2048, 2048), BF16),
        f(192, 128),
        f(192, 128),
        f(1, 128),
        f(1, 128),
        f(1, 128),
        f(1, 128),
        f(1, 512),
        pltpu.SemaphoreType.DMA((4, 16)),
        pltpu.SemaphoreType.DMA((4, 16)),
        pltpu.SemaphoreType.DMA((4, 4)),
        pltpu.SemaphoreType.DMA((4, 4)),
        pltpu.SemaphoreType.DMA((4, 4)),
        pltpu.SemaphoreType.DMA((4, 4)),
        pltpu.SemaphoreType.DMA((16,)),
        pltpu.SemaphoreType.DMA((16,)),
        pltpu.SemaphoreType.DMA((8,)),
        pltpu.SemaphoreType.DMA((4,)),
        pltpu.SemaphoreType.DMA((8,)),
        pltpu.SemaphoreType.DMA((4,)),
        pltpu.SemaphoreType.DMA((4,)),
        pltpu.SemaphoreType.DMA((8,)),
        pltpu.SemaphoreType.DMA((2,)),
        pltpu.SemaphoreType.DMA((2,)),
        pltpu.SemaphoreType.DMA((9,)),
        pltpu.SemaphoreType.DMA((9,)),
    ]
    results = pl.pallas_call(
        kernel,
        name="retriever_step",
        out_shape=(
            jax.ShapeDtypeStruct((1, 128), F32),
            jax.ShapeDtypeStruct((192, 128), F32),
            jax.ShapeDtypeStruct((192, 128), F32),
            jax.ShapeDtypeStruct((192, 2048), F32),
        ),
        in_specs=[vmem] * 5,
        out_specs=(vmem,) * 4,
        scratch_shapes=scratch,
        compiler_params=pltpu.CompilerParams(
            collective_id=0, has_side_effects=True, vmem_limit_bytes=60 * 1024 * 1024
        ),
    )(question_matrix.T, document_matrix.T, pool, hard_owner.T, hard_local.T)
    loss, dq, dd, gp = pl.pallas_call(
        hand_on,
        name="results",
        out_shape=tuple(jax.ShapeDtypeStruct(r.shape, r.dtype) for r in results),
        in_specs=[vmem] * 4,
        out_specs=(vmem,) * 4,
    )(*results)
    return loss.reshape(128), dq.T, dd.T, gp


def solution(mesh):
    placed = (P("blk", "dim"), P("blk", "dim"), P("dim", "blk"), P("blk", None), P("blk", None))
    return jax.shard_map(
        per_device,
        mesh=mesh,
        in_specs=placed,
        out_specs=(P("blk"), P("blk", "dim"), P("blk", "dim"), P("dim", "blk")),
        check_vma=False,
    )
```

```python
import jax
import jax.numpy as jnp
from jax import lax
from jax.experimental import pallas as pl
from jax.experimental.pallas import tpu as pltpu
from jax.sharding import PartitionSpec as P

MESH = pl.DeviceIdType.MESH
F32 = jnp.float32
BF16 = jnp.bfloat16
HIGHEST = lax.Precision.HIGHEST
SCALE = 20.0

NT = (((1,), (1,)), ((), ()))
NN = (((1,), (0,)), ((), ()))


def mm(a, b, dims, precision=None):
    return lax.dot_general(a, b, dims, precision=precision, preferred_element_type=F32)


def split3(x):
    high = x.astype(BF16)
    rest = x - high.astype(F32)
    mid = rest.astype(BF16)
    low = (rest - mid.astype(F32)).astype(BF16)
    return high, mid, low


def loop(count, body):
    def step(i, carry):
        body(i)
        return carry

    lax.fori_loop(0, count, step, 0)


def halves(x):
    return x[:, :128], x[:, 128:256], x[:, 256:384]


def low(rows):
    return lax.broadcasted_iota(jnp.int32, (rows, 128), 1) < 64


def turned(x):
    return pltpu.roll(x, 64, 1)


def fold(a, b):
    keep = low(a.shape[0])
    b0, b1 = turned(b[:, :128]), turned(b[:, 128:256])
    return jnp.concatenate(
        [a[:, :128], jnp.where(keep, a[:, 128:256], b0), jnp.where(keep, b0, b1)], axis=1
    )


def unfold(x):
    x0, x1, x2 = halves(x)
    x1t, x2t = turned(x1), turned(x2)
    return (
        jnp.concatenate([x0, x1], axis=1),
        jnp.concatenate([jnp.where(low(x.shape[0]), x1t, x2t), x2t], axis=1),
    )


def regroup(x, y):
    x0, x1, x2 = halves(x)
    y0, y1, y2 = halves(y)
    keep = low(x.shape[0])
    x1t, x2t, y0t, y1t = turned(x1), turned(x2), turned(y0), turned(y1)
    first = jnp.concatenate([x0, jnp.where(keep, x1, y0t), jnp.where(keep, y0t, y1t)], axis=1)
    last = jnp.concatenate([jnp.where(keep, x1t, x2t), jnp.where(keep, x2t, y1), y2], axis=1)
    return first, last


def upright(x):
    return jnp.concatenate([x, jnp.zeros((64, 128), F32)], axis=0).T


REQ, ROWS, QUERY, PROB = range(4)
SIB_D, SIB_Q, SIB_H, _, SIB_DD, SIB_P, PART_Q, PART_DQ, PART_L = range(9)
DOC_1, DOC_2, GRAD_1, GRAD_2 = range(4)


def kernel(
    q_ref, d_ref, pool_ref, owner_ref, local_ref,
    loss_ref, dq_ref, dd_ref, gp_ref,
    idx_mine, idx_all, q_part, q_all, q_re, d_nat, d_sib, d_raw, d_all, lr_all, sid,
    rq_out, rq_in, lt, pool_s,
    p_out, p_in, p_all, f_out, f_in, hs_mine, hs_sib, hq, st, ch, stat_out, stat_in,
    hc_out, hc_in, g3_out, c1x, c1y, cx, cy, c2x, c2y, dd_out, dd_sib, dd_nat, g_sib_out, g_sib_in, g_out, g_in, hots_t, hp, at_s, hots_r,
    dq_out, dq_in, loss_out, loss_in, pos_out, pos_in, lrow,
    plane_s, plane_r, x_s, x_r, y_s, y_r, row_s, row_r, idx_s, idx_r, qs, qr, gs, gr, sg_s, sg_r, one_s, one_r,
):
    blk, dim = lax.axis_index("blk"), lax.axis_index("dim")
    xy, z = blk // 8, blk % 8
    yh, c = dim // 2, dim % 2
    t = z // 2
    holder = (z % 2) == yh
    me_p = xy * 2 + yh
    me_r = z * 2 + c
    x, yl = xy // 2, xy % 2
    y = yh * 2 + yl

    def plane_dev(p):
        return ((p // 2) * 8 + z, (p % 2) * 2 + c)

    def row_dev(r):
        return (xy * 8 + r // 2, yh * 2 + r % 2)

    def x_dev(xx):
        return ((xx * 2 + yl) * 8 + z, dim)

    def y_dev(yy):
        return ((x * 2 + yy % 2) * 8 + z, (yy // 2) * 2 + c)

    def z_dev(zz):
        return (xy * 8 + zz, dim)

    sibling = (blk, yh * 2 + (1 - c))
    partner = (blk, (1 - yh) * 2 + c)

    def remote(src, dst, send, recv, device):
        return pltpu.make_async_remote_copy(
            src_ref=src, dst_ref=dst, send_sem=send, recv_sem=recv,
            device_id=device, device_id_type=MESH,
        )

    barrier = pltpu.get_barrier_semaphore()

    def greet(k):
        pl.semaphore_signal(barrier, inc=1, device_id=plane_dev((me_p + k + 1) % 16), device_id_type=MESH)
        pl.semaphore_signal(barrier, inc=1, device_id=row_dev((me_r + k + 1) % 16), device_id_type=MESH)

    loop(15, greet)
    idx_mine[0:8] = owner_ref[...]
    idx_mine[8:16] = local_ref[...]
    d_nat[...] = upright(d_ref[...])
    for k, part in enumerate(split3(pool_ref[...])):
        pool_s[k, 0:192] = part
        pool_s[k, 192:256] = jnp.zeros((64, 2048), BF16)
    pl.semaphore_wait(barrier, 30)

    def idx_copy(zz):
        return remote(idx_mine, idx_all.at[t], idx_s.at[zz], idx_r.at[t], z_dev(zz))

    def q_copy(zz):
        return remote(q_all.at[c, t], q_all.at[c, t], qs.at[zz], qr.at[t], z_dev(zz))

    sib_d = remote(
        d_nat.at[pl.ds((1 - c) * 64, 64)], d_sib, one_s.at[SIB_D], one_r.at[SIB_D], sibling
    )
    part_q = remote(q_ref, q_part, one_s.at[PART_Q], one_r.at[PART_Q], partner)

    @pl.when(holder)
    def _():
        loop(7, lambda k: idx_copy((z + k + 1) % 8).start())
        idx_all[t] = idx_mine[...]

    sib_d.start()

    @pl.when(jnp.logical_not(holder))
    def _():
        part_q.start()

    sib_d.wait_recv()
    own_d = d_nat[pl.ds(pl.multiple_of(c * 64, 64), 64), :]
    d_raw[yh, x, yl] = fold(
        jnp.where(c == 0, own_d, d_sib[...]), jnp.where(c == 0, d_sib[...], own_d)
    )

    def doc_x1(xx, slot):
        piece = d_raw.at[yh, slot, yl, pl.ds(0, 32)]
        return remote(piece, piece, x_s.at[DOC_1, xx], x_r.at[DOC_1, slot], x_dev(xx))

    def doc_y1(yy, slot):
        piece = d_raw.at[slot // 2, x, slot % 2, pl.ds(32, 32)]
        return remote(piece, piece, y_s.at[DOC_1, yy], y_r.at[DOC_1, slot], y_dev(yy))

    def doc_y2(yy, slot):
        piece = d_raw.at[slot // 2, :, slot % 2, pl.ds(0, 32)]
        return remote(piece, piece, y_s.at[DOC_2, yy], y_r.at[DOC_2, slot], y_dev(yy))

    def doc_x2(xx, slot):
        piece = d_raw.at[:, slot, :, pl.ds(32, 32)]
        return remote(piece, piece, x_s.at[DOC_2, xx], x_r.at[DOC_2, slot], x_dev(xx))

    def doc_first(k):
        doc_x1((x + k + 1) % 4, x).start()
        doc_y1((y + k + 1) % 4, y).start()

    loop(3, doc_first)

    def idx_wait(tt):
        @pl.when(2 * tt + yh != z)
        def _():
            remote(idx_mine, idx_all.at[tt], idx_s.at[0], idx_r.at[tt], partner).wait_recv()

    loop(4, idx_wait)
    sub8 = lax.broadcasted_iota(jnp.int32, (8, 128), 0)
    upper = jnp.where(
        lax.broadcasted_iota(jnp.int32, (128, 128), 0) < lax.broadcasted_iota(jnp.int32, (128, 128), 1),
        1.0, 0.0,
    ).astype(BF16)
    for tt in range(4):
        owner = idx_all[tt, 0:8]
        local = idx_all[tt, 8:16] + 1
        table = jnp.zeros((8, 128), jnp.int32)
        for a in range(8):
            row = jnp.sum(jnp.where(owner == a * 8 + z, local, 0), axis=0, keepdims=True)
            table = jnp.where(sub8 == a, row, table)
        marks = jnp.where(table > 0, 1.0, 0.0)
        rank = mm(marks.astype(BF16), upper, NN)
        lr_all[:, tt * 128 : (tt + 1) * 128] = table.astype(F32)
        sid[:, tt * 128 : (tt + 1) * 128] = jnp.where(table > 0, rank + float(tt * 32), -1.0)

    sub512 = lax.broadcasted_iota(jnp.int32, (128, 512), 0).astype(F32)
    lane128 = lax.broadcasted_iota(jnp.int32, (128, 128), 1)

    def hot(a):
        return sub512 == sid[pl.ds(a, 1), :]

    def columns(rows):
        def step(a, table):
            col = jnp.sum(jnp.where(hot(a), rows[pl.ds(a, 1), :], 0.0), axis=1, keepdims=True)
            return jnp.where(lane128 == a, col, table)

        return lax.fori_loop(0, 8, step, jnp.zeros((128, 128), F32))

    wanted = columns(lr_all).T
    for a in range(8):
        rq_out[a] = wanted[a : a + 1, :]
    rq_in[me_p] = rq_out[xy]

    def req_copy(p, slot):
        return remote(
            rq_out.at[p // 2], rq_in.at[slot], plane_s.at[REQ, p], plane_r.at[REQ, slot], plane_dev(p)
        )

    loop(15, lambda k: req_copy((me_p + k + 1) % 16, me_p).start())

    @pl.when(holder)
    def _():
        remote(q_ref, q_part, one_s.at[PART_Q], one_r.at[PART_Q], partner).wait_recv()
        own, other = upright(q_ref[...]), upright(q_part[...])
        q_all[c, t] = fold(jnp.where(yh == 0, own, other), jnp.where(yh == 0, other, own))
        loop(7, lambda k: q_copy((z + k + 1) % 8).start())

    def doc_second(k):
        xx, yy = (x + k + 1) % 4, (y + k + 1) % 4
        doc_x1(xx, xx).wait_recv()
        doc_y1(yy, yy).wait_recv()

    loop(3, doc_second)

    def doc_on(k):
        doc_y2((y + k + 1) % 4, y).start()
        doc_x2((x + k + 1) % 4, x).start()

    loop(3, doc_on)

    def req_wait(k):
        p = (me_p + k + 1) % 16
        req_copy(p, p).wait_recv()

    loop(15, req_wait)
    named = jnp.concatenate([rq_in[i] for i in range(16)] + [jnp.zeros((112, 128), F32)], axis=0)
    lt[...] = named.T
    lane2048 = lax.broadcasted_iota(jnp.int32, (128, 2048), 1).astype(F32) + 1.0

    def rows_copy(p, slot):
        return remote(
            p_out.at[p], p_in.at[slot % 2, slot // 2],
            plane_s.at[ROWS, p], plane_r.at[ROWS, slot], plane_dev(p),
        )

    def fetch(g):
        hots = []
        for i in range(4):
            col = jnp.sum(jnp.where(lane128 == g * 4 + i, lt[...], 0.0), axis=1, keepdims=True)
            hots.append(jnp.where(col == lane2048, 1.0, 0.0).astype(BF16))
        hots = jnp.concatenate(hots, axis=0)
        hots_r[pl.ds(pl.multiple_of(g * 512, 512), 512), :] = hots
        got = mm(hots, pool_s[0], NT) + mm(hots, pool_s[1], NT) + mm(hots, pool_s[2], NT)
        for i in range(4):
            p = g * 4 + i
            p_out[p] = fold(got[i * 128 : i * 128 + 64], got[i * 128 + 64 : i * 128 + 128])

            @pl.when(p != me_p)
            def _():
                rows_copy(p, me_p).start()

    loop(4, fetch)
    p_in[yh, xy] = p_out[me_p]

    def q_wait(tt):
        @pl.when(2 * tt + yh != z)
        def _():
            remote(q_all.at[c, tt], q_all.at[c, tt], qs.at[0], qr.at[tt], partner).wait_recv()

    loop(4, q_wait)
    sib_q = remote(q_all.at[c], q_all.at[c], one_s.at[SIB_Q], one_r.at[SIB_Q], sibling)
    sib_q.start()

    queries = split3(q_all[c].reshape(512, 384))

    def pick(g):
        hots = jnp.concatenate(
            [jnp.where(hot(g * 4 + i), 1.0, 0.0).astype(BF16) for i in range(4)], axis=0
        )
        got = mm(hots, queries[0], NN) + mm(hots, queries[1], NN) + mm(hots, queries[2], NN)
        for i in range(4):
            first, last = regroup(got[i * 128 : i * 128 + 64], got[i * 128 + 64 : i * 128 + 128])
            f_out[(g * 4 + i) * 2] = first
            f_out[(g * 4 + i) * 2 + 1] = last

    loop(2, pick)
    f_in[me_p] = f_out[me_p]

    remote(q_all.at[c], q_all.at[1 - c], one_s.at[SIB_Q], one_r.at[SIB_Q], sibling).wait_recv()

    def rearrange_q(tt):
        first, last = regroup(q_all[0, tt], q_all[1, tt])
        q_re[0, tt] = first
        q_re[1, tt] = last

    loop(4, rearrange_q)

    def doc_wait(k):
        xx, yy = (x + k + 1) % 4, (y + k + 1) % 4
        doc_y2(yy, yy).wait_recv()
        doc_x2(xx, xx).wait_recv()

    loop(3, doc_wait)

    def score(j):
        total = None
        for part in range(2):
            docs = d_raw[part, pl.ds(j * 2, 2)].reshape(256, 384)
            value = mm(docs, q_re[part].reshape(512, 384), NT, HIGHEST)
            total = value if total is None else total + value
        st[pl.ds(pl.multiple_of(j * 256, 256), 256), :] = total * SCALE

    loop(2, score)

    def top(j, best):
        rows = st[pl.ds(pl.multiple_of(j * 64, 64), 64), :].reshape(8, 8, 512)
        return jnp.maximum(best, jnp.max(rows, axis=0))

    best = lax.fori_loop(0, 8, top, jnp.full((8, 512), -jnp.inf, F32))
    best = jnp.max(best, axis=0, keepdims=True)

    def rows_wait(k):
        p = (me_p + k + 1) % 16
        rows_copy(p, p).wait_recv()

    loop(15, rows_wait)
    low64 = low(64)

    def hard_part(a, table):
        terms = p_in[0, a] * f_out[a * 2] + p_in[1, a] * f_out[a * 2 + 1]
        t0, t1, t2 = halves(terms)
        first = jnp.sum(t0 + jnp.where(low64, t1, 0.0), axis=1, keepdims=True)
        last = jnp.sum(t2 + jnp.where(low64, 0.0, t1), axis=1, keepdims=True)
        return jnp.where(lane128 == a, jnp.concatenate([first, last], axis=0), table)

    hs_mine[...] = lax.fori_loop(0, 8, hard_part, jnp.zeros((128, 128), F32))
    sib_h = remote(hs_mine, hs_sib, one_s.at[SIB_H], one_r.at[SIB_H], sibling)
    sib_h.start()

    def query_copy(p, slot):
        return remote(
            f_out.at[p], f_in.at[slot], plane_s.at[QUERY, p], plane_r.at[QUERY, slot], plane_dev(p)
        )

    loop(15, lambda k: query_copy((me_p + k + 1) % 16, me_p).start())

    sib_h.wait_recv()
    hard = (hs_mine[...] + hs_sib[...]) * SCALE
    for a in range(8):
        row = jnp.sum(jnp.where(hot(a), hard[:, a : a + 1], 0.0), axis=0, keepdims=True)
        hq[a : a + 1, :] = jnp.where(sid[a : a + 1, :] >= 0.0, row, -jnp.inf)
    peak = jnp.maximum(best, jnp.max(hq[...], axis=0, keepdims=True))

    def add(j, total):
        rows = jnp.exp(st[pl.ds(pl.multiple_of(j * 64, 64), 64), :] - peak)
        return total + jnp.sum(rows.reshape(8, 8, 512), axis=0)

    total = lax.fori_loop(0, 8, add, jnp.zeros((8, 512), F32))
    total = total + jnp.exp(hq[...] - peak) * jnp.where(c == 0, 1.0, 0.0)
    total = jnp.sum(total, axis=0, keepdims=True)
    square = st[pl.ds(pl.multiple_of(xy * 64, 64), 64), pl.ds(pl.multiple_of(t * 128, 128), 128)]
    on_diagonal = lax.broadcasted_iota(jnp.int32, (64, 128), 1) == (
        lax.broadcasted_iota(jnp.int32, (64, 128), 0) + c * 64
    )
    positive = jnp.sum(jnp.where(on_diagonal, square, 0.0), axis=0, keepdims=True)
    pos_out[...] = positive
    sib_p = remote(pos_out, pos_in, one_s.at[SIB_P], one_r.at[SIB_P], sibling)
    stat_out[:, 0:512] = peak
    stat_out[:, 512:1024] = total
    stat_in[me_r] = stat_out[...]

    def stat_copy(r, slot):
        return remote(stat_out, stat_in.at[slot], row_s.at[r], row_r.at[slot], row_dev(r))

    loop(15, lambda k: stat_copy((me_r + k + 1) % 16, me_r).start())
    sib_p.start()

    def rearrange_d(k):
        first, last = regroup(d_raw[0, k // 2, k % 2], d_raw[1, k // 2, k % 2])
        d_all[0, k] = first
        d_all[1, k] = last
        first, last = regroup(p_in[0, k], p_in[1, k])
        p_all[k, 0:64] = first
        p_all[k, 64:128] = last

    loop(8, rearrange_d)
    sid_t = jnp.concatenate([sid[...], jnp.zeros((120, 512), F32)], axis=0).T
    lane512 = lax.broadcasted_iota(jnp.int32, (512, 128), 1).astype(F32)
    for a in range(8):
        hots_t[:, a * 128 : (a + 1) * 128] = jnp.where(
            sid_t[:, a : a + 1] == lane512, 1.0, 0.0
        ).astype(BF16)

    def stat_wait(k):
        r = (me_r + k + 1) % 16
        stat_copy(r, r).wait_recv()

    loop(15, stat_wait)
    peaks = jnp.concatenate([stat_in[r, :, 0:512] for r in range(16)], axis=0)
    totals = jnp.concatenate([stat_in[r, :, 512:1024] for r in range(16)], axis=0)
    peak = jnp.max(peaks, axis=0, keepdims=True)
    total = jnp.sum(totals * jnp.exp(peaks - peak), axis=0, keepdims=True)
    log_total = peak + jnp.log(total)
    lrow[...] = log_total

    hq[...] = jnp.exp(hq[...] - log_total)

    shares = columns(hq)
    for a in range(8):
        for k, part in enumerate(split3(p_all[a] * shares[:, a : a + 1])):
            hp[k, a] = part

    def chance(j):
        rows = pl.ds(pl.multiple_of(j * 128, 128), 128)
        value = jnp.exp(st[rows, :] - log_total)
        st[rows, :] = value
        ch[:, rows] = value.T

    loop(4, chance)

    def sib_g(h):
        return remote(g_sib_out.at[h], g_sib_in.at[h], sg_s.at[h], sg_r.at[h], sibling)

    def grad_copy(tt, slot):
        return remote(g_out.at[tt], g_in.at[slot], gs.at[tt], gr.at[slot], z_dev(2 * tt + yh))

    def grad_half(h):
        rows = pl.ds(pl.multiple_of(h * 256, 256), 256)
        g_sib_out[h] = mm(ch[rows, :], d_all[1 - c].reshape(512, 384), NN, HIGHEST)
        sib_g(h).start()
        g_own = mm(ch[rows, :], d_all[c].reshape(512, 384), NN, HIGHEST)
        for k in range(3):
            g_own = g_own + mm(hots_t[rows, :], hp[k].reshape(1024, 384), NN)
        sib_g(h).wait_recv()
        g_out[pl.ds(h * 2, 2)] = (g_own + g_sib_in[h]).reshape(2, 128, 384)
        for i in range(2):
            tt = h * 2 + i

            @pl.when(2 * tt + yh != z)
            def _():
                grad_copy(tt, z).start()

    loop(2, grad_half)

    @pl.when(holder)
    def _():
        g_in[z] = g_out[t]

    chances = shares.T
    for a in range(8):
        hc_out[a] = chances[a : a + 1, :]
    hc_in[me_p] = hc_out[xy]

    def prob_copy(p, slot):
        return remote(
            hc_out.at[p // 2], hc_in.at[slot], plane_s.at[PROB, p], plane_r.at[PROB, slot], plane_dev(p)
        )

    loop(15, lambda k: prob_copy((me_p + k + 1) % 16, me_p).start())

    def doc_grad(part):
        value = mm(st[...], q_re[part].reshape(512, 384), NN, HIGHEST)
        g3_out[part] = value.reshape(4, 2, 64, 384)

    loop(2, doc_grad)

    def grad_y1(yy, slot):
        return remote(
            g3_out.at[yy // 2, :, yy % 2, pl.ds(0, 32)], c1y.at[slot],
            y_s.at[GRAD_1, yy], y_r.at[GRAD_1, slot], y_dev(yy),
        )

    def grad_x1(xx, slot):
        return remote(
            g3_out.at[:, xx, :, pl.ds(32, 32)], c1x.at[slot],
            x_s.at[GRAD_1, xx], x_r.at[GRAD_1, slot], x_dev(xx),
        )

    def grad_x2(xx, slot):
        return remote(cy.at[xx], c2x.at[slot], x_s.at[GRAD_2, xx], x_r.at[GRAD_2, slot], x_dev(xx))

    def grad_y2(yy, slot):
        return remote(
            cx.at[yy // 2, yy % 2], c2y.at[slot], y_s.at[GRAD_2, yy], y_r.at[GRAD_2, slot], y_dev(yy)
        )

    def grad_first(k):
        grad_y1((y + k + 1) % 4, y).start()
        grad_x1((x + k + 1) % 4, x).start()

    loop(3, grad_first)
    def query_wait(k):
        p = (me_p + k + 1) % 16
        query_copy(p, p).wait_recv()
        prob_copy(p, p).wait_recv()

    loop(15, query_wait)
    chances = jnp.concatenate([hc_in[i] for i in range(16)] + [jnp.zeros((112, 128), F32)], axis=0).T

    def turn(i):
        col = jnp.sum(jnp.where(lane128 == i, chances, 0.0), axis=1, keepdims=True)
        rows = jnp.concatenate(unfold(f_in[i]), axis=0) * (col * SCALE)
        terms = split3(rows.T[0:192])
        for k in range(2):
            at_s[k * 192 : k * 192 + 192, pl.ds(pl.multiple_of(i * 128, 128), 128)] = terms[k]

    loop(16, turn)

    def pool_grad(n):
        columns_n = pl.ds(pl.multiple_of(n * 256, 256), 256)
        value = mm(at_s[...], hots_r[:, columns_n], NN)
        gp_ref[:, columns_n] = value[0:192] + value[192:384]

    loop(4, pool_grad)

    def grad_second(k):
        xx, yy = (x + k + 1) % 4, (y + k + 1) % 4
        grad_y1(yy, yy).wait_recv()
        grad_x1(xx, xx).wait_recv()

    loop(3, grad_second)

    def sum_y(xx):
        cy[xx] = (g3_out[yh, xx, yl, 0:32] + c1y[(y + 1) % 4, xx]) + (
            c1y[(y + 2) % 4, xx] + c1y[(y + 3) % 4, xx]
        )

    loop(4, sum_y)

    def sum_x(k):
        a, b = k // 2, k % 2
        cx[a, b] = (g3_out[a, x, b, 32:64] + c1x[(x + 1) % 4, a, b]) + (
            c1x[(x + 2) % 4, a, b] + c1x[(x + 3) % 4, a, b]
        )

    loop(4, sum_x)

    def grad_on(k):
        grad_x2((x + k + 1) % 4, x).start()
        grad_y2((y + k + 1) % 4, y).start()

    loop(3, grad_on)
    loop(4, lambda n: pool_grad(n + 4))

    def grad_wait(k):
        xx, yy = (x + k + 1) % 4, (y + k + 1) % 4
        grad_x2(xx, xx).wait_recv()
        grad_y2(yy, yy).wait_recv()

    loop(3, grad_wait)
    upper_rows = (cy[x] + c2x[(x + 1) % 4]) + (c2x[(x + 2) % 4] + c2x[(x + 3) % 4])
    lower_rows = (cx[yh, yl] + c2y[(y + 1) % 4]) + (c2y[(y + 2) % 4] + c2y[(y + 3) % 4])
    value = jnp.concatenate([upper_rows, lower_rows], axis=0)
    first, last = unfold(value)
    dd_out[...] = jnp.where(c == 0, last, first)
    sib_dd = remote(dd_out, dd_sib, one_s.at[SIB_DD], one_r.at[SIB_DD], sibling)
    sib_dd.start()
    dd_nat[pl.ds(pl.multiple_of(c * 64, 64), 64), :] = jnp.where(c == 0, first, last)

    sib_d.wait_send()
    sib_q.wait_send()
    sib_h.wait_send()
    loop(2, lambda h: sib_g(h).wait_send())

    def sent(k):
        p = (me_p + k + 1) % 16
        for copy in (req_copy, rows_copy, query_copy, prob_copy):
            copy(p, me_p).wait_send()
        stat_copy((me_r + k + 1) % 16, me_r).wait_send()

    loop(15, sent)

    def sent4(k):
        for copy in (doc_x1, doc_x2, grad_x1, grad_x2):
            copy((x + k + 1) % 4, x).wait_send()
        for copy in (doc_y1, doc_y2, grad_y1, grad_y2):
            copy((y + k + 1) % 4, y).wait_send()

    loop(3, sent4)
    sib_p.wait_send()

    def grad_sent(tt):
        @pl.when(2 * tt + yh != z)
        def _():
            grad_copy(tt, z).wait_send()

    loop(4, grad_sent)

    @pl.when(holder)
    def _():
        def z_sent(k):
            zz = (z + k + 1) % 8
            idx_copy(zz).wait_send()
            q_copy(zz).wait_send()

        loop(7, z_sent)

    @pl.when(jnp.logical_not(holder))
    def _():
        part_q.wait_send()

    part_dq = remote(dq_out, dq_in, one_s.at[PART_DQ], one_r.at[PART_DQ], partner)
    part_l = remote(loss_out, loss_in, one_s.at[PART_L], one_r.at[PART_L], partner)
    sib_p.wait_recv()

    @pl.when(holder)
    def _():
        loss_out[...] = lrow[:, pl.ds(pl.multiple_of(t * 128, 128), 128)] - (pos_out[...] + pos_in[...])
        part_l.start()

        def wait(k):
            zz = (z + k + 1) % 8
            grad_copy(t, zz).wait_recv()

        loop(7, wait)
        value = g_in[0]
        for zz in range(1, 8):
            value = value + g_in[zz]
        first, last = unfold(value)
        dq_out[...] = jnp.where(yh == 0, last, first).T[0:192]
        part_dq.start()
        dq_ref[...] = (jnp.where(yh == 0, first, last).T[0:192] - d_ref[...]) * SCALE
        loss_ref[...] = loss_out[...]

    sib_dd.wait_recv()
    dd_nat[pl.ds(pl.multiple_of((1 - c) * 64, 64), 64), :] = dd_sib[...]
    dd_ref[...] = (dd_nat[...].T[0:192] - q_ref[...]) * SCALE

    @pl.when(jnp.logical_not(holder))
    def _():
        part_l.wait_recv()
        loss_ref[...] = loss_in[...]
        part_dq.wait_recv()
        dq_ref[...] = (dq_in[...] - d_ref[...]) * SCALE

    sib_dd.wait_send()

    @pl.when(holder)
    def _():
        part_l.wait_send()
        part_dq.wait_send()


def hand_on(*refs):
    for source, target in zip(refs[:4], refs[4:]):
        target[...] = source[...]


def per_device(question_matrix, document_matrix, pool, hard_owner, hard_local):
    vmem = pl.BlockSpec(memory_space=pltpu.VMEM)
    f = lambda *shape: pltpu.VMEM(shape, F32)
    scratch = [
        pltpu.VMEM((16, 128), jnp.int32),
        pltpu.VMEM((4, 16, 128), jnp.int32),
        f(192, 128),
        f(2, 4, 128, 384),
        f(2, 4, 128, 384),
        f(128, 256),
        f(64, 256),
        f(2, 4, 2, 64, 384),
        f(2, 8, 64, 384),
        f(8, 512),
        f(8, 512),
        f(8, 1, 128),
        f(16, 1, 128),
        f(128, 128),
        pltpu.VMEM((3, 256, 2048), BF16),
        f(16, 64, 384),
        f(2, 8, 64, 384),
        f(8, 128, 384),
        f(16, 64, 384),
        f(16, 64, 384),
        f(128, 128),
        f(128, 128),
        f(8, 512),
        f(512, 512),
        f(512, 512),
        f(1, 1024),
        f(16, 1, 1024),
        f(8, 1, 128),
        f(16, 1, 128),
        f(2, 4, 2, 64, 384),
        f(4, 2, 2, 32, 384),
        f(4, 4, 32, 384),
        f(2, 2, 32, 384),
        f(4, 32, 384),
        f(4, 32, 384),
        f(4, 32, 384),
        f(64, 256),
        f(64, 256),
        f(128, 256),
        f(2, 256, 384),
        f(2, 256, 384),
        f(4, 128, 384),
        f(8, 128, 384),
        pltpu.VMEM((512, 1024), BF16),
        pltpu.VMEM((3, 8, 128, 384), BF16),
        pltpu.VMEM((384, 2048), BF16),
        pltpu.VMEM((2048, 2048), BF16),
        f(192, 128),
        f(192, 128),
        f(1, 128),
        f(1, 128),
        f(1, 128),
        f(1, 128),
        f(1, 512),
        pltpu.SemaphoreType.DMA((4, 16)),
        pltpu.SemaphoreType.DMA((4, 16)),
        pltpu.SemaphoreType.DMA((4, 4)),
        pltpu.SemaphoreType.DMA((4, 4)),
        pltpu.SemaphoreType.DMA((4, 4)),
        pltpu.SemaphoreType.DMA((4, 4)),
        pltpu.SemaphoreType.DMA((16,)),
        pltpu.SemaphoreType.DMA((16,)),
        pltpu.SemaphoreType.DMA((8,)),
        pltpu.SemaphoreType.DMA((4,)),
        pltpu.SemaphoreType.DMA((8,)),
        pltpu.SemaphoreType.DMA((4,)),
        pltpu.SemaphoreType.DMA((4,)),
        pltpu.SemaphoreType.DMA((8,)),
        pltpu.SemaphoreType.DMA((2,)),
        pltpu.SemaphoreType.DMA((2,)),
        pltpu.SemaphoreType.DMA((9,)),
        pltpu.SemaphoreType.DMA((9,)),
    ]
    results = pl.pallas_call(
        kernel,
        name="retriever_step",
        out_shape=(
            jax.ShapeDtypeStruct((1, 128), F32),
            jax.ShapeDtypeStruct((192, 128), F32),
            jax.ShapeDtypeStruct((192, 128), F32),
            jax.ShapeDtypeStruct((192, 2048), F32),
        ),
        in_specs=[vmem] * 5,
        out_specs=(vmem,) * 4,
        scratch_shapes=scratch,
        compiler_params=pltpu.CompilerParams(
            collective_id=0, has_side_effects=True, vmem_limit_bytes=60 * 1024 * 1024
        ),
    )(question_matrix.T, document_matrix.T, pool, hard_owner.T, hard_local.T)
    loss, dq, dd, gp = pl.pallas_call(
        hand_on,
        name="results",
        out_shape=tuple(jax.ShapeDtypeStruct(r.shape, r.dtype) for r in results),
        in_specs=[vmem] * 4,
        out_specs=(vmem,) * 4,
    )(*results)
    return loss.reshape(128), dq.T, dd.T, gp


def solution(mesh):
    placed = (P("blk", "dim"), P("blk", "dim"), P("dim", "blk"), P("blk", None), P("blk", None))
    return jax.shard_map(
        per_device,
        mesh=mesh,
        in_specs=placed,
        out_specs=(P("blk"), P("blk", "dim"), P("blk", "dim"), P("dim", "blk")),
        check_vma=False,
    )
```

```python
import jax
import jax.numpy as jnp
from jax import lax
from jax.experimental import pallas as pl
from jax.experimental.pallas import tpu as pltpu
from jax.sharding import PartitionSpec as P

MESH = pl.DeviceIdType.MESH
F32 = jnp.float32
BF16 = jnp.bfloat16
HIGHEST = lax.Precision.HIGHEST
SCALE = 20.0

NT = (((1,), (1,)), ((), ()))
NN = (((1,), (0,)), ((), ()))


def mm(a, b, dims, precision=None):
    return lax.dot_general(a, b, dims, precision=precision, preferred_element_type=F32)


def split3(x):
    high = x.astype(BF16)
    rest = x - high.astype(F32)
    mid = rest.astype(BF16)
    low = (rest - mid.astype(F32)).astype(BF16)
    return high, mid, low


def loop(count, body):
    def step(i, carry):
        body(i)
        return carry

    lax.fori_loop(0, count, step, 0)


def halves(x):
    return x[:, :128], x[:, 128:256], x[:, 256:384]


def low(rows):
    return lax.broadcasted_iota(jnp.int32, (rows, 128), 1) < 64


def turned(x):
    return pltpu.roll(x, 64, 1)


def fold(a, b):
    keep = low(a.shape[0])
    b0, b1 = turned(b[:, :128]), turned(b[:, 128:256])
    return jnp.concatenate(
        [a[:, :128], jnp.where(keep, a[:, 128:256], b0), jnp.where(keep, b0, b1)], axis=1
    )


def unfold(x):
    x0, x1, x2 = halves(x)
    x1t, x2t = turned(x1), turned(x2)
    return (
        jnp.concatenate([x0, x1], axis=1),
        jnp.concatenate([jnp.where(low(x.shape[0]), x1t, x2t), x2t], axis=1),
    )


def regroup(x, y):
    x0, x1, x2 = halves(x)
    y0, y1, y2 = halves(y)
    keep = low(x.shape[0])
    x1t, x2t, y0t, y1t = turned(x1), turned(x2), turned(y0), turned(y1)
    first = jnp.concatenate([x0, jnp.where(keep, x1, y0t), jnp.where(keep, y0t, y1t)], axis=1)
    last = jnp.concatenate([jnp.where(keep, x1t, x2t), jnp.where(keep, x2t, y1), y2], axis=1)
    return first, last


def upright(x):
    return jnp.concatenate([x, jnp.zeros((64, 128), F32)], axis=0).T


REQ, ROWS, QUERY, PROB = range(4)
SIB_D, SIB_Q, SIB_H, _, SIB_DD, SIB_P, PART_Q, PART_DQ, PART_L = range(9)
DOC_1, DOC_2, GRAD_1, GRAD_2 = range(4)


def kernel(
    q_ref, d_ref, pool_ref, owner_ref, local_ref,
    loss_ref, dq_ref, dd_ref, gp_ref,
    idx_mine, idx_all, q_part, q_all, q_re, d_nat, d_sib, d_raw, d_all, lr_all, sid,
    rq_out, rq_in, lt, pool_s,
    p_out, p_in, p_all, f_out, f_in, hs_mine, hs_sib, hq, st, ch, stat_out, stat_in,
    hc_out, hc_in, g3_out, c1x, c1y, cx, cy, c2x, c2y, dd_out, dd_sib, dd_nat, g_sib_out, g_sib_in, g_out, g_in, hots_t, hp, at_s, hots_r,
    dq_out, dq_in, loss_out, loss_in, pos_out, pos_in, lrow,
    plane_s, plane_r, x_s, x_r, y_s, y_r, row_s, row_r, idx_s, idx_r, qs, qr, gs, gr, sg_s, sg_r, one_s, one_r,
):
    blk, dim = lax.axis_index("blk"), lax.axis_index("dim")
    xy, z = blk // 8, blk % 8
    yh, c = dim // 2, dim % 2
    t = z // 2
    holder = (z % 2) == yh
    me_p = xy * 2 + yh
    me_r = z * 2 + c
    x, yl = xy // 2, xy % 2
    y = yh * 2 + yl

    def plane_dev(p):
        return ((p // 2) * 8 + z, (p % 2) * 2 + c)

    def row_dev(r):
        return (xy * 8 + r // 2, yh * 2 + r % 2)

    def x_dev(xx):
        return ((xx * 2 + yl) * 8 + z, dim)

    def y_dev(yy):
        return ((x * 2 + yy % 2) * 8 + z, (yy // 2) * 2 + c)

    def z_dev(zz):
        return (xy * 8 + zz, dim)

    sibling = (blk, yh * 2 + (1 - c))
    partner = (blk, (1 - yh) * 2 + c)

    def remote(src, dst, send, recv, device):
        return pltpu.make_async_remote_copy(
            src_ref=src, dst_ref=dst, send_sem=send, recv_sem=recv,
            device_id=device, device_id_type=MESH,
        )

    barrier = pltpu.get_barrier_semaphore()

    def greet(k):
        pl.semaphore_signal(barrier, inc=1, device_id=plane_dev((me_p + k + 1) % 16), device_id_type=MESH)
        pl.semaphore_signal(barrier, inc=1, device_id=row_dev((me_r + k + 1) % 16), device_id_type=MESH)

    loop(15, greet)
    idx_mine[0:8] = owner_ref[...]
    idx_mine[8:16] = local_ref[...]
    d_nat[...] = upright(d_ref[...])
    for k, part in enumerate(split3(pool_ref[...])):
        pool_s[k, 0:192] = part
        pool_s[k, 192:256] = jnp.zeros((64, 2048), BF16)
    pl.semaphore_wait(barrier, 30)

    def idx_copy(zz):
        return remote(idx_mine, idx_all.at[t], idx_s.at[zz], idx_r.at[t], z_dev(zz))

    def q_copy(zz):
        return remote(q_all.at[c, t], q_all.at[c, t], qs.at[zz], qr.at[t], z_dev(zz))

    sib_d = remote(
        d_nat.at[pl.ds((1 - c) * 64, 64)], d_sib, one_s.at[SIB_D], one_r.at[SIB_D], sibling
    )
    part_q = remote(q_ref, q_part, one_s.at[PART_Q], one_r.at[PART_Q], partner)

    @pl.when(holder)
    def _():
        loop(7, lambda k: idx_copy((z + k + 1) % 8).start())
        idx_all[t] = idx_mine[...]

    sib_d.start()

    @pl.when(jnp.logical_not(holder))
    def _():
        part_q.start()

    sib_d.wait_recv()
    own_d = d_nat[pl.ds(pl.multiple_of(c * 64, 64), 64), :]
    d_raw[yh, x, yl] = fold(
        jnp.where(c == 0, own_d, d_sib[...]), jnp.where(c == 0, d_sib[...], own_d)
    )

    def doc_x1(xx, slot):
        piece = d_raw.at[yh, slot, yl, pl.ds(0, 32)]
        return remote(piece, piece, x_s.at[DOC_1, xx], x_r.at[DOC_1, slot], x_dev(xx))

    def doc_y1(yy, slot):
        piece = d_raw.at[slot // 2, x, slot % 2, pl.ds(32, 32)]
        return remote(piece, piece, y_s.at[DOC_1, yy], y_r.at[DOC_1, slot], y_dev(yy))

    def doc_y2(yy, slot):
        piece = d_raw.at[slot // 2, :, slot % 2, pl.ds(0, 32)]
        return remote(piece, piece, y_s.at[DOC_2, yy], y_r.at[DOC_2, slot], y_dev(yy))

    def doc_x2(xx, slot):
        piece = d_raw.at[:, slot, :, pl.ds(32, 32)]
        return remote(piece, piece, x_s.at[DOC_2, xx], x_r.at[DOC_2, slot], x_dev(xx))

    def doc_first(k):
        doc_x1((x + k + 1) % 4, x).start()
        doc_y1((y + k + 1) % 4, y).start()

    loop(3, doc_first)

    def idx_wait(tt):
        @pl.when(2 * tt + yh != z)
        def _():
            remote(idx_mine, idx_all.at[tt], idx_s.at[0], idx_r.at[tt], partner).wait_recv()

    loop(4, idx_wait)
    sub8 = lax.broadcasted_iota(jnp.int32, (8, 128), 0)
    upper = jnp.where(
        lax.broadcasted_iota(jnp.int32, (128, 128), 0) < lax.broadcasted_iota(jnp.int32, (128, 128), 1),
        1.0, 0.0,
    ).astype(BF16)
    for tt in range(4):
        owner = idx_all[tt, 0:8]
        local = idx_all[tt, 8:16] + 1
        table = jnp.zeros((8, 128), jnp.int32)
        for a in range(8):
            row = jnp.sum(jnp.where(owner == a * 8 + z, local, 0), axis=0, keepdims=True)
            table = jnp.where(sub8 == a, row, table)
        marks = jnp.where(table > 0, 1.0, 0.0)
        rank = mm(marks.astype(BF16), upper, NN)
        lr_all[:, tt * 128 : (tt + 1) * 128] = table.astype(F32)
        sid[:, tt * 128 : (tt + 1) * 128] = jnp.where(table > 0, rank + float(tt * 32), -1.0)

    sub512 = lax.broadcasted_iota(jnp.int32, (128, 512), 0).astype(F32)
    lane128 = lax.broadcasted_iota(jnp.int32, (128, 128), 1)

    def hot(a):
        return sub512 == sid[pl.ds(a, 1), :]

    def columns(rows):
        def step(a, table):
            col = jnp.sum(jnp.where(hot(a), rows[pl.ds(a, 1), :], 0.0), axis=1, keepdims=True)
            return jnp.where(lane128 == a, col, table)

        return lax.fori_loop(0, 8, step, jnp.zeros((128, 128), F32))

    wanted = columns(lr_all).T
    for a in range(8):
        rq_out[a] = wanted[a : a + 1, :]
    rq_in[me_p] = rq_out[xy]

    def req_copy(p, slot):
        return remote(
            rq_out.at[p // 2], rq_in.at[slot], plane_s.at[REQ, p], plane_r.at[REQ, slot], plane_dev(p)
        )

    loop(15, lambda k: req_copy((me_p + k + 1) % 16, me_p).start())

    @pl.when(holder)
    def _():
        remote(q_ref, q_part, one_s.at[PART_Q], one_r.at[PART_Q], partner).wait_recv()
        own, other = upright(q_ref[...]), upright(q_part[...])
        q_all[c, t] = fold(jnp.where(yh == 0, own, other), jnp.where(yh == 0, other, own))
        loop(7, lambda k: q_copy((z + k + 1) % 8).start())

    def doc_second(k):
        xx, yy = (x + k + 1) % 4, (y + k + 1) % 4
        doc_x1(xx, xx).wait_recv()
        doc_y1(yy, yy).wait_recv()

    loop(3, doc_second)

    def doc_on(k):
        doc_y2((y + k + 1) % 4, y).start()
        doc_x2((x + k + 1) % 4, x).start()

    loop(3, doc_on)

    def req_wait(k):
        p = (me_p + k + 1) % 16
        req_copy(p, p).wait_recv()

    loop(15, req_wait)
    named = jnp.concatenate([rq_in[i] for i in range(16)] + [jnp.zeros((112, 128), F32)], axis=0)
    lt[...] = named.T
    lane2048 = lax.broadcasted_iota(jnp.int32, (128, 2048), 1).astype(F32) + 1.0

    def rows_copy(p, slot):
        return remote(
            p_out.at[p], p_in.at[slot % 2, slot // 2],
            plane_s.at[ROWS, p], plane_r.at[ROWS, slot], plane_dev(p),
        )

    def fetch(g):
        hots = []
        for i in range(4):
            col = jnp.sum(jnp.where(lane128 == g * 4 + i, lt[...], 0.0), axis=1, keepdims=True)
            hots.append(jnp.where(col == lane2048, 1.0, 0.0).astype(BF16))
        hots = jnp.concatenate(hots, axis=0)
        hots_r[pl.ds(pl.multiple_of(g * 512, 512), 512), :] = hots
        got = mm(hots, pool_s[0], NT) + mm(hots, pool_s[1], NT) + mm(hots, pool_s[2], NT)
        for i in range(4):
            p = g * 4 + i
            p_out[p] = fold(got[i * 128 : i * 128 + 64], got[i * 128 + 64 : i * 128 + 128])

            @pl.when(p != me_p)
            def _():
                rows_copy(p, me_p).start()

    loop(4, fetch)
    p_in[yh, xy] = p_out[me_p]

    def q_wait(tt):
        @pl.when(2 * tt + yh != z)
        def _():
            remote(q_all.at[c, tt], q_all.at[c, tt], qs.at[0], qr.at[tt], partner).wait_recv()

    loop(4, q_wait)
    sib_q = remote(q_all.at[c], q_all.at[c], one_s.at[SIB_Q], one_r.at[SIB_Q], sibling)
    sib_q.start()

    queries = split3(q_all[c].reshape(512, 384))

    def pick(g):
        hots = jnp.concatenate(
            [jnp.where(hot(g * 4 + i), 1.0, 0.0).astype(BF16) for i in range(4)], axis=0
        )
        got = mm(hots, queries[0], NN) + mm(hots, queries[1], NN) + mm(hots, queries[2], NN)
        for i in range(4):
            first, last = regroup(got[i * 128 : i * 128 + 64], got[i * 128 + 64 : i * 128 + 128])
            f_out[(g * 4 + i) * 2] = first
            f_out[(g * 4 + i) * 2 + 1] = last

    loop(2, pick)
    f_in[me_p] = f_out[me_p]

    remote(q_all.at[c], q_all.at[1 - c], one_s.at[SIB_Q], one_r.at[SIB_Q], sibling).wait_recv()

    def rearrange_q(tt):
        first, last = regroup(q_all[0, tt], q_all[1, tt])
        q_re[0, tt] = first
        q_re[1, tt] = last

    loop(4, rearrange_q)

    def doc_wait(k):
        xx, yy = (x + k + 1) % 4, (y + k + 1) % 4
        doc_y2(yy, yy).wait_recv()
        doc_x2(xx, xx).wait_recv()

    loop(3, doc_wait)

    def score(j):
        total = None
        for part in range(2):
            docs = d_raw[part, pl.ds(j * 2, 2)].reshape(256, 384)
            value = mm(docs, q_re[part].reshape(512, 384), NT, HIGHEST)
            total = value if total is None else total + value
        st[pl.ds(pl.multiple_of(j * 256, 256), 256), :] = total * SCALE

    loop(2, score)

    def top(j, best):
        rows = st[pl.ds(pl.multiple_of(j * 64, 64), 64), :].reshape(8, 8, 512)
        return jnp.maximum(best, jnp.max(rows, axis=0))

    best = lax.fori_loop(0, 8, top, jnp.full((8, 512), -jnp.inf, F32))
    best = jnp.max(best, axis=0, keepdims=True)

    def rows_wait(k):
        p = (me_p + k + 1) % 16
        rows_copy(p, p).wait_recv()

    loop(15, rows_wait)
    low64 = low(64)

    def hard_part(a, table):
        terms = p_in[0, a] * f_out[a * 2] + p_in[1, a] * f_out[a * 2 + 1]
        t0, t1, t2 = halves(terms)
        first = jnp.sum(t0 + jnp.where(low64, t1, 0.0), axis=1, keepdims=True)
        last = jnp.sum(t2 + jnp.where(low64, 0.0, t1), axis=1, keepdims=True)
        return jnp.where(lane128 == a, jnp.concatenate([first, last], axis=0), table)

    hs_mine[...] = lax.fori_loop(0, 8, hard_part, jnp.zeros((128, 128), F32))
    sib_h = remote(hs_mine, hs_sib, one_s.at[SIB_H], one_r.at[SIB_H], sibling)
    sib_h.start()

    def query_copy(p, slot):
        return remote(
            f_out.at[p], f_in.at[slot], plane_s.at[QUERY, p], plane_r.at[QUERY, slot], plane_dev(p)
        )

    loop(15, lambda k: query_copy((me_p + k + 1) % 16, me_p).start())

    square = st[pl.ds(pl.multiple_of(xy * 64, 64), 64), pl.ds(pl.multiple_of(t * 128, 128), 128)]
    on_diagonal = lax.broadcasted_iota(jnp.int32, (64, 128), 1) == (
        lax.broadcasted_iota(jnp.int32, (64, 128), 0) + c * 64
    )
    positive = jnp.sum(jnp.where(on_diagonal, square, 0.0), axis=0, keepdims=True)
    pos_out[...] = positive
    sib_p = remote(pos_out, pos_in, one_s.at[SIB_P], one_r.at[SIB_P], sibling)

    def weigh(j, total):
        rows = pl.ds(pl.multiple_of(j * 64, 64), 64)
        value = jnp.exp(st[rows, :] - best)
        st[rows, :] = value
        return total + jnp.sum(value.reshape(8, 8, 512), axis=0)

    weight = lax.fori_loop(0, 8, weigh, jnp.zeros((8, 512), F32))
    weight = jnp.sum(weight, axis=0, keepdims=True)

    sib_h.wait_recv()
    hard = (hs_mine[...] + hs_sib[...]) * SCALE
    for a in range(8):
        row = jnp.sum(jnp.where(hot(a), hard[:, a : a + 1], 0.0), axis=0, keepdims=True)
        hq[a : a + 1, :] = jnp.where(sid[a : a + 1, :] >= 0.0, row, -jnp.inf)
    peak = jnp.maximum(best, jnp.max(hq[...], axis=0, keepdims=True))

    total = jnp.exp(hq[...] - peak) * jnp.where(c == 0, 1.0, 0.0)
    total = jnp.sum(total, axis=0, keepdims=True) + weight * jnp.exp(best - peak)
    stat_out[:, 0:512] = peak
    stat_out[:, 512:1024] = total
    stat_in[me_r] = stat_out[...]

    def stat_copy(r, slot):
        return remote(stat_out, stat_in.at[slot], row_s.at[r], row_r.at[slot], row_dev(r))

    loop(15, lambda k: stat_copy((me_r + k + 1) % 16, me_r).start())
    sib_p.start()

    def rearrange_d(k):
        first, last = regroup(d_raw[0, k // 2, k % 2], d_raw[1, k // 2, k % 2])
        d_all[0, k] = first
        d_all[1, k] = last
        first, last = regroup(p_in[0, k], p_in[1, k])
        p_all[k, 0:64] = first
        p_all[k, 64:128] = last

    loop(8, rearrange_d)
    sid_t = jnp.concatenate([sid[...], jnp.zeros((120, 512), F32)], axis=0).T
    lane512 = lax.broadcasted_iota(jnp.int32, (512, 128), 1).astype(F32)
    for a in range(8):
        hots_t[:, a * 128 : (a + 1) * 128] = jnp.where(
            sid_t[:, a : a + 1] == lane512, 1.0, 0.0
        ).astype(BF16)

    def stat_wait(k):
        r = (me_r + k + 1) % 16
        stat_copy(r, r).wait_recv()

    loop(15, stat_wait)
    peaks = jnp.concatenate([stat_in[r, :, 0:512] for r in range(16)], axis=0)
    totals = jnp.concatenate([stat_in[r, :, 512:1024] for r in range(16)], axis=0)
    peak = jnp.max(peaks, axis=0, keepdims=True)
    total = jnp.sum(totals * jnp.exp(peaks - peak), axis=0, keepdims=True)
    log_total = peak + jnp.log(total)
    lrow[...] = log_total

    hq[...] = jnp.exp(hq[...] - log_total)

    shares = columns(hq)
    chances = shares.T
    for a in range(8):
        hc_out[a] = chances[a : a + 1, :]
    hc_in[me_p] = hc_out[xy]

    def prob_copy(p, slot):
        return remote(
            hc_out.at[p // 2], hc_in.at[slot], plane_s.at[PROB, p], plane_r.at[PROB, slot], plane_dev(p)
        )

    loop(15, lambda k: prob_copy((me_p + k + 1) % 16, me_p).start())

    for a in range(8):
        for k, part in enumerate(split3(p_all[a] * shares[:, a : a + 1])):
            hp[k, a] = part

    to_own = jnp.exp(best - log_total)

    def chance(j):
        rows = pl.ds(pl.multiple_of(j * 128, 128), 128)
        value = st[rows, :] * to_own
        st[rows, :] = value
        ch[:, rows] = value.T

    loop(4, chance)

    def sib_g(h):
        return remote(g_sib_out.at[h], g_sib_in.at[h], sg_s.at[h], sg_r.at[h], sibling)

    def grad_copy(tt, slot):
        return remote(g_out.at[tt], g_in.at[slot], gs.at[tt], gr.at[slot], z_dev(2 * tt + yh))

    def grad_half(h):
        rows = pl.ds(pl.multiple_of(h * 256, 256), 256)
        g_sib_out[h] = mm(ch[rows, :], d_all[1 - c].reshape(512, 384), NN, HIGHEST)
        sib_g(h).start()
        g_own = mm(ch[rows, :], d_all[c].reshape(512, 384), NN, HIGHEST)
        for k in range(3):
            g_own = g_own + mm(hots_t[rows, :], hp[k].reshape(1024, 384), NN)
        sib_g(h).wait_recv()
        g_out[pl.ds(h * 2, 2)] = (g_own + g_sib_in[h]).reshape(2, 128, 384)
        for i in range(2):
            tt = h * 2 + i

            @pl.when(2 * tt + yh != z)
            def _():
                grad_copy(tt, z).start()

    loop(2, grad_half)

    @pl.when(holder)
    def _():
        g_in[z] = g_out[t]

    def doc_grad(part):
        value = mm(st[...], q_re[part].reshape(512, 384), NN, HIGHEST)
        g3_out[part] = value.reshape(4, 2, 64, 384)

    loop(2, doc_grad)

    def grad_y1(yy, slot):
        return remote(
            g3_out.at[yy // 2, :, yy % 2, pl.ds(0, 32)], c1y.at[slot],
            y_s.at[GRAD_1, yy], y_r.at[GRAD_1, slot], y_dev(yy),
        )

    def grad_x1(xx, slot):
        return remote(
            g3_out.at[:, xx, :, pl.ds(32, 32)], c1x.at[slot],
            x_s.at[GRAD_1, xx], x_r.at[GRAD_1, slot], x_dev(xx),
        )

    def grad_x2(xx, slot):
        return remote(cy.at[xx], c2x.at[slot], x_s.at[GRAD_2, xx], x_r.at[GRAD_2, slot], x_dev(xx))

    def grad_y2(yy, slot):
        return remote(
            cx.at[yy // 2, yy % 2], c2y.at[slot], y_s.at[GRAD_2, yy], y_r.at[GRAD_2, slot], y_dev(yy)
        )

    def grad_first(k):
        grad_y1((y + k + 1) % 4, y).start()
        grad_x1((x + k + 1) % 4, x).start()

    loop(3, grad_first)
    def query_wait(k):
        p = (me_p + k + 1) % 16
        query_copy(p, p).wait_recv()
        prob_copy(p, p).wait_recv()

    loop(15, query_wait)
    chances = jnp.concatenate([hc_in[i] for i in range(16)] + [jnp.zeros((112, 128), F32)], axis=0).T

    def turn(i):
        col = jnp.sum(jnp.where(lane128 == i, chances, 0.0), axis=1, keepdims=True)
        rows = jnp.concatenate(unfold(f_in[i]), axis=0) * (col * SCALE)
        terms = split3(rows.T[0:192])
        for k in range(2):
            at_s[k * 192 : k * 192 + 192, pl.ds(pl.multiple_of(i * 128, 128), 128)] = terms[k]

    loop(16, turn)

    def pool_grad(n):
        columns_n = pl.ds(pl.multiple_of(n * 256, 256), 256)
        value = mm(at_s[...], hots_r[:, columns_n], NN)
        gp_ref[:, columns_n] = value[0:192] + value[192:384]

    loop(4, pool_grad)

    def grad_second(k):
        xx, yy = (x + k + 1) % 4, (y + k + 1) % 4
        grad_y1(yy, yy).wait_recv()
        grad_x1(xx, xx).wait_recv()

    loop(3, grad_second)

    def sum_y(xx):
        cy[xx] = (g3_out[yh, xx, yl, 0:32] + c1y[(y + 1) % 4, xx]) + (
            c1y[(y + 2) % 4, xx] + c1y[(y + 3) % 4, xx]
        )

    loop(4, sum_y)

    def sum_x(k):
        a, b = k // 2, k % 2
        cx[a, b] = (g3_out[a, x, b, 32:64] + c1x[(x + 1) % 4, a, b]) + (
            c1x[(x + 2) % 4, a, b] + c1x[(x + 3) % 4, a, b]
        )

    loop(4, sum_x)

    def grad_on(k):
        grad_x2((x + k + 1) % 4, x).start()
        grad_y2((y + k + 1) % 4, y).start()

    loop(3, grad_on)
    loop(4, lambda n: pool_grad(n + 4))

    def grad_wait(k):
        xx, yy = (x + k + 1) % 4, (y + k + 1) % 4
        grad_x2(xx, xx).wait_recv()
        grad_y2(yy, yy).wait_recv()

    loop(3, grad_wait)
    upper_rows = (cy[x] + c2x[(x + 1) % 4]) + (c2x[(x + 2) % 4] + c2x[(x + 3) % 4])
    lower_rows = (cx[yh, yl] + c2y[(y + 1) % 4]) + (c2y[(y + 2) % 4] + c2y[(y + 3) % 4])
    value = jnp.concatenate([upper_rows, lower_rows], axis=0)
    first, last = unfold(value)
    dd_out[...] = jnp.where(c == 0, last, first)
    sib_dd = remote(dd_out, dd_sib, one_s.at[SIB_DD], one_r.at[SIB_DD], sibling)
    sib_dd.start()
    dd_nat[pl.ds(pl.multiple_of(c * 64, 64), 64), :] = jnp.where(c == 0, first, last)

    sib_d.wait_send()
    sib_q.wait_send()
    sib_h.wait_send()
    loop(2, lambda h: sib_g(h).wait_send())

    def sent(k):
        p = (me_p + k + 1) % 16
        for copy in (req_copy, rows_copy, query_copy, prob_copy):
            copy(p, me_p).wait_send()
        stat_copy((me_r + k + 1) % 16, me_r).wait_send()

    loop(15, sent)

    def sent4(k):
        for copy in (doc_x1, doc_x2, grad_x1, grad_x2):
            copy((x + k + 1) % 4, x).wait_send()
        for copy in (doc_y1, doc_y2, grad_y1, grad_y2):
            copy((y + k + 1) % 4, y).wait_send()

    loop(3, sent4)
    sib_p.wait_send()

    def grad_sent(tt):
        @pl.when(2 * tt + yh != z)
        def _():
            grad_copy(tt, z).wait_send()

    loop(4, grad_sent)

    @pl.when(holder)
    def _():
        def z_sent(k):
            zz = (z + k + 1) % 8
            idx_copy(zz).wait_send()
            q_copy(zz).wait_send()

        loop(7, z_sent)

    @pl.when(jnp.logical_not(holder))
    def _():
        part_q.wait_send()

    part_dq = remote(dq_out, dq_in, one_s.at[PART_DQ], one_r.at[PART_DQ], partner)
    part_l = remote(loss_out, loss_in, one_s.at[PART_L], one_r.at[PART_L], partner)
    sib_p.wait_recv()

    @pl.when(holder)
    def _():
        loss_out[...] = lrow[:, pl.ds(pl.multiple_of(t * 128, 128), 128)] - (pos_out[...] + pos_in[...])
        part_l.start()

        def wait(k):
            zz = (z + k + 1) % 8
            grad_copy(t, zz).wait_recv()

        loop(7, wait)
        value = g_in[0]
        for zz in range(1, 8):
            value = value + g_in[zz]
        first, last = unfold(value)
        dq_out[...] = jnp.where(yh == 0, last, first).T[0:192]
        part_dq.start()
        dq_ref[...] = (jnp.where(yh == 0, first, last).T[0:192] - d_ref[...]) * SCALE
        loss_ref[...] = loss_out[...]

    sib_dd.wait_recv()
    dd_nat[pl.ds(pl.multiple_of((1 - c) * 64, 64), 64), :] = dd_sib[...]
    dd_ref[...] = (dd_nat[...].T[0:192] - q_ref[...]) * SCALE

    @pl.when(jnp.logical_not(holder))
    def _():
        part_l.wait_recv()
        loss_ref[...] = loss_in[...]
        part_dq.wait_recv()
        dq_ref[...] = (dq_in[...] - d_ref[...]) * SCALE

    sib_dd.wait_send()

    @pl.when(holder)
    def _():
        part_l.wait_send()
        part_dq.wait_send()


def hand_on(*refs):
    for source, target in zip(refs[:4], refs[4:]):
        target[...] = source[...]


def per_device(question_matrix, document_matrix, pool, hard_owner, hard_local):
    vmem = pl.BlockSpec(memory_space=pltpu.VMEM)
    f = lambda *shape: pltpu.VMEM(shape, F32)
    scratch = [
        pltpu.VMEM((16, 128), jnp.int32),
        pltpu.VMEM((4, 16, 128), jnp.int32),
        f(192, 128),
        f(2, 4, 128, 384),
        f(2, 4, 128, 384),
        f(128, 256),
        f(64, 256),
        f(2, 4, 2, 64, 384),
        f(2, 8, 64, 384),
        f(8, 512),
        f(8, 512),
        f(8, 1, 128),
        f(16, 1, 128),
        f(128, 128),
        pltpu.VMEM((3, 256, 2048), BF16),
        f(16, 64, 384),
        f(2, 8, 64, 384),
        f(8, 128, 384),
        f(16, 64, 384),
        f(16, 64, 384),
        f(128, 128),
        f(128, 128),
        f(8, 512),
        f(512, 512),
        f(512, 512),
        f(1, 1024),
        f(16, 1, 1024),
        f(8, 1, 128),
        f(16, 1, 128),
        f(2, 4, 2, 64, 384),
        f(4, 2, 2, 32, 384),
        f(4, 4, 32, 384),
        f(2, 2, 32, 384),
        f(4, 32, 384),
        f(4, 32, 384),
        f(4, 32, 384),
        f(64, 256),
        f(64, 256),
        f(128, 256),
        f(2, 256, 384),
        f(2, 256, 384),
        f(4, 128, 384),
        f(8, 128, 384),
        pltpu.VMEM((512, 1024), BF16),
        pltpu.VMEM((3, 8, 128, 384), BF16),
        pltpu.VMEM((384, 2048), BF16),
        pltpu.VMEM((2048, 2048), BF16),
        f(192, 128),
        f(192, 128),
        f(1, 128),
        f(1, 128),
        f(1, 128),
        f(1, 128),
        f(1, 512),
        pltpu.SemaphoreType.DMA((4, 16)),
        pltpu.SemaphoreType.DMA((4, 16)),
        pltpu.SemaphoreType.DMA((4, 4)),
        pltpu.SemaphoreType.DMA((4, 4)),
        pltpu.SemaphoreType.DMA((4, 4)),
        pltpu.SemaphoreType.DMA((4, 4)),
        pltpu.SemaphoreType.DMA((16,)),
        pltpu.SemaphoreType.DMA((16,)),
        pltpu.SemaphoreType.DMA((8,)),
        pltpu.SemaphoreType.DMA((4,)),
        pltpu.SemaphoreType.DMA((8,)),
        pltpu.SemaphoreType.DMA((4,)),
        pltpu.SemaphoreType.DMA((4,)),
        pltpu.SemaphoreType.DMA((8,)),
        pltpu.SemaphoreType.DMA((2,)),
        pltpu.SemaphoreType.DMA((2,)),
        pltpu.SemaphoreType.DMA((9,)),
        pltpu.SemaphoreType.DMA((9,)),
    ]
    results = pl.pallas_call(
        kernel,
        name="retriever_step",
        out_shape=(
            jax.ShapeDtypeStruct((1, 128), F32),
            jax.ShapeDtypeStruct((192, 128), F32),
            jax.ShapeDtypeStruct((192, 128), F32),
            jax.ShapeDtypeStruct((192, 2048), F32),
        ),
        in_specs=[vmem] * 5,
        out_specs=(vmem,) * 4,
        scratch_shapes=scratch,
        compiler_params=pltpu.CompilerParams(
            collective_id=0, has_side_effects=True, vmem_limit_bytes=60 * 1024 * 1024
        ),
    )(question_matrix.T, document_matrix.T, pool, hard_owner.T, hard_local.T)
    loss, dq, dd, gp = pl.pallas_call(
        hand_on,
        name="results",
        out_shape=tuple(jax.ShapeDtypeStruct(r.shape, r.dtype) for r in results),
        in_specs=[vmem] * 4,
        out_specs=(vmem,) * 4,
    )(*results)
    return loss.reshape(128), dq.T, dd.T, gp


def solution(mesh):
    placed = (P("blk", "dim"), P("blk", "dim"), P("dim", "blk"), P("blk", None), P("blk", None))
    return jax.shard_map(
        per_device,
        mesh=mesh,
        in_specs=placed,
        out_specs=(P("blk"), P("blk", "dim"), P("blk", "dim"), P("dim", "blk")),
        check_vma=False,
    )
```
